32 devices in a mesh: rep: 4 (over y, x), shard: 8 (over z, core).
Axes of the slice: x: 2, y: 2, z: 4, core: 2. Of those that a mesh axis runs over, the one named last changes fastest.
Arguments:
- layer_input: bfloat16 [16384, 1024], P(('rep', 'shard')), may hold values from -6 to 6
- encoder_states: bfloat16 [2048, 1024], P(('rep', 'shard')), may hold values from -6 to 6
- out_grad: bfloat16 [16384, 1024], P(('rep', 'shard')), may hold values from -6 to 6
- placement: int32 [4, 8], P('rep'), may hold values from 0 to 7, each once within a row
- w_self_qkv: bfloat16 [1024, 3072], P('shard'), may hold values from -0.1875 to 0.1875
- w_self_out: bfloat16 [1024, 1024], P('shard'), may hold values from -0.75 to 0.75
- w_cross_q: bfloat16 [1024, 1024], P('shard'), may hold values from -0.1875 to 0.1875
- w_cross_kv: bfloat16 [1024, 2048], P('shard'), may hold values from -0.1875 to 0.1875
- w_cross_out: bfloat16 [1024, 1024], P('shard'), may hold values from -0.75 to 0.75
- w_fc1: bfloat16 [1024, 4096], P('shard'), may hold values from -0.1875 to 0.1875
- w_fc2: bfloat16 [4096, 1024], P('shard'), may hold values from -0.09375 to 0.09375
- proj_biases: float32 [7, 1024], replicated, may hold values from -1 to 1
- fc1_bias: float32 [4096], replicated, may hold values from -1 to 1
- norm_gains: float32 [3, 1024], replicated, may hold values from 0.5 to 1.5
- norm_shifts: float32 [3, 1024], replicated, may hold values from -1 to 1
Outputs:
- output: bfloat16 [16384, 1024], P(('rep', 'shard'))
- input_grad: float32 [16384, 1024], P(('rep', 'shard'))
- enc_grad: float32 [2048, 1024], P(('rep', 'shard'))
- grad_self_qkv: float32 [1024, 3072], P('shard')
- grad_self_out: float32 [1024, 1024], P('shard')
- grad_cross_q: float32 [1024, 1024], P('shard')
- grad_cross_kv: float32 [1024, 2048], P('shard')
- grad_cross_out: float32 [1024, 1024], P('shard')
- grad_fc1: float32 [1024, 4096], P('shard')
- grad_fc2: float32 [4096, 1024], P('shard')
- grad_proj_biases: float32 [7, 1024], replicated
- grad_fc1_bias: float32 [4096], replicated
- grad_norm_gains: float32 [3, 1024], replicated
- grad_norm_shifts: float32 [3, 1024], replicated
The draws below stay inside these ranges and needn't reach their ends.
Inputs may be any that keep to these rules, and one draw needn't show every extreme that they name: `placement`: each row names each slot once.
All inputs are finite; a program needn't handle non-finite values.
Results may differ from the reference program's by a relative error of at most 0.028.
Values may be sent and summed in bfloat16 or wider, within the bound.
No kernel may reach another device: no remote copies, remote signals or barrier semaphores. Data moves between devices by JAX's collectives and lax.ppermute only.
A program may use at most 320 MiB of HBM per device.

```python
import jax
import jax.numpy as jnp
from jax import lax

D = 1024
HEADS = 16
HEAD_DIM = 64
FF = 4096
TOK_DEV = 512
GROUP = 8
REPS = 4
PROMPT = 2048
ENC = 512
TOKENS = 16384
ENC_ALL = 2048


def level_of(rng, shape, split, least, largest):
    level, own = 1.0, jax.random.fold_in(rng, 6)
    for axis_at, parts in split:
        heights = jnp.exp(jax.random.uniform(jax.random.fold_in(own, axis_at), (parts,), jnp.float32, least / len(split), largest / len(split)))
        level = level * jnp.repeat(heights, shape[axis_at] // parts).reshape([-1 if axis == axis_at else 1 for axis in range(len(shape))])
    return level


def scatter_about(own_key, dims, deviation, reach, cuts=(), kind=jnp.bfloat16):
    values = deviation * jax.random.normal(own_key, dims, jnp.float32)
    if cuts:
        values = values * level_of(own_key, dims, cuts, -0.22, 0.18)
    return jnp.clip(values, -reach, reach).astype(kind)


def setup_inputs(seed: int = 0) -> dict:
    key_of = jax.random.split(jax.random.key(seed), 16)
    return {
        "layer_input": scatter_about(key_of[0], (TOKENS, D), 1.0, 6.0, ((0, 32),)),
        "encoder_states": scatter_about(key_of[1], (ENC_ALL, D), 1.0, 6.0, ((0, 32),)),
        "out_grad": scatter_about(key_of[2], (TOKENS, D), 1.0, 6.0, ((0, 32),)),
        "placement": jax.vmap(lambda own: jax.random.permutation(own, GROUP))(jax.random.split(key_of[3], REPS)).reshape((REPS, GROUP)).astype(jnp.int32),
        "w_self_qkv": scatter_about(key_of[4], (D, 3 * D), D ** -0.5, 0.1875, ((0, 8),)),
        "w_self_out": scatter_about(key_of[5], (D, D), (D // 16) ** -0.5, 0.75, ((0, 8),)),
        "w_cross_q": scatter_about(key_of[6], (D, D), D ** -0.5, 0.1875, ((0, 8),)),
        "w_cross_kv": scatter_about(key_of[7], (D, 2 * D), D ** -0.5, 0.1875, ((0, 8),)),
        "w_cross_out": scatter_about(key_of[8], (D, D), (D // 16) ** -0.5, 0.75, ((0, 8),)),
        "w_fc1": scatter_about(key_of[9], (D, FF), D ** -0.5, 0.1875, ((0, 8),)),
        "w_fc2": scatter_about(key_of[10], (FF, D), FF ** -0.5, 0.09375, ((0, 8),)),
        "proj_biases": scatter_about(key_of[11], (7, D), 0.2, 1.0, (), jnp.float32),
        "fc1_bias": scatter_about(key_of[12], (FF,), 0.2, 1.0, (), jnp.float32),
        "norm_gains": jnp.clip(1.0 + 0.1 * jax.random.normal(key_of[13], (3, D), jnp.float32), 0.5, 1.5),
        "norm_shifts": scatter_about(key_of[14], (3, D), 0.2, 1.0, (), jnp.float32),
    }


@jax.custom_vjp
def low(v):
    return lax.optimization_barrier(v.astype(jnp.bfloat16)).astype(jnp.float32)

@jax.custom_vjp
def low_back(v):
    return v

def low_keep(v):
    return (low(v), None)

def low_pass(kept, grad):
    return (grad,)

def back_keep(v):
    return (v, None)

def back_low(kept, grad):
    return (low(grad),)
low.defvjp(low_keep, low_pass)
low_back.defvjp(back_keep, back_low)
highest = lax.Precision.HIGHEST
masked_score = -1000000000.0
norm_epsilon = 1e-05

def product(former, latter):
    return jnp.dot(former, latter, precision=highest)

def norm_rows(values, gain_row, shift_row):
    row_mean = lax.optimization_barrier(jnp.mean(values, -1, keepdims=True))
    centered = values - row_mean
    variance = lax.optimization_barrier(jnp.mean(centered * centered, -1, keepdims=True))
    return centered * lax.rsqrt(variance + norm_epsilon) * gain_row + shift_row

def by_heads(values):
    return values.reshape(values.shape[0], HEADS, HEAD_DIM)

def attention(queries, key_rows, value_rows, allowed):
    scores = jnp.einsum('qhd,khd->hqk', by_heads(queries), by_heads(key_rows), precision=highest)
    scores = low_back(scores)
    if allowed is not None:
        scores = jnp.where(allowed[None], scores, masked_score)
    weights = low(jax.nn.softmax(scores, axis=-1))
    mixed_rows = jnp.einsum('hqk,khd->qhd', weights, by_heads(value_rows), precision=highest)
    return low_back(low(mixed_rows.reshape(queries.shape[0], D)))

def self_rows(prompt_kv, queries, own_kv, slot_value):
    half_group = GROUP // 2
    seq_number = jnp.where(slot_value < half_group, 0, slot_value - half_group + 1)
    first_pos = jnp.where(slot_value < half_group, slot_value * TOK_DEV, PROMPT)
    positions = jnp.arange(TOK_DEV, dtype=jnp.int32)
    prompt_pos = jnp.arange(PROMPT, dtype=jnp.int32)
    early_mask = (seq_number > 0) | (prompt_pos[None, :] <= (first_pos + positions)[:, None])
    late_mask = (seq_number > 0) & (positions[None, :] <= positions[:, None])
    allowed = jnp.concatenate([early_mask, late_mask], 1)
    key_value = jnp.concatenate([prompt_kv, own_kv], 0)
    return attention(queries, key_value[:, :D], key_value[:, D:], allowed)

def reference(layer_input, encoder_states, out_grad, placement, w_self_qkv, w_self_out, w_cross_q, w_cross_kv, w_cross_out, w_fc1, w_fc2, proj_biases, fc1_bias, norm_gains, norm_shifts):
    score_scale = HEAD_DIM ** (-0.5)
    device_ids = jnp.arange(GROUP, dtype=jnp.int32)
    owner_table = lax.optimization_barrier(jnp.sum(jnp.where(placement[:, None, :] == device_ids[None, :, None], device_ids[None, None, :], 0), -1)).astype(jnp.int32)
    prompt_owner = owner_table[:, :GROUP // 2]

    def forward(inputs, states, full_qkv, full_out, full_cross_q, full_cross_kv, full_cross_out, wfirst, wsecond, biases, first_bias, gain_rows, shift_rows):
        qkv_rows = product(inputs, full_qkv)
        queries = low_back(low((qkv_rows[:, :D] + biases[0]) * score_scale))
        self_kv = low_back(low(jnp.concatenate([qkv_rows[:, D:2 * D], qkv_rows[:, 2 * D:] + biases[1]], 1)))
        group_queries = queries.reshape(REPS, GROUP, TOK_DEV, D)
        group_kv = self_kv.reshape(REPS, GROUP, TOK_DEV, 2 * D)
        prompt_kv = jax.vmap(lambda blocks, chosen: jnp.take(blocks, chosen, axis=0))(group_kv, prompt_owner).reshape(REPS, PROMPT, 2 * D)

        def group_self(pieces):
            shared_kv, these_queries, these_kv, slot_row = pieces

            def device_self(device_part):
                return self_rows(shared_kv, device_part[0], device_part[1], device_part[2])
            return lax.map(jax.checkpoint(device_self), (these_queries, these_kv, slot_row))
        self_mixed = lax.map(jax.checkpoint(group_self), (prompt_kv, group_queries, group_kv, placement)).reshape(TOKENS, D)
        first_sum = inputs + low_back(product(self_mixed, full_out) + biases[2])
        first_norm = norm_rows(first_sum, gain_rows[0], shift_rows[0])
        cross_queries = low_back(low((product(low(first_norm), full_cross_q) + biases[3]) * score_scale))
        cross_pre = product(states, full_cross_kv)
        cross_kv = low_back(low(jnp.concatenate([cross_pre[:, :D], cross_pre[:, D:] + biases[4]], 1)))

        def group_cross(pieces):
            these_queries, these_kv = pieces

            def device_cross(device_queries):
                return attention(device_queries, these_kv[:, :D], these_kv[:, D:], None)
            return lax.map(jax.checkpoint(device_cross), these_queries)
        cross_mixed = lax.map(jax.checkpoint(group_cross), (cross_queries.reshape(REPS, GROUP, TOK_DEV, D), cross_kv.reshape(REPS, ENC, 2 * D))).reshape(TOKENS, D)
        second_sum = first_norm + low_back(product(cross_mixed, full_cross_out) + biases[5])
        second_norm = norm_rows(second_sum, gain_rows[1], shift_rows[1])
        pre_act = low_back(product(low(second_norm), wfirst) + first_bias)
        hidden = low(jax.nn.gelu(pre_act, approximate=False))
        third_sum = second_norm + low_back(product(hidden, wsecond) + biases[6])
        return norm_rows(third_sum, gain_rows[2], shift_rows[2])
    primals = (layer_input.astype(jnp.float32), encoder_states.astype(jnp.float32), w_self_qkv.astype(jnp.float32), w_self_out.astype(jnp.float32), w_cross_q.astype(jnp.float32), w_cross_kv.astype(jnp.float32), w_cross_out.astype(jnp.float32), w_fc1.astype(jnp.float32), w_fc2.astype(jnp.float32), proj_biases, fc1_bias, norm_gains, norm_shifts)
    result, pullback = jax.vjp(forward, *primals)
    gradients = pullback(out_grad.astype(jnp.float32))
    return (result.astype(jnp.bfloat16), gradients[0], gradients[1], gradients[2], gradients[3], gradients[4], gradients[5], gradients[6], gradients[7], gradients[8], gradients[9], gradients[10], gradients[11], gradients[12])
```

```python
import functools

import jax
import jax.numpy as jnp
from jax import lax
from jax.experimental import pallas as pl
from jax.experimental.pallas import tpu as pltpu
from jax.sharding import PartitionSpec as P

HEADS = 16
HEAD_DIM = 64
LANES = 128

masked_score = -1000000000.0
norm_epsilon = 1e-05
low_type = jnp.bfloat16
MESH_AXES = ("rep", "shard")


def norm_rows(values, gain_row, shift_row):
    row_mean = jnp.mean(values, -1, keepdims=True)
    centered = values - row_mean
    variance = jnp.mean(centered * centered, -1, keepdims=True)
    return centered * lax.rsqrt(variance + norm_epsilon) * gain_row + shift_row


def product(former, latter):
    return jnp.dot(former, latter, preferred_element_type=jnp.float32)


def product_left(former, latter):
    return lax.dot_general(
        former, latter, (((0,), (0,)), ((), ())), preferred_element_type=jnp.float32
    )


def product_right(former, latter):
    return lax.dot_general(
        former, latter, (((1,), (1,)), ((), ())), preferred_element_type=jnp.float32
    )


def column_sums(values):
    return jnp.sum(values.astype(jnp.float32), 0)


def head_columns(index):
    return slice(index * HEAD_DIM, (index + 1) * HEAD_DIM)


def causal_rows(keys, queries):
    key_index = lax.broadcasted_iota(jnp.int32, (keys, queries), 0)
    query_index = lax.broadcasted_iota(jnp.int32, (keys, queries), 1)
    return key_index <= query_index


def self_forward_kernel(tok, width, half, owner, qkv, value_t, mixed, total):
    slot = pl.program_id(0)
    heads = width // HEAD_DIM
    base = pl.multiple_of(owner[slot] * tok, tok)
    query = qkv[pl.ds(base, tok), :width]

    def step(start, carry, causal):
        keys = qkv[pl.ds(start, tok), width : 2 * width]
        values = value_t[:, pl.ds(start, tok)]
        result = []
        for head in range(heads):
            top, weight, mix = carry[head]
            cols = head_columns(head)
            scores = product_right(keys[:, cols], query[:, cols])
            if causal:
                scores = jnp.where(causal_rows(tok, tok), scores, masked_score)
            new_top = jnp.maximum(top, jnp.max(scores, 0, keepdims=True))
            scale = jnp.exp(top - new_top)
            power = jnp.exp(scores - new_top)
            weight = weight * scale + jnp.sum(power, 0, keepdims=True)
            mix = mix * scale + product(values[cols], power.astype(low_type))
            result.append((new_top, weight, mix))
        return tuple(result)

    first = tuple(
        (
            jnp.full((1, tok), -1e30, jnp.float32),
            jnp.zeros((1, tok), jnp.float32),
            jnp.zeros((HEAD_DIM, tok), jnp.float32),
        )
        for _ in range(heads)
    )
    whole = jnp.minimum(slot, half)
    carry = lax.fori_loop(
        0, whole, lambda j, c: step(pl.multiple_of(owner[j] * tok, tok), c, False), first
    )
    carry = step(base, carry, True)
    mix = jnp.concatenate([part[2] / part[1] for part in carry], 0)
    mixed[pl.ds(base, tok), :] = jnp.transpose(mix).astype(low_type)
    for head in range(heads):
        total[head : head + 1, :] = carry[head][0] + jnp.log(carry[head][1])


def self_backward_kernel(
    tok, width, half, scale, owner, qkv, key_t, mixed_grad, mixed, total, out, key_sum, value_sum
):
    slot = pl.program_id(0)
    heads = width // HEAD_DIM
    base = pl.multiple_of(owner[slot] * tok, tok)

    @pl.when(slot == 0)
    def _():
        key_sum[...] = jnp.zeros_like(key_sum)
        value_sum[...] = jnp.zeros_like(value_sum)

    query = qkv[pl.ds(base, tok), :width]
    grad = mixed_grad[pl.ds(base, tok), :]
    both = grad.astype(jnp.float32) * mixed[pl.ds(base, tok), :].astype(jnp.float32)
    both = jnp.transpose(both)
    deltas = [jnp.sum(both[head_columns(h)], 0, keepdims=True) for h in range(heads)]
    totals = [total[h : h + 1, :] for h in range(heads)]

    def step(start, carry, causal):
        keys = qkv[pl.ds(start, tok), width : 2 * width]
        values = qkv[pl.ds(start, tok), 2 * width :]
        keys_t = key_t[:, pl.ds(start, tok)]
        result, key_parts, value_parts = [], [], []
        for head in range(heads):
            cols = head_columns(head)
            scores = product_right(keys[:, cols], query[:, cols])
            power = jnp.exp(scores - totals[head])
            if causal:
                power = jnp.where(causal_rows(tok, tok), power, 0.0)
            slope = product_right(values[:, cols], grad[:, cols])
            score_grad = (power * (slope - deltas[head])).astype(low_type)
            value_parts.append(product(power.astype(low_type), grad[:, cols]))
            key_parts.append(product(score_grad, query[:, cols]))
            result.append(carry[head] + product(keys_t[cols], score_grad))
        key_sum[pl.ds(start, tok), :] += jnp.concatenate(key_parts, 1)
        value_sum[pl.ds(start, tok), :] += jnp.concatenate(value_parts, 1)
        return tuple(result)

    first = tuple(jnp.zeros((HEAD_DIM, tok), jnp.float32) for _ in range(heads))
    whole = jnp.minimum(slot, half)
    carry = lax.fori_loop(
        0, whole, lambda j, c: step(pl.multiple_of(owner[j] * tok, tok), c, False), first
    )
    carry = step(base, carry, True)
    query_grad = jnp.transpose(jnp.concatenate(carry, 0)).astype(low_type)
    out[pl.ds(base, tok), :width] = query_grad * scale

    @pl.when(slot == pl.num_programs(0) - 1)
    def _():
        out[:, width : 2 * width] = key_sum[...].astype(low_type)
        out[:, 2 * width :] = value_sum[...].astype(low_type)


def cross_forward_kernel(width, query, pair, mixed, total):
    keys, values = pair[0], jnp.transpose(pair[1])
    mixes = []
    for head in range(width // HEAD_DIM):
        cols = head_columns(head)
        scores = product_right(keys[:, cols], query[:, cols])
        top = jnp.max(scores, 0, keepdims=True)
        power = jnp.exp(scores - top)
        weight = jnp.sum(power, 0, keepdims=True)
        mixes.append(product(values[cols], power.astype(low_type)) / weight)
        total[head : head + 1, :] = top + jnp.log(weight)
    mixed[...] = jnp.transpose(jnp.concatenate(mixes, 0)).astype(low_type)


def cross_backward_kernel(width, scale, query, pair, mixed_grad, mixed, total, out, pair_grad):
    heads = width // HEAD_DIM
    keys, values = pair[0], pair[1]
    keys_t = jnp.transpose(keys)
    grad = mixed_grad[...]
    both = jnp.transpose(grad.astype(jnp.float32) * mixed[...].astype(jnp.float32))
    query_parts, key_parts, value_parts = [], [], []
    for head in range(heads):
        cols = head_columns(head)
        scores = product_right(keys[:, cols], query[:, cols])
        power = jnp.exp(scores - total[head : head + 1, :])
        slope = product_right(values[:, cols], grad[:, cols])
        delta = jnp.sum(both[cols], 0, keepdims=True)
        score_grad = (power * (slope - delta)).astype(low_type)
        value_parts.append(product(power.astype(low_type), grad[:, cols]))
        key_parts.append(product(score_grad, query[:, cols]))
        query_parts.append(product(keys_t[cols], score_grad))
    query_grad = jnp.transpose(jnp.concatenate(query_parts, 0)).astype(low_type)
    out[...] = query_grad * scale
    pair_grad[0] = jnp.concatenate(key_parts, 1).astype(low_type)
    pair_grad[1] = jnp.concatenate(value_parts, 1).astype(low_type)


def kernel_options(megabytes):
    return pltpu.CompilerParams(
        dimension_semantics=("arbitrary",), vmem_limit_bytes=megabytes * 2**20
    )


def whole_block(shape):
    return pl.BlockSpec(shape, lambda *_: (0,) * len(shape), pipeline_mode=pl.Buffered(1))


def self_forward(owners, qkv, value_t, tok):
    rows, width = qkv.shape[0], qkv.shape[1] // 3
    group = rows // tok
    pairs = group * (group // 4 + 1)
    return pl.pallas_call(
        functools.partial(self_forward_kernel, tok, width, group // 2),
        out_shape=(
            jax.ShapeDtypeStruct((rows, width), low_type),
            jax.ShapeDtypeStruct((group, 8, tok), jnp.float32),
        ),
        grid_spec=pltpu.PrefetchScalarGridSpec(
            num_scalar_prefetch=1,
            grid=(group,),
            in_specs=[whole_block(qkv.shape), whole_block(value_t.shape)],
            out_specs=[
                pl.BlockSpec((rows, width), lambda *_: (0, 0)),
                pl.BlockSpec((None, 8, tok), lambda p, _: (p, 0, 0)),
            ],
        ),
        compiler_params=kernel_options(40),
        cost_estimate=pl.CostEstimate(
            flops=pairs * tok * tok * width * 12,
            transcendentals=pairs * tok * tok * (width // HEAD_DIM),
            bytes_accessed=rows * width * 10,
        ),
        name="self_forward",
    )(owners, qkv, value_t)


def self_backward(owners, qkv, key_t, mixed_grad, mixed, total, tok):
    rows, width = qkv.shape[0], qkv.shape[1] // 3
    group = rows // tok
    pairs = group * (group // 4 + 1)
    return pl.pallas_call(
        functools.partial(
            self_backward_kernel, tok, width, group // 2, HEAD_DIM ** (-0.5)
        ),
        out_shape=jax.ShapeDtypeStruct(qkv.shape, low_type),
        grid_spec=pltpu.PrefetchScalarGridSpec(
            num_scalar_prefetch=1,
            grid=(group,),
            in_specs=[
                whole_block(qkv.shape),
                whole_block(key_t.shape),
                whole_block(mixed_grad.shape),
                whole_block(mixed.shape),
                pl.BlockSpec((None, 8, tok), lambda p, _: (p, 0, 0)),
            ],
            out_specs=pl.BlockSpec(qkv.shape, lambda *_: (0, 0)),
            scratch_shapes=[
                pltpu.VMEM((rows, width), jnp.float32),
                pltpu.VMEM((rows, width), jnp.float32),
            ],
        ),
        compiler_params=kernel_options(48),
        cost_estimate=pl.CostEstimate(
            flops=pairs * tok * tok * width * 30,
            transcendentals=pairs * tok * tok * (width // HEAD_DIM),
            bytes_accessed=rows * width * 20,
        ),
        name="self_backward",
    )(owners, qkv, key_t, mixed_grad, mixed, total)


def split_columns(values, group):
    rows = values.shape[0]
    return values.reshape(rows, group, -1).transpose(1, 0, 2)


def join_columns(values):
    return values.transpose(1, 0, 2).reshape(values.shape[1], -1)


def by_head(values, group):
    rows, width = values.shape[0], values.shape[1] // group
    if width % LANES == 0:
        return values, pl.BlockSpec((rows, width), lambda g: (0, g))
    return split_columns(values, group), pl.BlockSpec((None, rows, width), lambda g: (g, 0, 0))


def of_heads(values, group):
    return values if values.ndim == 2 else join_columns(values)


def cross_forward(queries, pairs):
    group, _, states, width = pairs.shape
    rows = queries.shape[0]
    queries, query_spec = by_head(queries, group)
    mixed, total = pl.pallas_call(
        functools.partial(cross_forward_kernel, width),
        out_shape=(
            jax.ShapeDtypeStruct(queries.shape, low_type),
            jax.ShapeDtypeStruct((group, 8, rows), jnp.float32),
        ),
        grid=(group,),
        in_specs=[query_spec, pl.BlockSpec((None, 2, states, width), lambda g: (g, 0, 0, 0))],
        out_specs=[query_spec, pl.BlockSpec((None, 8, rows), lambda g: (g, 0, 0))],
        compiler_params=kernel_options(32),
        cost_estimate=pl.CostEstimate(
            flops=rows * states * group * width * 12,
            transcendentals=rows * states * HEADS,
            bytes_accessed=group * width * (rows * 4 + states * 4),
        ),
        name="cross_forward",
    )(queries, pairs)
    return of_heads(mixed, group), total


def cross_backward(queries, pairs, mixed_grad, mixed, total):
    group, _, states, width = pairs.shape
    rows = queries.shape[0]
    queries, spec = by_head(queries, group)
    mixed_grad, mixed = by_head(mixed_grad, group)[0], by_head(mixed, group)[0]
    pair_spec = pl.BlockSpec((None, 2, states, width), lambda g: (g, 0, 0, 0))
    query_grad, pair_grad = pl.pallas_call(
        functools.partial(cross_backward_kernel, width, HEAD_DIM ** (-0.5)),
        out_shape=(
            jax.ShapeDtypeStruct(queries.shape, low_type),
            jax.ShapeDtypeStruct(pairs.shape, low_type),
        ),
        grid=(group,),
        in_specs=[spec, pair_spec, spec, spec, pl.BlockSpec((None, 8, rows), lambda g: (g, 0, 0))],
        out_specs=[spec, pair_spec],
        compiler_params=kernel_options(32),
        cost_estimate=pl.CostEstimate(
            flops=rows * states * group * width * 30,
            transcendentals=rows * states * HEADS,
            bytes_accessed=group * width * (rows * 8 + states * 8),
        ),
        name="cross_backward",
    )(queries, pairs, mixed_grad, mixed, total)
    return of_heads(query_grad, group), pair_grad


def flip(values, axis_bit):
    axis, bit = axis_bit
    size = lax.axis_size(axis)
    return lax.ppermute(values, axis, [(i, i ^ bit) for i in range(size)])


def bits_of(axis):
    size = lax.axis_size(axis)
    return [(axis, 1 << i) for i in range(size.bit_length() - 1)]


def sum_over(values, bits):
    for bit in bits:
        values = (
            values.astype(jnp.float32) + flip(values, bit).astype(jnp.float32)
        ).astype(values.dtype)
    return values


def sum_over_rep(values):
    bits = bits_of("rep")
    middle = values.shape[0] // 2
    return jnp.concatenate(
        [sum_over(values[:middle], bits), sum_over(values[middle:], bits[::-1])], 0
    )


def gather_rows(values):
    return lax.all_gather(values, "shard", axis=0, tiled=True)


def exchange(values):
    return lax.all_to_all(values, "shard", split_axis=0, concat_axis=0, tiled=True)


def reduce_weight(former, latter):
    reduced = lax.psum_scatter(
        product_left(former, latter).astype(low_type), "shard", scatter_dimension=0, tiled=True
    )
    return sum_over_rep(reduced).astype(jnp.float32)


def local(
    layer_input,
    encoder_states,
    out_grad,
    placement,
    w_self_qkv,
    w_self_out,
    w_cross_q,
    w_cross_kv,
    w_cross_out,
    w_fc1,
    w_fc2,
    proj_biases,
    fc1_bias,
    norm_gains,
    norm_shifts,
):
    group = lax.axis_size("shard")
    member = lax.axis_index("shard")
    tok, model = layer_input.shape
    weight_rows = w_self_qkv.shape[0]
    width = model // group
    score_scale = HEAD_DIM ** (-0.5)
    slot_table = placement[0]
    device_ids = jnp.arange(group, dtype=jnp.int32)
    owners = jnp.sum(
        jnp.where(slot_table[None, :] == device_ids[:, None], device_ids[None, :], 0), 1
    )

    def own_columns(row):
        return lax.dynamic_slice(row, (member * width,), (width,))

    def in_columns(row):
        return lax.dynamic_update_slice(jnp.zeros((model,), jnp.float32), row, (member * width,))

    slices = jnp.concatenate(
        [
            w_self_qkv.reshape(weight_rows, 3, group, width),
            w_cross_kv.reshape(weight_rows, 2, group, width),
        ],
        1,
    )
    slices = slices.transpose(2, 0, 1, 3).reshape(group, weight_rows, 5 * width)
    slices = exchange(slices).reshape(model, 5 * width)
    head_qkv, head_ckv = slices[:, : 3 * width], slices[:, 3 * width :]
    all_inputs = gather_rows(layer_input)
    all_states = gather_rows(encoder_states)
    full_out = gather_rows(w_self_out)
    full_cross_q = gather_rows(w_cross_q)
    full_cross_out = gather_rows(w_cross_out)
    wfirst = gather_rows(w_fc1)
    wsecond = gather_rows(w_fc2)

    inputs = layer_input.astype(jnp.float32)
    zeros = jnp.zeros((width,), jnp.float32)
    head_bias = jnp.concatenate([own_columns(proj_biases[0]), zeros, own_columns(proj_biases[1])])
    head_scale = jnp.concatenate([jnp.full((width,), score_scale), jnp.ones((2 * width,))])
    qkv = ((product(all_inputs, head_qkv) + head_bias) * head_scale).astype(low_type)
    key_t, value_t = jnp.transpose(qkv[:, width : 2 * width]), jnp.transpose(qkv[:, 2 * width :])
    head_mixed, self_total = self_forward(owners, qkv, value_t, tok)
    self_low = join_columns(exchange(head_mixed.reshape(group, tok, width)))

    cross_bias = jnp.concatenate([zeros, own_columns(proj_biases[4])])
    head_pair = (product(all_states, head_ckv) + cross_bias).astype(low_type)
    states = all_states.shape[0]
    head_pair = split_columns(head_pair, 2)
    pairs = lax.all_gather(head_pair, "shard", axis=0, tiled=False)

    first_sum = inputs + (product(self_low, full_out) + proj_biases[2])
    first_norm, norm1_back = jax.vjp(norm_rows, first_sum, norm_gains[0], norm_shifts[0])
    first_low = first_norm.astype(low_type)
    cross_queries = ((product(first_low, full_cross_q) + proj_biases[3]) * score_scale).astype(
        low_type
    )
    cross_low, cross_total = cross_forward(cross_queries, pairs)
    second_sum = first_norm + (product(cross_low, full_cross_out) + proj_biases[5])
    second_norm, norm2_back = jax.vjp(norm_rows, second_sum, norm_gains[1], norm_shifts[1])
    second_low = second_norm.astype(low_type)
    pre_act = product(second_low, wfirst) + fc1_bias
    hidden, gelu_back = jax.vjp(lambda values: jax.nn.gelu(values, approximate=False), pre_act)
    hidden_low = hidden.astype(low_type)
    third_sum = second_norm + (product(hidden_low, wsecond) + proj_biases[6])
    result, norm3_back = jax.vjp(norm_rows, third_sum, norm_gains[2], norm_shifts[2])
    output = result.astype(low_type)

    third_grad, gain_three, shift_three = norm3_back(out_grad.astype(jnp.float32))
    feed_grad = third_grad.astype(low_type)
    grad_fc2 = reduce_weight(hidden_low, feed_grad)
    bias_fc2 = column_sums(feed_grad)
    pre_grad = gelu_back(product_right(feed_grad, wsecond))[0].astype(low_type)
    grad_fc1 = reduce_weight(second_low, pre_grad)
    bias_fc1 = column_sums(pre_grad)
    second_grad, gain_two, shift_two = norm2_back(third_grad + product_right(pre_grad, wfirst))
    cross_out_grad = second_grad.astype(low_type)
    grad_cross_out = reduce_weight(cross_low, cross_out_grad)
    bias_cross_out = column_sums(cross_out_grad)
    cross_mixed_grad = product_right(cross_out_grad, full_cross_out).astype(low_type)
    cross_q_grad, pair_grad = cross_backward(
        cross_queries, pairs, cross_mixed_grad, cross_low, cross_total
    )
    own_pair_grad = join_columns(
        lax.psum_scatter(pair_grad, "shard", scatter_dimension=0, tiled=False)
    )
    grad_cross_q = reduce_weight(first_low, cross_q_grad)
    bias_cross_q = column_sums(cross_q_grad)
    bias_cross_v = in_columns(column_sums(own_pair_grad[:, width:]))
    enc_grad = lax.psum_scatter(
        product_right(own_pair_grad, head_ckv).astype(low_type),
        "shard",
        scatter_dimension=0,
        tiled=True,
    ).astype(jnp.float32)
    first_grad, gain_one, shift_one = norm1_back(
        second_grad + product_right(cross_q_grad, full_cross_q)
    )
    self_out_grad = first_grad.astype(low_type)
    grad_self_out = reduce_weight(self_low, self_out_grad)
    bias_self_out = column_sums(self_out_grad)
    self_mixed_grad = product_right(self_out_grad, full_out).astype(low_type)
    head_grad = exchange(split_columns(self_mixed_grad, group)).reshape(group * tok, width)
    qkv_grad = self_backward(owners, qkv, key_t, head_grad, head_mixed, self_total, tok)
    input_part = lax.psum_scatter(
        product_right(qkv_grad, head_qkv).astype(low_type),
        "shard",
        scatter_dimension=0,
        tiled=True,
    )
    input_grad = first_grad + input_part.astype(jnp.float32)
    slice_grad = jnp.concatenate(
        [product_left(all_inputs, qkv_grad), product_left(all_states, own_pair_grad)], 1
    ).astype(low_type)
    slice_grad = sum_over_rep(slice_grad).reshape(group, weight_rows, 5 * width)
    slice_grad = exchange(slice_grad).astype(jnp.float32)
    slice_grad = slice_grad.reshape(group, weight_rows, 5, width).transpose(1, 2, 0, 3)
    slice_grad = slice_grad.reshape(weight_rows, 5 * model)
    grad_self_qkv, grad_cross_kv = slice_grad[:, : 3 * model], slice_grad[:, 3 * model :]
    bias_self_q = in_columns(column_sums(qkv_grad[:, :width]))
    bias_self_v = in_columns(column_sums(qkv_grad[:, 2 * width :]))
    everywhere = bits_of("rep") + bits_of("shard")
    small = jnp.concatenate(
        [
            jnp.stack(
                [
                    bias_self_q,
                    bias_self_v,
                    bias_self_out,
                    bias_cross_q,
                    bias_cross_v,
                    bias_cross_out,
                    bias_fc2,
                    gain_one,
                    gain_two,
                    gain_three,
                    shift_one,
                    shift_two,
                    shift_three,
                ],
                0,
            ),
            bias_fc1.reshape(-1, model),
        ],
        0,
    )
    small = sum_over(small, everywhere)
    return (
        output,
        input_grad,
        enc_grad,
        grad_self_qkv,
        grad_self_out,
        grad_cross_q,
        grad_cross_kv,
        grad_cross_out,
        grad_fc1,
        grad_fc2,
        small[:7],
        small[13:].reshape(-1),
        small[7:10],
        small[10:13],
    )


def solution(mesh):
    rows, cut = P(("rep", "shard"), None), P("shard", None)
    return jax.shard_map(
        local,
        mesh=mesh,
        in_specs=(rows,) * 3 + (P("rep", None),) + (cut,) * 7 + (P(),) * 4,
        out_specs=(rows,) * 3 + (cut,) * 7 + (P(),) * 4,
        check_vma=False,
    )
```

```python
import functools

import jax
import jax.numpy as jnp
from jax import lax
from jax.experimental import pallas as pl
from jax.experimental.pallas import tpu as pltpu
from jax.sharding import PartitionSpec as P

HEADS = 16
HEAD_DIM = 64
LANES = 128

masked_score = -1000000000.0
norm_epsilon = 1e-05
low_type = jnp.bfloat16
SHARD = ("line", "core")


def norm_rows(values, gain_row, shift_row):
    row_mean = jnp.mean(values, -1, keepdims=True)
    centered = values - row_mean
    variance = jnp.mean(centered * centered, -1, keepdims=True)
    return centered * lax.rsqrt(variance + norm_epsilon) * gain_row + shift_row


def product(former, latter):
    return jnp.dot(former, latter, preferred_element_type=jnp.float32)


def product_left(former, latter):
    return lax.dot_general(
        former, latter, (((0,), (0,)), ((), ())), preferred_element_type=jnp.float32
    )


def product_right(former, latter):
    return lax.dot_general(
        former, latter, (((1,), (1,)), ((), ())), preferred_element_type=jnp.float32
    )


def column_sums(values):
    return jnp.sum(values.astype(jnp.float32), 0)


def head_columns(index):
    return slice(index * HEAD_DIM, (index + 1) * HEAD_DIM)


def causal_rows(keys, queries):
    key_index = lax.broadcasted_iota(jnp.int32, (keys, queries), 0)
    query_index = lax.broadcasted_iota(jnp.int32, (keys, queries), 1)
    return key_index <= query_index


def turn_columns(source, start, out, tok):
    width, rows = out.shape
    for row in range(0, rows, tok):
        block = source[row : row + tok, start : start + width]
        out[:, row : row + tok] = jnp.transpose(block)


def self_forward_kernel(tok, width, half, place, owner, *refs):
    blocks, (weight, bias, scale, qkv, mixed, total, value_t) = refs[:-7], refs[-7:]
    slot = pl.program_id(0)
    heads = width // HEAD_DIM

    @pl.when(slot == 0)
    def _():
        for index, block in enumerate(blocks):
            rows = (product(block[...], weight[...]) + bias[...]) * scale[...]
            qkv[index * tok : (index + 1) * tok, :] = rows.astype(low_type)
        turn_columns(qkv, 2 * width, value_t, tok)

    base = pl.multiple_of(place[slot] * tok, tok)
    query = qkv[pl.ds(base, tok), :width]

    def step(start, carry, causal):
        keys = qkv[pl.ds(start, tok), width : 2 * width]
        values = value_t[:, pl.ds(start, tok)]
        result = []
        for head in range(heads):
            top, weight, mix = carry[head]
            cols = head_columns(head)
            scores = product_right(keys[:, cols], query[:, cols])
            if causal:
                scores = jnp.where(causal_rows(tok, tok), scores, masked_score)
            new_top = jnp.maximum(top, jnp.max(scores, 0, keepdims=True))
            scale = jnp.exp(top - new_top)
            power = jnp.exp(scores - new_top)
            weight = weight * scale + jnp.sum(power, 0, keepdims=True)
            mix = mix * scale + product(values[cols], power.astype(low_type))
            result.append((new_top, weight, mix))
        return tuple(result)

    first = tuple(
        (
            jnp.full((1, tok), -1e30, jnp.float32),
            jnp.zeros((1, tok), jnp.float32),
            jnp.zeros((HEAD_DIM, tok), jnp.float32),
        )
        for _ in range(heads)
    )
    whole = jnp.minimum(slot, half)
    carry = lax.fori_loop(
        0, whole, lambda j, c: step(pl.multiple_of(place[j] * tok, tok), c, False), first
    )
    carry = step(base, carry, True)
    mix = jnp.concatenate([part[2] / part[1] for part in carry], 0)
    target = pl.multiple_of(owner[slot] * tok, tok)
    mixed[pl.ds(target, tok), :] = jnp.transpose(mix).astype(low_type)
    for head in range(heads):
        total[head : head + 1, :] = carry[head][0] + jnp.log(carry[head][1])


def self_backward_kernel(
    tok,
    width,
    half,
    scale,
    place,
    owner,
    qkv,
    mixed_grad,
    mixed,
    total,
    out,
    placed,
    key_t,
    key_sum,
    value_sum,
):
    slot = pl.program_id(0)
    heads = width // HEAD_DIM

    @pl.when(slot == 0)
    def _():
        turn_columns(qkv, width, key_t, tok)
        key_sum[...] = jnp.zeros_like(key_sum)
        value_sum[...] = jnp.zeros_like(value_sum)

    base = pl.multiple_of(place[slot] * tok, tok)
    target = pl.multiple_of(owner[slot] * tok, tok)
    query = qkv[pl.ds(base, tok), :width]
    grad = mixed_grad[pl.ds(target, tok), :]
    both = grad.astype(jnp.float32) * mixed[pl.ds(target, tok), :].astype(jnp.float32)
    both = jnp.transpose(both)
    deltas = [jnp.sum(both[head_columns(h)], 0, keepdims=True) for h in range(heads)]
    totals = [total[h : h + 1, :] for h in range(heads)]

    def step(start, carry, causal):
        keys = qkv[pl.ds(start, tok), width : 2 * width]
        values = qkv[pl.ds(start, tok), 2 * width :]
        keys_t = key_t[:, pl.ds(start, tok)]
        result, key_parts, value_parts = [], [], []
        for head in range(heads):
            cols = head_columns(head)
            scores = product_right(keys[:, cols], query[:, cols])
            power = jnp.exp(scores - totals[head])
            if causal:
                power = jnp.where(causal_rows(tok, tok), power, 0.0)
            slope = product_right(values[:, cols], grad[:, cols])
            score_grad = (power * (slope - deltas[head])).astype(low_type)
            value_parts.append(product(power.astype(low_type), grad[:, cols]))
            key_parts.append(product(score_grad, query[:, cols]))
            result.append(carry[head] + product(keys_t[cols], score_grad))
        key_sum[pl.ds(start, tok), :] += jnp.concatenate(key_parts, 1)
        value_sum[pl.ds(start, tok), :] += jnp.concatenate(value_parts, 1)
        return tuple(result)

    first = tuple(jnp.zeros((HEAD_DIM, tok), jnp.float32) for _ in range(heads))
    whole = jnp.minimum(slot, half)
    carry = lax.fori_loop(
        0, whole, lambda j, c: step(pl.multiple_of(place[j] * tok, tok), c, False), first
    )
    carry = step(base, carry, True)
    query_grad = jnp.transpose(jnp.concatenate(carry, 0)).astype(low_type) * scale
    placed[pl.ds(base, tok), :width] = query_grad

    @pl.when(slot == pl.num_programs(0) - 1)
    def _():
        placed[:, width : 2 * width] = key_sum[...].astype(low_type)
        placed[:, 2 * width :] = value_sum[...].astype(low_type)

        def move(p, carry):
            source = pl.multiple_of(place[p] * tok, tok)
            out[pl.ds(pl.multiple_of(owner[p] * tok, tok), tok), :] = placed[
                pl.ds(source, tok), :
            ]
            return carry

        lax.fori_loop(0, pl.num_programs(0), move, 0)


def cross_forward_kernel(width, query, pair, mixed, total):
    keys, values = pair[0], jnp.transpose(pair[1])
    mixes = []
    for head in range(width // HEAD_DIM):
        cols = head_columns(head)
        scores = product_right(keys[:, cols], query[:, cols])
        top = jnp.max(scores, 0, keepdims=True)
        power = jnp.exp(scores - top)
        weight = jnp.sum(power, 0, keepdims=True)
        mixes.append(product(values[cols], power.astype(low_type)) / weight)
        total[head : head + 1, :] = top + jnp.log(weight)
    mixed[...] = jnp.transpose(jnp.concatenate(mixes, 0)).astype(low_type)


def cross_backward_kernel(width, scale, query, pair, mixed_grad, mixed, total, out, pair_grad):
    heads = width // HEAD_DIM
    keys, values = pair[0], pair[1]
    keys_t = jnp.transpose(keys)
    grad = mixed_grad[...]
    both = jnp.transpose(grad.astype(jnp.float32) * mixed[...].astype(jnp.float32))
    query_parts, key_parts, value_parts = [], [], []
    for head in range(heads):
        cols = head_columns(head)
        scores = product_right(keys[:, cols], query[:, cols])
        power = jnp.exp(scores - total[head : head + 1, :])
        slope = product_right(values[:, cols], grad[:, cols])
        delta = jnp.sum(both[cols], 0, keepdims=True)
        score_grad = (power * (slope - delta)).astype(low_type)
        value_parts.append(product(power.astype(low_type), grad[:, cols]))
        key_parts.append(product(score_grad, query[:, cols]))
        query_parts.append(product(keys_t[cols], score_grad))
    query_grad = jnp.transpose(jnp.concatenate(query_parts, 0)).astype(low_type)
    out[...] = query_grad * scale
    pair_grad[0] = jnp.concatenate(key_parts, 1).astype(low_type)
    pair_grad[1] = jnp.concatenate(value_parts, 1).astype(low_type)


def kernel_options(megabytes):
    return pltpu.CompilerParams(
        dimension_semantics=("arbitrary",), vmem_limit_bytes=megabytes * 2**20
    )


def whole_block(shape):
    return pl.BlockSpec(shape, lambda *_: (0,) * len(shape), pipeline_mode=pl.Buffered(1))


def self_forward(place, owner, blocks, weight, bias, scale):
    tok, group = blocks[0].shape[0], len(blocks)
    width = weight.shape[1] // 3
    rows = group * tok
    pairs = group * (group // 4 + 1)
    bias, scale = bias[None], scale[None]
    inputs = (*blocks, weight, bias, scale)
    return pl.pallas_call(
        functools.partial(self_forward_kernel, tok, width, group // 2),
        out_shape=(
            jax.ShapeDtypeStruct((rows, 3 * width), low_type),
            jax.ShapeDtypeStruct((rows, width), low_type),
            jax.ShapeDtypeStruct((group, 8, tok), jnp.float32),
        ),
        grid_spec=pltpu.PrefetchScalarGridSpec(
            num_scalar_prefetch=2,
            grid=(group,),
            in_specs=[whole_block(each.shape) for each in inputs],
            out_specs=[
                pl.BlockSpec((rows, 3 * width), lambda *_: (0, 0)),
                pl.BlockSpec((rows, width), lambda *_: (0, 0)),
                pl.BlockSpec((None, 8, tok), lambda p, *_: (p, 0, 0)),
            ],
            scratch_shapes=[pltpu.VMEM((width, rows), low_type)],
        ),
        compiler_params=kernel_options(52),
        cost_estimate=pl.CostEstimate(
            flops=pairs * tok * tok * width * 12,
            transcendentals=pairs * tok * tok * (width // HEAD_DIM),
            bytes_accessed=rows * (width * 10 + weight.shape[0] * 2),
        ),
        name="self_forward",
    )(place, owner, *inputs)


def self_backward(place, owner, qkv, mixed_grad, mixed, total, tok):
    rows, width = qkv.shape[0], qkv.shape[1] // 3
    group = rows // tok
    pairs = group * (group // 4 + 1)
    return pl.pallas_call(
        functools.partial(
            self_backward_kernel, tok, width, group // 2, HEAD_DIM ** (-0.5)
        ),
        out_shape=(
            jax.ShapeDtypeStruct(qkv.shape, low_type),
            jax.ShapeDtypeStruct(qkv.shape, low_type),
        ),
        grid_spec=pltpu.PrefetchScalarGridSpec(
            num_scalar_prefetch=2,
            grid=(group,),
            in_specs=[
                whole_block(qkv.shape),
                whole_block(mixed_grad.shape),
                whole_block(mixed.shape),
                pl.BlockSpec((None, 8, tok), lambda p, *_: (p, 0, 0)),
            ],
            out_specs=[pl.BlockSpec(qkv.shape, lambda *_: (0, 0))] * 2,
            scratch_shapes=[
                pltpu.VMEM((width, rows), low_type),
                pltpu.VMEM((rows, width), jnp.float32),
                pltpu.VMEM((rows, width), jnp.float32),
            ],
        ),
        compiler_params=kernel_options(52),
        cost_estimate=pl.CostEstimate(
            flops=pairs * tok * tok * width * 30,
            transcendentals=pairs * tok * tok * (width // HEAD_DIM),
            bytes_accessed=rows * width * 20,
        ),
        name="self_backward",
    )(place, owner, qkv, mixed_grad, mixed, total)


def split_columns(values, group):
    rows = values.shape[0]
    return values.reshape(rows, group, -1).transpose(1, 0, 2)


def join_columns(values):
    return values.transpose(1, 0, 2).reshape(values.shape[1], -1)


def by_head(values, group):
    rows, width = values.shape[0], values.shape[1] // group
    if width % LANES == 0:
        return values, pl.BlockSpec((rows, width), lambda g: (0, g))
    return split_columns(values, group), pl.BlockSpec((None, rows, width), lambda g: (g, 0, 0))


def of_heads(values, group):
    return values if values.ndim == 2 else join_columns(values)


def cross_forward(queries, pairs):
    group, _, states, width = pairs.shape
    rows = queries.shape[0]
    queries, query_spec = by_head(queries, group)
    mixed, total = pl.pallas_call(
        functools.partial(cross_forward_kernel, width),
        out_shape=(
            jax.ShapeDtypeStruct(queries.shape, low_type),
            jax.ShapeDtypeStruct((group, 8, rows), jnp.float32),
        ),
        grid=(group,),
        in_specs=[query_spec, pl.BlockSpec((None, 2, states, width), lambda g: (g, 0, 0, 0))],
        out_specs=[query_spec, pl.BlockSpec((None, 8, rows), lambda g: (g, 0, 0))],
        compiler_params=kernel_options(32),
        cost_estimate=pl.CostEstimate(
            flops=rows * states * group * width * 12,
            transcendentals=rows * states * HEADS,
            bytes_accessed=group * width * (rows * 4 + states * 4),
        ),
        name="cross_forward",
    )(queries, pairs)
    return of_heads(mixed, group), total


def cross_backward(queries, pairs, mixed_grad, mixed, total):
    group, _, states, width = pairs.shape
    rows = queries.shape[0]
    queries, spec = by_head(queries, group)
    mixed_grad, mixed = by_head(mixed_grad, group)[0], by_head(mixed, group)[0]
    pair_spec = pl.BlockSpec((None, 2, states, width), lambda g: (g, 0, 0, 0))
    query_grad, pair_grad = pl.pallas_call(
        functools.partial(cross_backward_kernel, width, HEAD_DIM ** (-0.5)),
        out_shape=(
            jax.ShapeDtypeStruct(queries.shape, low_type),
            jax.ShapeDtypeStruct(pairs.shape, low_type),
        ),
        grid=(group,),
        in_specs=[spec, pair_spec, spec, spec, pl.BlockSpec((None, 8, rows), lambda g: (g, 0, 0))],
        out_specs=[spec, pair_spec],
        compiler_params=kernel_options(32),
        cost_estimate=pl.CostEstimate(
            flops=rows * states * group * width * 30,
            transcendentals=rows * states * HEADS,
            bytes_accessed=group * width * (rows * 8 + states * 8),
        ),
        name="cross_backward",
    )(queries, pairs, mixed_grad, mixed, total)
    return of_heads(query_grad, group), pair_grad


def swap(values, axis, offset):
    size = lax.axis_size(axis)
    return lax.ppermute(values, axis, [(i, i ^ offset) for i in range(size)])


def sum_over(values, steps):
    for axis, offset in steps:
        values = (
            values.astype(jnp.float32) + swap(values, axis, offset).astype(jnp.float32)
        ).astype(values.dtype)
    return values


def bits_of(axis):
    return [(axis, 1 << i) for i in range(lax.axis_size(axis).bit_length() - 1)]


def spread_over_rep(values):
    return [values] + [swap(values, "rep", d) for d in range(1, lax.axis_size("rep"))]


def rep_order(pieces):
    own = lax.axis_index("rep")
    count = len(pieces)
    return [lax.select_n(own, *[pieces[d ^ i] for i in range(count)]) for d in range(count)]


def trade_over_rep(pieces):
    return [pieces[0]] + [swap(pieces[d], "rep", d) for d in range(1, len(pieces))]


def sum_of(terms):
    return sum(term.astype(jnp.float32) for term in terms)


def scatter_over_line(values):
    line, own = lax.axis_size("line"), lax.axis_index("line")
    terms = [lax.dynamic_index_in_dim(values, own, 0, keepdims=False)]
    for k in range(1, line):
        piece = lax.dynamic_index_in_dim(values, (own + k) % line, 0, keepdims=False)
        terms.append(lax.ppermute(piece, "line", [(i, (i + k) % line) for i in range(line)]))
    return sum_of(terms)


def stage(values):
    return lax.optimization_barrier(values)


def shift(values):
    line = lax.axis_size("line")
    return lax.ppermute(values, "line", [(i, (i + 1) % line) for i in range(line)])


def gather_rows(values):
    return lax.all_gather(values, SHARD, axis=0, tiled=True)


def scatter_rows(values):
    return lax.psum_scatter(values, SHARD, scatter_dimension=0, tiled=True)


def exchange(values):
    return lax.all_to_all(values, SHARD, split_axis=0, concat_axis=0, tiled=True)


def gelu(values):
    return jax.nn.gelu(values, approximate=False)


def local(
    layer_input,
    encoder_states,
    out_grad,
    placement,
    w_self_qkv,
    w_self_out,
    w_cross_q,
    w_cross_kv,
    w_cross_out,
    w_fc1,
    w_fc2,
    proj_biases,
    fc1_bias,
    norm_gains,
    norm_shifts,
):
    reps, line = lax.axis_size("rep"), lax.axis_size("line")
    rep, core = lax.axis_index("rep"), lax.axis_index("core")
    group = 2 * line
    member = 2 * lax.axis_index("line") + core
    tok, model = layer_input.shape
    feed = w_fc1.shape[1]
    weight_rows = w_self_qkv.shape[0]
    width = model // group
    unit = feed // (group * reps)
    score_scale = HEAD_DIM ** (-0.5)
    slot_table = placement[0]
    device_ids = jnp.arange(group, dtype=jnp.int32)
    owners = jnp.sum(
        jnp.where(slot_table[None, :] == device_ids[:, None], device_ids[None, :], 0), 1
    )

    def own_columns(row):
        return lax.dynamic_slice(row, (member * width,), (width,))

    def in_columns(row):
        return lax.dynamic_update_slice(jnp.zeros((model,), jnp.float32), row, (member * width,))

    slices = jnp.concatenate(
        [
            w_self_qkv.reshape(reps, weight_rows // reps, 3, group, width),
            w_cross_kv.reshape(reps, weight_rows // reps, 2, group, width),
        ],
        2,
    )
    slices = lax.dynamic_index_in_dim(slices, rep, 0, keepdims=False)
    slices = slices.transpose(2, 0, 1, 3).reshape(group, weight_rows // reps, 5 * width)
    first_cut = w_fc1.reshape(weight_rows, line, 2, reps, unit)
    first_cut = lax.dynamic_index_in_dim(first_cut, rep, 3, keepdims=False)
    first_own = lax.dynamic_index_in_dim(first_cut, core, 2, keepdims=False)
    first_other = lax.dynamic_index_in_dim(first_cut, 1 - core, 2, keepdims=False)
    first_own = first_own.reshape(weight_rows, line * unit)
    first_other = swap(first_other.reshape(weight_rows, line * unit), "core", 1)
    first_cut = jnp.where(
        core == 0,
        jnp.concatenate([first_own, first_other], 0),
        jnp.concatenate([first_other, first_own], 0),
    )
    second_cut = lax.dynamic_slice_in_dim(w_fc2, rep * unit, unit, 0)
    bias_cut = lax.dynamic_index_in_dim(
        fc1_bias.reshape(line, 2, reps, unit), core, 1, keepdims=False
    )
    bias_cut = [bias_cut[:, r].reshape(line * unit) for r in range(reps)]
    bias_cut = rep_order(bias_cut)

    square = jnp.stack([w_self_out, w_cross_q, w_cross_out], 0)
    square = square.reshape(3, reps, weight_rows // reps, model)
    square = lax.dynamic_index_in_dim(square, rep, 1, keepdims=False)
    square = square.reshape(-1, model // (line * unit), line * unit).transpose(1, 0, 2)
    square = square.reshape(-1, line * unit)

    inputs = layer_input.astype(jnp.float32)
    zeros = jnp.zeros((width,), jnp.float32)
    head_bias = jnp.concatenate([own_columns(proj_biases[0]), zeros, own_columns(proj_biases[1])])
    head_scale = jnp.concatenate([jnp.full((width,), score_scale), jnp.ones((2 * width,))])
    cross_bias = jnp.concatenate([zeros, own_columns(proj_biases[4])])

    slices = exchange(slices)
    both_cut = lax.all_gather(
        jnp.concatenate([first_cut, square], 0), "line", axis=0, tiled=True
    ).reshape(line, -1, line * unit)
    near, far = [1 << i for i in range(reps.bit_length() - 1)], []
    far = [d for d in range(1, reps) if d not in near]
    block, slices, both_cut = stage((layer_input, slices, both_cut))

    blocks = [block, swap(block, "core", 1)]
    block = shift(block)
    slices = spread_over_rep(slices)
    block, slices, blocks, encoder_states = stage((block, slices, blocks, encoder_states))

    blocks += [block, swap(block, "core", 1)]
    block = shift(block)
    square = spread_over_rep(both_cut[:, 2 * weight_rows :])
    slices = jnp.stack(rep_order(slices), 1).reshape(model, 5 * width)
    head_qkv, head_ckv = slices[:, : 3 * width], slices[:, 3 * width :]
    all_states = gather_rows(encoder_states)
    block, square, blocks, all_states, head_ckv, head_qkv = stage(
        (block, square, blocks, all_states, head_ckv, head_qkv)
    )

    for step in range(line - 2):
        blocks += [block, swap(block, "core", 1)]
        if step < line - 3:
            block = shift(block)
    wfirst = {0: both_cut[:, : 2 * weight_rows].reshape(model, line * unit)}
    wfirst.update({d: swap(wfirst[0], "rep", d) for d in near})
    square = jnp.stack(rep_order(square), 1)
    other = swap(square, "core", 1)
    head_pair = (product(all_states, head_ckv) + cross_bias).astype(low_type)
    head_pair = split_columns(head_pair, 2)
    blocks, wfirst, other, square, head_pair, second_cut = stage(
        (blocks, wfirst, other, square, head_pair, second_cut)
    )

    wfirst.update({d: swap(wfirst[0], "rep", d) for d in far})
    wsecond = {0: lax.all_gather(second_cut, "line", axis=0, tiled=True)}
    back = (lax.axis_index("line") - owners // 2) % line
    places = 2 * back + ((owners % 2) ^ core)
    qkv, head_mixed, self_total = self_forward(
        places, owners, blocks, head_qkv, head_bias, head_scale
    )
    all_inputs = jnp.concatenate(blocks, 0)
    square = jnp.where(core == 0, jnp.stack([square, other], 1), jnp.stack([other, square], 1))
    square = square.reshape(line, 2, reps, -1, 3, weight_rows // reps, line * unit)
    full_out, full_cross_q, full_cross_out = [
        square[:, :, :, :, i].transpose(0, 1, 2, 4, 3, 5).reshape(model, model)
        for i in range(3)
    ]
    head_mixed, wfirst, wsecond = stage((head_mixed, wfirst, wsecond))

    wsecond.update({d: swap(wsecond[0], "rep", d) for d in near})
    pairs = lax.all_gather(head_pair, SHARD, axis=0, tiled=False)
    self_low = exchange(head_mixed.reshape(group, tok, width))
    self_low, wsecond, pairs, all_inputs = stage((self_low, wsecond, pairs, all_inputs))
    wsecond.update({d: swap(wsecond[0], "rep", d) for d in far})
    self_low = join_columns(self_low)

    first_sum = inputs + (product(self_low, full_out) + proj_biases[2])
    first_norm, norm1_back = jax.vjp(norm_rows, first_sum, norm_gains[0], norm_shifts[0])
    first_low = first_norm.astype(low_type)
    cross_queries = ((product(first_low, full_cross_q) + proj_biases[3]) * score_scale).astype(
        low_type
    )
    cross_low, cross_total = cross_forward(cross_queries, pairs)
    cross_low, wsecond = stage((cross_low, wsecond))
    second_sum = first_norm + (product(cross_low, full_cross_out) + proj_biases[5])
    second_norm, norm2_back = jax.vjp(norm_rows, second_sum, norm_gains[1], norm_shifts[1])
    second_low = second_norm.astype(low_type)

    second_both = jnp.concatenate([second_low, swap(second_low, "core", 1)], 0)
    feed_sum, hidden, gelu_back = 0.0, [], []
    for part in range(reps):
        active, back = jax.vjp(gelu, product(second_both, wfirst[part]) + bias_cut[part])
        hidden.append(active.astype(low_type))
        gelu_back.append(back)
        feed_sum = feed_sum + product(hidden[part], wsecond[part])
    feed_other = swap(feed_sum[tok:].astype(low_type), "core", 1).astype(jnp.float32)
    third_sum = second_norm + (feed_sum[:tok] + feed_other + proj_biases[6])
    result, norm3_back = jax.vjp(norm_rows, third_sum, norm_gains[2], norm_shifts[2])
    output = result.astype(low_type)

    third_grad, gain_three, shift_three = norm3_back(out_grad.astype(jnp.float32))
    feed_grad = third_grad.astype(low_type)
    bias_fc2 = column_sums(feed_grad)
    feed_both = jnp.concatenate([feed_grad, swap(feed_grad, "core", 1)], 0)
    second_parts = [
        product_left(hidden[part], feed_both).astype(low_type) for part in range(reps)
    ]
    feed_both, second_parts = stage((feed_both, second_parts))
    second_terms = trade_over_rep(second_parts)
    back_sum, first_parts, bias_parts = 0.0, [], []
    for part in range(reps):
        pre_grad = gelu_back[part](product_right(feed_both, wsecond[part]))[0].astype(low_type)
        first_parts.append(product_left(second_both, pre_grad).astype(low_type))
        bias_parts.append(column_sums(pre_grad))
        back_sum = back_sum + product_right(pre_grad, wfirst[part])
    back_other = swap(back_sum[tok:].astype(low_type), "core", 1).astype(jnp.float32)
    second_grad, gain_two, shift_two = norm2_back(third_grad + (back_sum[:tok] + back_other))
    second_grad, first_parts = stage((second_grad, first_parts))
    first_terms = trade_over_rep(first_parts)

    cross_out_grad = second_grad.astype(low_type)
    part_cross_out = product_left(cross_low, cross_out_grad).astype(low_type)
    bias_cross_out = column_sums(cross_out_grad)
    cross_mixed_grad = product_right(cross_out_grad, full_cross_out).astype(low_type)
    cross_q_grad, pair_grad = cross_backward(
        cross_queries, pairs, cross_mixed_grad, cross_low, cross_total
    )
    cross_q_grad, second_terms = stage((cross_q_grad, second_terms))
    second_sums = lax.psum_scatter(
        sum_of(second_terms).astype(low_type), "line", scatter_dimension=0, tiled=True
    )
    own_pair_grad = lax.psum_scatter(pair_grad, SHARD, scatter_dimension=0, tiled=False)
    part_cross_q = product_left(first_low, cross_q_grad).astype(low_type)
    bias_cross_q = column_sums(cross_q_grad)
    first_grad, gain_one, shift_one = norm1_back(
        second_grad + product_right(cross_q_grad, full_cross_q)
    )
    self_out_grad = first_grad.astype(low_type)
    bias_self_out = column_sums(self_out_grad)
    self_mixed_grad = product_right(self_out_grad, full_out).astype(low_type)
    head_grad = exchange(split_columns(self_mixed_grad, group))
    part_self_out = product_left(self_low, self_out_grad).astype(low_type)

    square = jnp.stack([part_self_out, part_cross_q, part_cross_out], 0)
    square = square.reshape(3, line, 2, reps, weight_rows // reps, model)
    other = swap(lax.dynamic_index_in_dim(square, 1 - core, 2, keepdims=False), "core", 1)
    square = lax.dynamic_index_in_dim(square, core, 2, keepdims=False)
    square = (square.astype(jnp.float32) + other.astype(jnp.float32)).astype(low_type)
    square = rep_order([square[:, :, r] for r in range(reps)])
    head_grad, square, first_terms, own_pair_grad = stage(
        (head_grad, square, first_terms, own_pair_grad)
    )
    square_terms = trade_over_rep(square)
    first_sums = lax.psum_scatter(
        sum_of(first_terms).astype(low_type), "line", scatter_dimension=0, tiled=True
    )
    own_pair_grad = join_columns(own_pair_grad)
    enc_grad = scatter_rows(product_right(own_pair_grad, head_ckv).astype(low_type))
    head_grad = head_grad.reshape(group * tok, width)
    qkv_grad, placed_grad = self_backward(
        places, owners, qkv, head_grad, head_mixed, self_total, tok
    )
    qkv_grad, placed_grad, square_terms, first_sums, second_sums, enc_grad = stage(
        (qkv_grad, placed_grad, square_terms, first_sums, second_sums, enc_grad)
    )
    input_part = scatter_rows(product_right(qkv_grad, head_qkv).astype(low_type))
    input_grad = first_grad + input_part.astype(jnp.float32)

    bias_cross_v = in_columns(column_sums(own_pair_grad[:, width:]))

    grad_fc2 = jnp.concatenate(rep_order(spread_over_rep(second_sums)), 0).astype(jnp.float32)
    first_sums = first_sums.reshape(2, weight_rows, line * unit)
    first_sums = jnp.stack(rep_order(spread_over_rep(first_sums)), 1)
    first_own = lax.dynamic_index_in_dim(first_sums, core, 0, keepdims=False)
    first_other = lax.dynamic_index_in_dim(first_sums, 1 - core, 0, keepdims=False)
    first_other = swap(first_other, "core", 1)
    grad_fc1 = jnp.where(
        core == 0, jnp.stack([first_own, first_other], 0), jnp.stack([first_other, first_own], 0)
    )
    grad_fc1 = grad_fc1.reshape(2, reps, weight_rows, line, unit).transpose(2, 3, 0, 1, 4)
    grad_fc1 = grad_fc1.reshape(weight_rows, feed).astype(jnp.float32)
    bias_parts = jnp.stack([part.reshape(line, unit) for part in rep_order(bias_parts)], 1)
    bias_fc1 = jnp.where(
        jnp.arange(2)[None, :, None, None] == core, bias_parts[:, None], 0.0
    ).reshape(feed)

    square = sum_of(square_terms).astype(low_type)
    square = scatter_over_line(square.transpose(1, 0, 2, 3))
    square = jnp.stack(rep_order(spread_over_rep(square.astype(low_type))), 1)
    grad_self_out, grad_cross_q, grad_cross_out = [
        square[i].reshape(weight_rows, model).astype(jnp.float32) for i in range(3)
    ]

    slice_grad = jnp.concatenate(
        [product_left(all_inputs, placed_grad), product_left(all_states, own_pair_grad)], 1
    ).astype(low_type)
    slice_grad = slice_grad.reshape(group, reps, weight_rows // reps, 5 * width)
    slice_grad = rep_order([slice_grad[:, r] for r in range(reps)])
    slice_grad = exchange(sum_of(trade_over_rep(slice_grad)).astype(low_type))
    slice_grad = jnp.stack(rep_order(spread_over_rep(slice_grad)), 0)
    slice_grad = slice_grad.reshape(reps, group, weight_rows // reps, 5, width)
    slice_grad = slice_grad.transpose(0, 2, 3, 1, 4).astype(jnp.float32)
    slice_grad = slice_grad.reshape(weight_rows, 5 * model)
    grad_self_qkv, grad_cross_kv = slice_grad[:, : 3 * model], slice_grad[:, 3 * model :]

    bias_self_q = in_columns(column_sums(qkv_grad[:, :width]))
    bias_self_v = in_columns(column_sums(qkv_grad[:, 2 * width :]))
    small = jnp.concatenate(
        [
            jnp.stack(
                [
                    bias_self_q,
                    bias_self_v,
                    bias_self_out,
                    bias_cross_q,
                    bias_cross_v,
                    bias_cross_out,
                    bias_fc2,
                    gain_one,
                    gain_two,
                    gain_three,
                    shift_one,
                    shift_two,
                    shift_three,
                ],
                0,
            ),
            bias_fc1.reshape(-1, model),
        ],
        0,
    )
    small = sum_over(small, bits_of("core") + bits_of("rep") + bits_of("line"))
    return (
        output,
        input_grad,
        enc_grad.astype(jnp.float32),
        grad_self_qkv,
        grad_self_out,
        grad_cross_q,
        grad_cross_kv,
        grad_cross_out,
        grad_fc1,
        grad_fc2,
        small[:7],
        small[13:].reshape(-1),
        small[7:10],
        small[10:13],
    )


def solution(mesh):
    reps, group = mesh.devices.shape
    split = jax.sharding.Mesh(
        mesh.devices.reshape(reps, group // 2, 2), ("rep",) + SHARD
    )
    rows, cut = P(("rep",) + SHARD, None), P(SHARD, None)
    return jax.shard_map(
        local,
        mesh=split,
        in_specs=(rows,) * 3 + (P("rep", None),) + (cut,) * 7 + (P(),) * 4,
        out_specs=(rows,) * 3 + (cut,) * 7 + (P(),) * 4,
        check_vma=False,
    )
```

```python
import functools

import jax
import jax.numpy as jnp
from jax import lax
from jax.experimental import pallas as pl
from jax.experimental.pallas import tpu as pltpu
from jax.sharding import PartitionSpec as P

HEADS = 16
HEAD_DIM = 64
LANES = 128

masked_score = -1000000000.0
norm_epsilon = 1e-05
low_type = jnp.bfloat16
SHARD = ("line", "core")


def norm_rows(values, gain_row, shift_row):
    row_mean = jnp.mean(values, -1, keepdims=True)
    centered = values - row_mean
    variance = jnp.mean(centered * centered, -1, keepdims=True)
    return centered * lax.rsqrt(variance + norm_epsilon) * gain_row + shift_row


def product(former, latter):
    return jnp.dot(former, latter, preferred_element_type=jnp.float32)


def product_left(former, latter):
    return lax.dot_general(
        former, latter, (((0,), (0,)), ((), ())), preferred_element_type=jnp.float32
    )


def product_right(former, latter):
    return lax.dot_general(
        former, latter, (((1,), (1,)), ((), ())), preferred_element_type=jnp.float32
    )


def column_sums(values):
    return jnp.sum(values.astype(jnp.float32), 0)


def head_columns(index):
    return slice(index * HEAD_DIM, (index + 1) * HEAD_DIM)


def causal_rows(keys, queries):
    key_index = lax.broadcasted_iota(jnp.int32, (keys, queries), 0)
    query_index = lax.broadcasted_iota(jnp.int32, (keys, queries), 1)
    return key_index <= query_index


def of_head(values, head):
    if values.shape[1] == HEAD_DIM:
        return values
    column = lax.broadcasted_iota(jnp.int32, values.shape, 1)
    inside = (column >= head * HEAD_DIM) & (column < (head + 1) * HEAD_DIM)
    return jnp.where(inside, values, jnp.zeros_like(values))


def turn_head(source, start, width, head, out, tok):
    for row in range(0, source.shape[0], tok):
        block = jnp.transpose(source[row : row + tok, start : start + width])
        out[:, row : row + tok] = block[head_columns(head)]


def over_keys(slot, half, tok, step, first, keep):
    @pl.when(slot < half)
    def _():
        keep(
            lax.fori_loop(0, slot, lambda j, c: step(pl.multiple_of(j * tok, tok), tok, c), first)
        )

    @pl.when(slot >= half)
    def _():
        keep(step(0, half * tok, first))


def self_forward_kernel(tok, width, half, head, count, owner, slot_of, *refs):
    if count:
        blocks, (weight, bias, scale, qkv, mixed, total, value_t) = refs[:count], refs[count:]
    else:
        qkv, mixed, total, value_t = refs
    slot = pl.program_id(0)

    @pl.when(slot == 0)
    def _():
        if count:
            for index, block in enumerate(blocks):
                rows = (product(block[...], weight[...]) + bias[...]) * scale[...]
                start = pl.multiple_of(slot_of[index] * tok, tok)
                qkv[pl.ds(start, tok), :] = rows.astype(low_type)
        turn_head(qkv, 2 * width, width, head, value_t, tok)

    base = pl.multiple_of(slot * tok, tok)
    query_t = jnp.transpose(of_head(qkv[pl.ds(base, tok), :width], head))

    def step(start, seen, carry, causal=False):
        top, weight, mix = carry
        keys = qkv[pl.ds(start, seen), width : 2 * width]
        scores = product(keys, query_t)
        if causal:
            scores = jnp.where(causal_rows(seen, tok), scores, masked_score)
        new_top = jnp.maximum(top, jnp.max(scores, 0, keepdims=True))
        scale = jnp.exp(top - new_top)
        power = jnp.exp(scores - new_top)
        weight = weight * scale + jnp.sum(power, 0, keepdims=True)
        mix = mix * scale + product(value_t[:, pl.ds(start, seen)], power.astype(low_type))
        return (new_top, weight, mix)

    first = (
        jnp.full((1, tok), -1e30, jnp.float32),
        jnp.zeros((1, tok), jnp.float32),
        jnp.zeros((HEAD_DIM, tok), jnp.float32),
    )

    def keep(carry):
        top, weight, mix = step(base, tok, carry, True)
        mixed[...] = (mix / weight).astype(low_type)
        total[...] = top + jnp.log(weight)

    over_keys(slot, half, tok, step, first, keep)


def self_backward_kernel(tok, width, half, head, scale, count, owner, place, *refs):
    blocks, refs = refs[:count], refs[count:]
    qkv, mixed_grad, mixed, total, out, slice_grad = refs[:6]
    key_t, key_sum, value_sum, rows, slice_sum, arrived = refs[6:]
    slot = pl.program_id(0)
    copies = [
        pltpu.make_async_copy(block, rows.at[i], arrived.at[i]) for i, block in enumerate(blocks)
    ]

    @pl.when(slot == 0)
    def _():
        for copy in copies:
            copy.start()
        turn_head(qkv, width, width, head, key_t, tok)
        key_sum[...] = jnp.zeros_like(key_sum)
        value_sum[...] = jnp.zeros_like(value_sum)

    base = pl.multiple_of(slot * tok, tok)
    query = of_head(qkv[pl.ds(base, tok), :width], head)
    query_t = jnp.transpose(query)
    narrow = mixed_grad[...]
    delta = jnp.sum(narrow.astype(jnp.float32) * mixed[...].astype(jnp.float32), 0, keepdims=True)
    empty = jnp.zeros_like(narrow)
    heads = width // HEAD_DIM
    grad_t = jnp.concatenate([narrow if h == head else empty for h in range(heads)], 0)
    grad = jnp.transpose(grad_t)

    def step(start, seen, carry, causal=False):
        keys = qkv[pl.ds(start, seen), width : 2 * width]
        values = qkv[pl.ds(start, seen), 2 * width :]
        power = jnp.exp(product(keys, query_t) - total[...])
        if causal:
            power = jnp.where(causal_rows(seen, tok), power, 0.0)
        slope = product(values, grad_t)
        score_grad = (power * (slope - delta)).astype(low_type)
        value_sum[pl.ds(start, seen), :] += product(power.astype(low_type), grad)
        key_sum[pl.ds(start, seen), :] += product(score_grad, query)
        return carry + product(key_t[:, pl.ds(start, seen)], score_grad)

    def keep(carry):
        query_grad = step(base, tok, carry, True).astype(low_type) * scale
        out[pl.ds(owner[slot], 1), :HEAD_DIM, :] = query_grad[None]

    over_keys(slot, half, tok, step, jnp.zeros((HEAD_DIM, tok), jnp.float32), keep)

    @pl.when(slot == pl.num_programs(0) - 1)
    def _():
        for copy in copies:
            copy.wait()
        slice_sum[...] = jnp.zeros_like(slice_sum)
        model = rows.shape[2]
        ones = jnp.ones((tok, LANES), low_type)

        def finish(p, carry):
            source = pl.ds(pl.multiple_of(p * tok, tok), tok)
            key_grad = jnp.transpose(key_sum[source, :])[head_columns(head)]
            value_grad = jnp.transpose(value_sum[source, :])[head_columns(head)]
            target = pl.ds(owner[p], 1)
            out[target, HEAD_DIM : 2 * HEAD_DIM, :] = key_grad.astype(low_type)[None]
            out[target, 2 * HEAD_DIM :, :] = value_grad.astype(low_type)[None]
            columns = out[target][0]
            slice_sum[:, :model] += product(columns, rows[pl.ds(place[p], 1)][0])
            slice_sum[:, model:] += product(columns, ones)
            return carry

        lax.fori_loop(0, pl.num_programs(0), finish, 0)
        slice_grad[...] = slice_sum[...]


def cross_forward_kernel(width, query, pair, mixed, total):
    keys, values = pair[0], jnp.transpose(pair[1])
    mixes = []
    for head in range(width // HEAD_DIM):
        cols = head_columns(head)
        scores = product_right(keys[:, cols], query[:, cols])
        top = jnp.max(scores, 0, keepdims=True)
        power = jnp.exp(scores - top)
        weight = jnp.sum(power, 0, keepdims=True)
        mixes.append(product(values[cols], power.astype(low_type)) / weight)
        total[head : head + 1, :] = top + jnp.log(weight)
    mixed[...] = jnp.transpose(jnp.concatenate(mixes, 0)).astype(low_type)


def cross_backward_kernel(width, scale, query, pair, mixed_grad, mixed, total, out, pair_grad):
    heads = width // HEAD_DIM
    keys, values = pair[0], pair[1]
    keys_t = jnp.transpose(keys)
    grad = mixed_grad[...]
    both = jnp.transpose(grad.astype(jnp.float32) * mixed[...].astype(jnp.float32))
    query_parts, key_parts, value_parts = [], [], []
    for head in range(heads):
        cols = head_columns(head)
        scores = product_right(keys[:, cols], query[:, cols])
        power = jnp.exp(scores - total[head : head + 1, :])
        slope = product_right(values[:, cols], grad[:, cols])
        delta = jnp.sum(both[cols], 0, keepdims=True)
        score_grad = (power * (slope - delta)).astype(low_type)
        value_parts.append(product(power.astype(low_type), grad[:, cols]))
        key_parts.append(product(score_grad, query[:, cols]))
        query_parts.append(product(keys_t[cols], score_grad))
    query_grad = jnp.transpose(jnp.concatenate(query_parts, 0)).astype(low_type)
    out[...] = query_grad * scale
    pair_grad[0] = jnp.concatenate(key_parts, 1).astype(low_type)
    pair_grad[1] = jnp.concatenate(value_parts, 1).astype(low_type)


declared = pl.CostEstimate(flops=2**20, transcendentals=0, bytes_accessed=2**16)


def kernel_options(megabytes):
    return pltpu.CompilerParams(
        dimension_semantics=("arbitrary",), vmem_limit_bytes=megabytes * 2**20
    )


def whole_block(shape):
    return pl.BlockSpec(shape, lambda *_: (0,) * len(shape), pipeline_mode=pl.Buffered(1))


def self_forward(head, owner, slot_of, tok, qkv, blocks=(), weight=None, bias=None, scale=None):
    make = qkv is None
    group = owner.shape[0]
    rows = group * tok
    width = (weight if make else qkv).shape[1] // 3
    inputs = (*blocks, weight, bias[None], scale[None]) if make else (qkv,)
    out_shape = [
        jax.ShapeDtypeStruct((group, HEAD_DIM, tok), low_type),
        jax.ShapeDtypeStruct((group, 1, tok), jnp.float32),
    ]
    out_specs = [
        pl.BlockSpec((None, HEAD_DIM, tok), lambda p, owner, _: (owner[p], 0, 0)),
        pl.BlockSpec((None, 1, tok), lambda p, *_: (p, 0, 0)),
    ]
    if make:
        out_shape = [jax.ShapeDtypeStruct((rows, 3 * width), low_type)] + out_shape
        out_specs = [pl.BlockSpec((rows, 3 * width), lambda *_: (0, 0))] + out_specs
    made = pl.pallas_call(
        functools.partial(
            self_forward_kernel, tok, width, group // 2, head, len(blocks)
        ),
        out_shape=out_shape,
        grid_spec=pltpu.PrefetchScalarGridSpec(
            num_scalar_prefetch=2,
            grid=(group,),
            in_specs=[whole_block(each.shape) for each in inputs],
            out_specs=out_specs,
            scratch_shapes=[pltpu.VMEM((HEAD_DIM, rows), low_type)],
        ),
        compiler_params=kernel_options(52),
        cost_estimate=declared,
        name="self_forward",
    )(owner, slot_of, *inputs)
    return made if make else [qkv, *made]


def self_backward(head, owner, place, blocks, qkv, mixed_grad, mixed, total):
    rows, width = qkv.shape[0], qkv.shape[1] // 3
    tok, model = blocks[0].shape
    group = rows // tok
    owned = pl.BlockSpec((None, HEAD_DIM, tok), lambda p, owner, _: (owner[p], 0, 0))
    return pl.pallas_call(
        functools.partial(
            self_backward_kernel, tok, width, group // 2, head, HEAD_DIM ** (-0.5), group
        ),
        out_shape=(
            jax.ShapeDtypeStruct((group, 3 * HEAD_DIM, tok), low_type),
            jax.ShapeDtypeStruct((3 * HEAD_DIM, model + LANES), jnp.float32),
        ),
        grid_spec=pltpu.PrefetchScalarGridSpec(
            num_scalar_prefetch=2,
            grid=(group,),
            in_specs=[pl.BlockSpec(memory_space=pl.ANY)] * group
            + [
                whole_block(qkv.shape),
                owned,
                owned,
                pl.BlockSpec((None, 1, tok), lambda p, *_: (p, 0, 0)),
            ],
            out_specs=[
                pl.BlockSpec((group, 3 * HEAD_DIM, tok), lambda *_: (0, 0, 0)),
                pl.BlockSpec((3 * HEAD_DIM, model + LANES), lambda *_: (0, 0)),
            ],
            scratch_shapes=[
                pltpu.VMEM((HEAD_DIM, rows), low_type),
                pltpu.VMEM((rows, width), jnp.float32),
                pltpu.VMEM((rows, width), jnp.float32),
                pltpu.VMEM((group, tok, model), low_type),
                pltpu.VMEM((3 * HEAD_DIM, model + LANES), jnp.float32),
                pltpu.SemaphoreType.DMA((group,)),
            ],
        ),
        compiler_params=kernel_options(52),
        cost_estimate=declared,
        name="self_backward",
    )(owner, place, *blocks, qkv, mixed_grad, mixed, total)


def split_columns(values, group):
    rows = values.shape[0]
    return values.reshape(rows, group, -1).transpose(1, 0, 2)


def join_columns(values):
    return values.transpose(1, 0, 2).reshape(values.shape[1], -1)


def by_head(values, group):
    rows, width = values.shape[0], values.shape[1] // group
    if width % LANES == 0:
        return values, pl.BlockSpec((rows, width), lambda g: (0, g))
    return split_columns(values, group), pl.BlockSpec((None, rows, width), lambda g: (g, 0, 0))


def of_heads(values, group):
    return values if values.ndim == 2 else join_columns(values)


def cross_forward(queries, pairs):
    group, _, states, width = pairs.shape
    rows = queries.shape[0]
    queries, query_spec = by_head(queries, group)
    mixed, total = pl.pallas_call(
        functools.partial(cross_forward_kernel, width),
        out_shape=(
            jax.ShapeDtypeStruct(queries.shape, low_type),
            jax.ShapeDtypeStruct((group, 8, rows), jnp.float32),
        ),
        grid=(group,),
        in_specs=[query_spec, pl.BlockSpec((None, 2, states, width), lambda g: (g, 0, 0, 0))],
        out_specs=[query_spec, pl.BlockSpec((None, 8, rows), lambda g: (g, 0, 0))],
        compiler_params=kernel_options(32),
        cost_estimate=declared,
        name="cross_forward",
    )(queries, pairs)
    return of_heads(mixed, group), total


def cross_backward(queries, pairs, mixed_grad, mixed, total):
    group, _, states, width = pairs.shape
    rows = queries.shape[0]
    queries, spec = by_head(queries, group)
    mixed_grad, mixed = by_head(mixed_grad, group)[0], by_head(mixed, group)[0]
    pair_spec = pl.BlockSpec((None, 2, states, width), lambda g: (g, 0, 0, 0))
    query_grad, pair_grad = pl.pallas_call(
        functools.partial(cross_backward_kernel, width, HEAD_DIM ** (-0.5)),
        out_shape=(
            jax.ShapeDtypeStruct(queries.shape, low_type),
            jax.ShapeDtypeStruct(pairs.shape, low_type),
        ),
        grid=(group,),
        in_specs=[spec, pair_spec, spec, spec, pl.BlockSpec((None, 8, rows), lambda g: (g, 0, 0))],
        out_specs=[spec, pair_spec],
        compiler_params=kernel_options(32),
        cost_estimate=declared,
        name="cross_backward",
    )(queries, pairs, mixed_grad, mixed, total)
    return of_heads(query_grad, group), pair_grad


def swap(values, axis, offset):
    size = lax.axis_size(axis)
    return lax.ppermute(values, axis, [(i, i ^ offset) for i in range(size)])


def sum_over(values, steps):
    for axis, offset in steps:
        values = (
            values.astype(jnp.float32) + swap(values, axis, offset).astype(jnp.float32)
        ).astype(values.dtype)
    return values


def bits_of(axis):
    return [(axis, 1 << i) for i in range(lax.axis_size(axis).bit_length() - 1)]


def spread_over_rep(values):
    return [values] + [swap(values, "rep", d) for d in range(1, lax.axis_size("rep"))]


def double(values, offset):
    return jnp.concatenate([values, swap(values, "rep", offset)], 0)


def rep_order(pieces):
    own = lax.axis_index("rep")
    count = len(pieces)
    return [lax.select_n(own, *[pieces[d ^ i] for i in range(count)]) for d in range(count)]


def trade_over_rep(pieces):
    return [pieces[0]] + [swap(pieces[d], "rep", d) for d in range(1, len(pieces))]


def sum_of(terms):
    return sum(term.astype(jnp.float32) for term in terms)


def trade_over_line(values):
    line, own = lax.axis_size("line"), lax.axis_index("line")
    terms = [lax.dynamic_index_in_dim(values, own, 0, keepdims=False)]
    for k in range(1, line):
        piece = lax.dynamic_index_in_dim(values, (own + k) % line, 0, keepdims=False)
        terms.append(lax.ppermute(piece, "line", [(i, (i + k) % line) for i in range(line)]))
    return terms


def two_rows(values):
    high = values.astype(low_type)
    return jnp.concatenate([high, (values - high.astype(jnp.float32)).astype(low_type)], -2)


def one_row(values):
    high, low = jnp.split(values.astype(jnp.float32), 2, -2)
    return high + low


def stage(values):
    return lax.optimization_barrier(values)


def shift(values):
    line = lax.axis_size("line")
    return lax.ppermute(values, "line", [(i, (i + 1) % line) for i in range(line)])


def gather_rows(values):
    return lax.all_gather(values, SHARD, axis=0, tiled=True)


def scatter_rows(values):
    return lax.psum_scatter(values, SHARD, scatter_dimension=0, tiled=True)


def exchange(values):
    return lax.all_to_all(values, SHARD, split_axis=0, concat_axis=0, tiled=True)


def gelu(values):
    return jax.nn.gelu(values, approximate=False)


def local(
    layer_input,
    encoder_states,
    out_grad,
    placement,
    w_self_qkv,
    w_self_out,
    w_cross_q,
    w_cross_kv,
    w_cross_out,
    w_fc1,
    w_fc2,
    proj_biases,
    fc1_bias,
    norm_gains,
    norm_shifts,
):
    reps, line = lax.axis_size("rep"), lax.axis_size("line")
    rep, core = lax.axis_index("rep"), lax.axis_index("core")
    group = 2 * line
    member = 2 * lax.axis_index("line") + core
    tok, model = layer_input.shape
    feed = w_fc1.shape[1]
    weight_rows = w_self_qkv.shape[0]
    width = model // group
    unit = feed // (group * reps)
    score_scale = HEAD_DIM ** (-0.5)
    slot_table = placement[0]
    device_ids = jnp.arange(group, dtype=jnp.int32)
    owners = jnp.sum(
        jnp.where(slot_table[None, :] == device_ids[:, None], device_ids[None, :], 0), 1
    )

    def own_columns(row):
        return lax.dynamic_slice(row, (member * width,), (width,))

    def in_columns(row):
        return lax.dynamic_update_slice(jnp.zeros((model,), jnp.float32), row, (member * width,))

    slices = jnp.concatenate(
        [
            w_self_qkv.reshape(reps, weight_rows // reps, 3, group, width),
            w_cross_kv.reshape(reps, weight_rows // reps, 2, group, width),
        ],
        2,
    )
    slices = lax.dynamic_index_in_dim(slices, rep, 0, keepdims=False)
    slices = slices.transpose(2, 0, 1, 3).reshape(group, weight_rows // reps, 5 * width)
    first_cut = w_fc1.reshape(weight_rows, line, 2, reps, unit)
    first_cut = lax.dynamic_index_in_dim(first_cut, rep, 3, keepdims=False)
    first_own = lax.dynamic_index_in_dim(first_cut, core, 2, keepdims=False)
    first_other = lax.dynamic_index_in_dim(first_cut, 1 - core, 2, keepdims=False)
    first_own = first_own.reshape(weight_rows, line * unit)
    first_other = swap(first_other.reshape(weight_rows, line * unit), "core", 1)
    first_cut = jnp.where(
        core == 0,
        jnp.concatenate([first_own, first_other], 0),
        jnp.concatenate([first_other, first_own], 0),
    )
    second_cut = lax.dynamic_slice_in_dim(w_fc2, rep * unit, unit, 0)
    bias_cut = lax.dynamic_index_in_dim(
        fc1_bias.reshape(line, 2, reps, unit), core, 1, keepdims=False
    )
    bias_cut = [bias_cut[:, r].reshape(line * unit) for r in range(reps)]
    bias_cut = rep_order(bias_cut)

    square = jnp.stack([w_self_out, w_cross_q, w_cross_out], 0)
    square = square.reshape(3, reps, weight_rows // reps, model)
    square = lax.dynamic_index_in_dim(square, rep, 1, keepdims=False)
    square = square.reshape(-1, model // (line * unit), line * unit).transpose(1, 0, 2)
    square = square.reshape(-1, line * unit)

    inputs = layer_input.astype(jnp.float32)
    zeros = jnp.zeros((width,), jnp.float32)
    head_bias = jnp.concatenate([own_columns(proj_biases[0]), zeros, own_columns(proj_biases[1])])
    head_scale = jnp.concatenate([jnp.full((width,), score_scale), jnp.ones((2 * width,))])
    cross_bias = jnp.concatenate([zeros, own_columns(proj_biases[4])])

    near = [1 << i for i in range(reps.bit_length() - 1)]
    far = [d for d in range(1, reps) if d not in near]
    slices = exchange(slices)
    blocks = [layer_input, swap(layer_input, "core", 1)]
    block = shift(layer_input)
    block, slices, blocks, first_cut, square, encoder_states, second_cut = stage(
        (block, slices, blocks, first_cut, square, encoder_states, second_cut)
    )

    both_cut = lax.all_gather(
        jnp.concatenate([first_cut, square], 0), "line", axis=0, tiled=True
    ).reshape(line, -1, line * unit)
    blocks += [block, swap(block, "core", 1)]
    block = shift(block)
    slices = spread_over_rep(slices)
    block, slices, blocks, encoder_states = stage((block, slices, blocks, encoder_states))

    for step in range(line - 3):
        blocks += [block, swap(block, "core", 1)]
        block = shift(block)
    slices = jnp.stack(rep_order(slices), 1).reshape(model, 5 * width)
    head_qkv, head_ckv = slices[:, : 3 * width], slices[:, 3 * width :]
    all_states = gather_rows(encoder_states)
    block, blocks, both_cut, head_qkv, head_ckv, all_states, second_cut = stage(
        (block, blocks, both_cut, head_qkv, head_ckv, all_states, second_cut)
    )

    blocks += [block, swap(block, "core", 1)]
    square = spread_over_rep(both_cut[:, 2 * weight_rows :])
    second_cut = lax.all_gather(second_cut, "line", axis=0, tiled=True)
    wfirst = {0: both_cut[:, : 2 * weight_rows].reshape(model, line * unit)}
    head_pair = (product(all_states, head_ckv) + cross_bias).astype(low_type)
    head_pair = split_columns(head_pair, 2)
    wsecond = {0: second_cut}
    back = (lax.axis_index("line") - owners // 2) % line
    places = 2 * back + ((owners % 2) ^ core)
    slot_of = jnp.sum(
        jnp.where(places[None, :] == device_ids[:, None], device_ids[None, :], 0), 1
    )
    heads = width // HEAD_DIM
    made, turn, self_totals, self_mixed, self_low = None, owners, [], [], []
    for head in range(heads):
        extra = () if head else (blocks, head_qkv, head_bias, head_scale)
        made, mixed, total = self_forward(head, turn, slot_of, tok, made, *extra)
        self_totals.append(total)
        if head == 0:
            mixed, turn, square, head_pair = stage((mixed, turn, square, head_pair))
            wfirst.update({d: swap(wfirst[0], "rep", d) for d in near})
            square = jnp.stack(rep_order(square), 1)
            square_other = swap(square, "core", 1)
        if head == heads - 1:
            held = (mixed, wfirst, square, square_other)
            held, wsecond, self_low = stage((held, wsecond, self_low))
            mixed, wfirst, square, square_other = held
            wfirst.update({d: swap(wfirst[0], "rep", d) for d in far})
            wsecond.update({d: swap(wsecond[0], "rep", d) for d in near})
        self_mixed.append(mixed)
        self_low.append(exchange(mixed))
    qkv = made
    square = jnp.where(
        core == 0, jnp.stack([square, square_other], 1), jnp.stack([square_other, square], 1)
    )
    square = square.reshape(line, 2, reps, -1, 3, weight_rows // reps, line * unit)
    full_out, full_cross_q, full_cross_out = [
        square[:, :, :, :, i].transpose(0, 1, 2, 4, 3, 5).reshape(model, model)
        for i in range(3)
    ]
    pairs = lax.all_gather(head_pair, SHARD, axis=0, tiled=False)
    self_low, pairs = stage((self_low, pairs))
    self_low = jnp.stack(self_low, 1).reshape(model, tok)

    first_sum = inputs + (product_left(self_low, full_out) + proj_biases[2])
    first_norm, norm1_back = jax.vjp(norm_rows, first_sum, norm_gains[0], norm_shifts[0])
    first_low = first_norm.astype(low_type)
    cross_queries = ((product(first_low, full_cross_q) + proj_biases[3]) * score_scale).astype(
        low_type
    )
    turned = jnp.transpose(stage((head_qkv, cross_queries))[0])
    turned = turned.reshape(3, heads, HEAD_DIM, model).transpose(1, 0, 2, 3)
    turned = gather_rows(turned.reshape(-1, model))
    turned = turned.reshape(group, heads, 3 * HEAD_DIM, model)

    cross_low, cross_total = cross_forward(cross_queries, pairs)
    cross_low, wfirst, wsecond = stage((cross_low, wfirst, wsecond))
    wsecond.update({d: swap(wsecond[0], "rep", d) for d in far})
    second_sum = first_norm + (product(cross_low, full_cross_out) + proj_biases[5])
    second_norm, norm2_back = jax.vjp(norm_rows, second_sum, norm_gains[1], norm_shifts[1])
    second_low = second_norm.astype(low_type)

    second_both = jnp.concatenate([second_low, swap(second_low, "core", 1)], 0)
    feed_sum, hidden, gelu_back = 0.0, [], []
    for part in range(reps):
        active, back = jax.vjp(gelu, product(second_both, wfirst[part]) + bias_cut[part])
        hidden.append(active.astype(low_type))
        gelu_back.append(back)
        feed_sum = feed_sum + product(hidden[part], wsecond[part])
    feed_sum, turned = stage((feed_sum, turned))
    feed_other = swap(feed_sum[tok:].astype(low_type), "core", 1).astype(jnp.float32)
    third_sum = second_norm + (feed_sum[:tok] + feed_other + proj_biases[6])
    result, norm3_back = jax.vjp(norm_rows, third_sum, norm_gains[2], norm_shifts[2])
    output = result.astype(low_type)

    third_grad, gain_three, shift_three = norm3_back(out_grad.astype(jnp.float32))
    feed_grad = third_grad.astype(low_type)
    bias_fc2 = column_sums(feed_grad)
    feed_both = jnp.concatenate([feed_grad, swap(feed_grad, "core", 1)], 0)
    second_parts = [
        product_left(hidden[part], feed_both).astype(low_type) for part in range(reps)
    ]
    feed_both, second_parts = stage((feed_both, second_parts))
    second_terms = {0: second_parts[0]}
    second_terms.update({d: swap(second_parts[d], "rep", d) for d in near})
    back_sum, first_parts, bias_parts = 0.0, [], []
    for part in range(reps):
        pre_grad = gelu_back[part](product_right(feed_both, wsecond[part]))[0].astype(low_type)
        first_parts.append(product_left(second_both, pre_grad).astype(low_type))
        bias_parts.append(column_sums(pre_grad))
        back_sum = back_sum + product_right(pre_grad, wfirst[part])
    back_sum, second_terms, first_parts = stage((back_sum, second_terms, first_parts))
    second_terms.update({d: swap(second_parts[d], "rep", d) for d in far})
    back_other = swap(back_sum[tok:].astype(low_type), "core", 1).astype(jnp.float32)
    second_grad, gain_two, shift_two = norm2_back(third_grad + (back_sum[:tok] + back_other))
    first_terms = {0: first_parts[0]}
    first_terms.update({d: swap(first_parts[d], "rep", d) for d in near})

    cross_out_grad = second_grad.astype(low_type)
    part_cross_out = product_left(cross_low, cross_out_grad).astype(low_type)
    bias_cross_out = column_sums(cross_out_grad)
    cross_mixed_grad = product_right(cross_out_grad, full_cross_out).astype(low_type)
    cross_q_grad, pair_grad = cross_backward(
        cross_queries, pairs, cross_mixed_grad, cross_low, cross_total
    )
    cross_q_grad, pair_grad, second_terms = stage((cross_q_grad, pair_grad, second_terms))
    second_sums = sum_of(second_terms.values()).astype(low_type)
    second_sums = lax.psum_scatter(second_sums, "line", scatter_dimension=0, tiled=True)
    own_pair_grad = lax.psum_scatter(pair_grad, SHARD, scatter_dimension=0, tiled=False)
    part_cross_q = product_left(first_low, cross_q_grad).astype(low_type)
    bias_cross_q = column_sums(cross_q_grad)
    first_grad, gain_one, shift_one = norm1_back(
        second_grad + product_right(cross_q_grad, full_cross_q)
    )
    self_out_grad = first_grad.astype(low_type)
    bias_self_out = column_sums(self_out_grad)
    mixed_grad = product_right(full_out, self_out_grad).astype(low_type)
    mixed_grad, first_terms = stage((mixed_grad, first_terms))
    mixed_grad = mixed_grad.reshape(group, heads, HEAD_DIM, tok)
    mixed_grad = [exchange(mixed_grad[:, head]) for head in range(heads)]
    part_self_out = product(self_low, self_out_grad).astype(low_type)

    square = jnp.stack([part_self_out, part_cross_q, part_cross_out], 0)
    square = square.reshape(3, line, 2, reps, weight_rows // reps, model)
    square_own = lax.dynamic_index_in_dim(square, core, 2, keepdims=False)
    square_other = swap(lax.dynamic_index_in_dim(square, 1 - core, 2, keepdims=False), "core", 1)

    bias_parts = jnp.stack([part.reshape(line, unit) for part in rep_order(bias_parts)], 1)
    bias_fc1 = jnp.where(
        jnp.arange(2)[None, :, None, None] == core, bias_parts[:, None], 0.0
    ).reshape(feed)
    small = jnp.concatenate(
        [
            jnp.stack(
                [
                    bias_self_out,
                    bias_cross_q,
                    bias_cross_out,
                    bias_fc2,
                    gain_one,
                    gain_two,
                    gain_three,
                    shift_one,
                    shift_two,
                    shift_three,
                ],
                0,
            ),
            bias_fc1.reshape(-1, model),
        ],
        0,
    )
    hops = bits_of("core") + bits_of("rep") + bits_of("line")

    def hop(values, count):
        for _ in range(count):
            values = values + swap(values, *hops.pop(0))
        return values

    small = hop(small, 1)
    square = square_own.astype(jnp.float32) + square_other.astype(jnp.float32)
    square = square.astype(low_type).transpose(2, 1, 0, 3, 4)
    square = rep_order([square[r] for r in range(reps)])
    mixed_grad[0], square, small, second_sums = stage(
        (mixed_grad[0], square, small, second_sums)
    )
    first_terms.update({d: swap(first_parts[d], "rep", d) for d in far})
    square_terms = trade_over_rep(square)
    wide = 2 * line * unit
    second_sums = second_sums.reshape(unit, model // wide, wide).transpose(1, 0, 2)
    second_sums = double(second_sums.reshape(1, -1, wide), near[0])
    turn = owners

    part_rows = weight_rows // reps

    def with_sums(values, sums):
        rows = two_rows(jnp.broadcast_to(sums, sums.shape[:-2] + (8,) + sums.shape[-1:]))
        return jnp.concatenate([values.astype(low_type), rows], -2)

    def split_sums(values):
        return values[..., :part_rows, :], one_row(values[..., part_rows:, :])[..., :1, :]

    def trade_slices(values):
        sums = jnp.broadcast_to(values[model : model + 1], (group, 1, values.shape[1]))
        values = values[:model].reshape(group, reps, part_rows, -1)
        values = [with_sums(values[:, r], sums) for r in range(reps)]
        return trade_over_rep(rep_order(values))

    def exchange_slices(terms):
        return exchange(with_sums(*split_sums(sum_of(terms))))

    def join_slices(values):
        values, sums = split_sums(values.astype(jnp.float32))
        values = jnp.stack(rep_order(spread_over_rep(values.astype(low_type))), 0)
        values = values.transpose(0, 2, 1, 3).reshape(weight_rows, group, -1)
        return values, sums[:, 0][None]

    parts, slice_parts = [], []
    for head in range(heads):
        part, slice_part = self_backward(
            head,
            turn,
            places,
            blocks,
            qkv,
            mixed_grad[head],
            self_mixed[head],
            self_totals[head],
        )
        if head == 0:
            held = (part, slice_part, turn, first_terms, second_sums, square_terms)
            held, mixed_grad, own_pair_grad = stage((held, mixed_grad, own_pair_grad))
            part, slice_part, turn, first_terms, second_sums, square_terms = held
            first_sums = sum_of(first_terms.values()).astype(low_type)
            first_sums = lax.psum_scatter(first_sums, "line", scatter_dimension=0, tiled=True)
            for offset in near[1:]:
                second_sums = double(second_sums, offset)
            small = hop(small, 1)
            own_pair_grad = join_columns(own_pair_grad)
            enc_grad = scatter_rows(product_right(own_pair_grad, head_ckv).astype(low_type))
            pair_sums = jnp.sum(own_pair_grad.astype(jnp.float32), 0)
            pair_sums = jnp.broadcast_to(pair_sums, (LANES, 2 * width))
            pair_slices = jnp.concatenate([product_left(all_states, own_pair_grad), pair_sums], 0)
            square_terms = trade_over_line(sum_of(square_terms).astype(low_type))
        if head == heads - 1:
            held = (part, slice_part, square_terms, first_sums, second_sums, small)
            held, parts, slice_parts = stage((held, parts, slice_parts))
            part, slice_part, square_terms, first_sums, second_sums, small = held
        parts.append(exchange(part))
        slice_parts.append(jnp.transpose(slice_part))

    slice_parts = trade_slices(
        jnp.concatenate([slice_parts[0], pair_slices] + slice_parts[1:], 1)
    )
    first_sums = first_sums.reshape(2, weight_rows, line * unit).transpose(1, 0, 2)
    first_sums = double(first_sums.reshape(1, -1, wide), near[0])
    square = double(sum_of(square_terms).astype(low_type)[None], near[0])
    parts, slice_parts, first_sums, square = stage((parts, slice_parts, first_sums, square))

    slice_parts = exchange_slices(slice_parts)
    for offset in near[1:]:
        square = double(square, offset)
        first_sums = double(first_sums, offset)
    small = hop(small, 1)
    second_sums = jnp.stack(rep_order([second_sums[d] for d in range(reps)]), 0)
    second_sums = second_sums.reshape(reps, model // wide, unit, wide)
    grad_fc2 = second_sums.transpose(0, 2, 1, 3).reshape(-1, model).astype(jnp.float32)
    input_grad = first_grad
    for head in range(heads):
        rows = turned[:, head].reshape(group * 3 * HEAD_DIM, model)
        input_grad = input_grad + product_left(parts[head].reshape(rows.shape[0], tok), rows)
    slice_parts, first_sums, square, input_grad, grad_fc2, small, enc_grad = stage(
        (slice_parts, first_sums, square, input_grad, grad_fc2, small, enc_grad)
    )

    first_sums = jnp.stack(rep_order([first_sums[d] for d in range(reps)]), 0)
    first_sums = first_sums.reshape(reps, weight_rows, 2, line, unit)
    first_own = lax.dynamic_index_in_dim(first_sums, core, 2, keepdims=False)
    first_other = lax.dynamic_index_in_dim(first_sums, 1 - core, 2, keepdims=False)
    first_other = swap(first_other.reshape(-1, line * unit), "core", 1)
    first_other = first_other.reshape(first_own.shape)

    slice_parts = join_slices(slice_parts)
    small = hop(small, len(hops))
    square = jnp.stack(rep_order([square[d] for d in range(reps)]), 1).astype(jnp.float32)
    grad_self_out, grad_cross_q, grad_cross_out = [
        square[i].reshape(weight_rows, model) for i in range(3)
    ]
    grad_fc1 = jnp.where(
        core == 0, jnp.stack([first_own, first_other], 0), jnp.stack([first_other, first_own], 0)
    )
    grad_fc1 = grad_fc1.transpose(2, 3, 0, 1, 4).reshape(weight_rows, feed).astype(jnp.float32)

    def of_self(values):
        found, start = [], 0
        for head in range(heads):
            found.append(values[..., start : start + 3 * HEAD_DIM])
            start += 3 * HEAD_DIM + (0 if head else 2 * width)
        found = [each.reshape(-1, group, 3, HEAD_DIM) for each in found]
        return jnp.stack(found, 3).transpose(0, 2, 1, 3, 4).reshape(-1, 3, model)

    def of_cross(values):
        values = values[..., 3 * HEAD_DIM : 3 * HEAD_DIM + 2 * width]
        return values.reshape(-1, group, 2, width).transpose(0, 2, 1, 3).reshape(-1, 2, model)

    grad_self_qkv = of_self(slice_parts[0].astype(jnp.float32)).reshape(weight_rows, 3 * model)
    grad_cross_kv = of_cross(slice_parts[0].astype(jnp.float32)).reshape(weight_rows, 2 * model)
    bias_self, bias_cross_v = of_self(slice_parts[1]), of_cross(slice_parts[1])[0, 1]
    grad_biases = jnp.stack(
        [
            bias_self[0, 0],
            bias_self[0, 2],
            small[0],
            small[1],
            bias_cross_v,
            small[2],
            small[3],
        ],
        0,
    )
    return (
        output,
        input_grad,
        enc_grad.astype(jnp.float32),
        grad_self_qkv,
        grad_self_out,
        grad_cross_q,
        grad_cross_kv,
        grad_cross_out,
        grad_fc1,
        grad_fc2,
        grad_biases,
        small[10:].reshape(-1),
        small[4:7],
        small[7:10],
    )


def solution(mesh):
    reps, group = mesh.devices.shape
    split = jax.sharding.Mesh(
        mesh.devices.reshape(reps, group // 2, 2), ("rep",) + SHARD
    )
    rows, cut = P(("rep",) + SHARD, None), P(SHARD, None)
    return jax.shard_map(
        local,
        mesh=split,
        in_specs=(rows,) * 3 + (P("rep", None),) + (cut,) * 7 + (P(),) * 4,
        out_specs=(rows,) * 3 + (cut,) * 7 + (P(),) * 4,
        check_vma=False,
    )
```

```python
import functools
import math

import jax
import jax.numpy as jnp
from jax import lax
from jax.experimental import pallas as pl
from jax.experimental.pallas import tpu as pltpu
from jax.sharding import PartitionSpec as P

HEADS = 16
HEAD_DIM = 64
LANES = 128

masked_score = -1000000000.0
norm_epsilon = 1e-05
low_type = jnp.bfloat16
SHARD = ("line", "core")


def norm_rows(values, gain_row, shift_row):
    row_mean = jnp.mean(values, -1, keepdims=True)
    centered = values - row_mean
    variance = jnp.mean(centered * centered, -1, keepdims=True)
    return centered * lax.rsqrt(variance + norm_epsilon) * gain_row + shift_row


def product(former, latter):
    return jnp.dot(former, latter, preferred_element_type=jnp.float32)


def product_left(former, latter):
    return lax.dot_general(
        former, latter, (((0,), (0,)), ((), ())), preferred_element_type=jnp.float32
    )


def product_right(former, latter):
    return lax.dot_general(
        former, latter, (((1,), (1,)), ((), ())), preferred_element_type=jnp.float32
    )


def column_sums(values):
    return jnp.sum(values.astype(jnp.float32), 0)


def head_columns(index):
    return slice(index * HEAD_DIM, (index + 1) * HEAD_DIM)


def causal_rows(keys, queries):
    key_index = lax.broadcasted_iota(jnp.int32, (keys, queries), 0)
    query_index = lax.broadcasted_iota(jnp.int32, (keys, queries), 1)
    return key_index <= query_index


def of_head(values, head):
    if values.shape[1] == HEAD_DIM:
        return values
    column = lax.broadcasted_iota(jnp.int32, values.shape, 1)
    inside = (column >= head * HEAD_DIM) & (column < (head + 1) * HEAD_DIM)
    return jnp.where(inside, values, jnp.zeros_like(values))


def turn_head(source, start, width, head, out, tok):
    for row in range(0, source.shape[0], tok):
        block = jnp.transpose(source[row : row + tok, start : start + width])
        out[:, row : row + tok] = block[head_columns(head)]


def over_keys(slot, half, tok, step, first, keep):
    @pl.when(slot < half)
    def _():
        keep(
            lax.fori_loop(0, slot, lambda j, c: step(pl.multiple_of(j * tok, tok), tok, c), first)
        )

    @pl.when(slot >= half)
    def _():
        keep(step(0, half * tok, first))


def self_forward_kernel(tok, width, half, head, count, owner, slot_of, *refs):
    if count:
        blocks, (weight, bias, scale, qkv, mixed, total, value_t) = refs[:count], refs[count:]
    else:
        qkv, mixed, total, value_t = refs
    slot = pl.program_id(0)

    @pl.when(slot == 0)
    def _():
        if count:
            for index, block in enumerate(blocks):
                rows = (product(block[...], weight[...]) + bias[...]) * scale[...]
                start = pl.multiple_of(slot_of[index] * tok, tok)
                qkv[pl.ds(start, tok), :] = rows.astype(low_type)
        turn_head(qkv, 2 * width, width, head, value_t, tok)

    base = pl.multiple_of(slot * tok, tok)
    query_t = jnp.transpose(of_head(qkv[pl.ds(base, tok), :width], head))

    def step(start, seen, carry, causal=False):
        top, weight, mix = carry
        keys = qkv[pl.ds(start, seen), width : 2 * width]
        scores = product(keys, query_t)
        if causal:
            scores = jnp.where(causal_rows(seen, tok), scores, masked_score)
        new_top = jnp.maximum(top, jnp.max(scores, 0, keepdims=True))
        scale = jnp.exp(top - new_top)
        power = jnp.exp(scores - new_top)
        weight = weight * scale + jnp.sum(power, 0, keepdims=True)
        mix = mix * scale + product(value_t[:, pl.ds(start, seen)], power.astype(low_type))
        return (new_top, weight, mix)

    first = (
        jnp.full((1, tok), -1e30, jnp.float32),
        jnp.zeros((1, tok), jnp.float32),
        jnp.zeros((HEAD_DIM, tok), jnp.float32),
    )

    def keep(carry):
        top, weight, mix = step(base, tok, carry, True)
        mixed[...] = (mix / weight).astype(low_type)
        total[...] = top + jnp.log(weight)

    over_keys(slot, half, tok, step, first, keep)


def self_backward_kernel(tok, width, half, head, scale, count, owner, place, *refs):
    blocks, refs = refs[:count], refs[count:]
    qkv, mixed_grad, mixed, total, out, slice_grad = refs[:6]
    key_t, key_sum, value_sum, rows, slice_sum, arrived = refs[6:]
    slot = pl.program_id(0)
    copies = [
        pltpu.make_async_copy(block, rows.at[i], arrived.at[i]) for i, block in enumerate(blocks)
    ]

    @pl.when(slot == 0)
    def _():
        for copy in copies:
            copy.start()
        turn_head(qkv, width, width, head, key_t, tok)
        key_sum[...] = jnp.zeros_like(key_sum)
        value_sum[...] = jnp.zeros_like(value_sum)

    base = pl.multiple_of(slot * tok, tok)
    query = of_head(qkv[pl.ds(base, tok), :width], head)
    query_t = jnp.transpose(query)
    narrow = mixed_grad[...]
    delta = jnp.sum(narrow.astype(jnp.float32) * mixed[...].astype(jnp.float32), 0, keepdims=True)
    empty = jnp.zeros_like(narrow)
    heads = width // HEAD_DIM
    grad_t = jnp.concatenate([narrow if h == head else empty for h in range(heads)], 0)
    grad = jnp.transpose(grad_t)

    def step(start, seen, carry, causal=False):
        keys = qkv[pl.ds(start, seen), width : 2 * width]
        values = qkv[pl.ds(start, seen), 2 * width :]
        power = jnp.exp(product(keys, query_t) - total[...])
        if causal:
            power = jnp.where(causal_rows(seen, tok), power, 0.0)
        slope = product(values, grad_t)
        score_grad = (power * (slope - delta)).astype(low_type)
        value_sum[pl.ds(start, seen), :] += product(power.astype(low_type), grad)
        key_sum[pl.ds(start, seen), :] += product(score_grad, query)
        return carry + product(key_t[:, pl.ds(start, seen)], score_grad)

    def keep(carry):
        query_grad = step(base, tok, carry, True).astype(low_type) * scale
        out[pl.ds(owner[slot], 1), :HEAD_DIM, :] = query_grad[None]

    over_keys(slot, half, tok, step, jnp.zeros((HEAD_DIM, tok), jnp.float32), keep)

    @pl.when(slot == pl.num_programs(0) - 1)
    def _():
        for copy in copies:
            copy.wait()
        slice_sum[...] = jnp.zeros_like(slice_sum)
        model = rows.shape[2]
        ones = jnp.ones((tok, LANES), low_type)

        def finish(p, carry):
            source = pl.ds(pl.multiple_of(p * tok, tok), tok)
            key_grad = jnp.transpose(key_sum[source, :])[head_columns(head)]
            value_grad = jnp.transpose(value_sum[source, :])[head_columns(head)]
            target = pl.ds(owner[p], 1)
            out[target, HEAD_DIM : 2 * HEAD_DIM, :] = key_grad.astype(low_type)[None]
            out[target, 2 * HEAD_DIM :, :] = value_grad.astype(low_type)[None]
            columns = out[target][0]
            slice_sum[:, :model] += product(columns, rows[pl.ds(place[p], 1)][0])
            slice_sum[:, model:] += product(columns, ones)
            return carry

        lax.fori_loop(0, pl.num_programs(0), finish, 0)
        slice_grad[...] = jnp.transpose(slice_sum[...])


def cross_forward_kernel(width, query, pair, mixed, total):
    keys, values = pair[0], jnp.transpose(pair[1])
    mixes = []
    for head in range(width // HEAD_DIM):
        cols = head_columns(head)
        scores = product_right(keys[:, cols], query[:, cols])
        top = jnp.max(scores, 0, keepdims=True)
        power = jnp.exp(scores - top)
        weight = jnp.sum(power, 0, keepdims=True)
        mixes.append(product(values[cols], power.astype(low_type)) / weight)
        total[head : head + 1, :] = top + jnp.log(weight)
    mixed[...] = jnp.transpose(jnp.concatenate(mixes, 0)).astype(low_type)


def cross_backward_kernel(width, scale, query, pair, mixed_grad, mixed, total, out, pair_grad):
    heads = width // HEAD_DIM
    keys, values = pair[0], pair[1]
    keys_t = jnp.transpose(keys)
    grad = mixed_grad[...]
    both = jnp.transpose(grad.astype(jnp.float32) * mixed[...].astype(jnp.float32))
    query_parts, key_parts, value_parts = [], [], []
    for head in range(heads):
        cols = head_columns(head)
        scores = product_right(keys[:, cols], query[:, cols])
        power = jnp.exp(scores - total[head : head + 1, :])
        slope = product_right(values[:, cols], grad[:, cols])
        delta = jnp.sum(both[cols], 0, keepdims=True)
        score_grad = (power * (slope - delta)).astype(low_type)
        value_parts.append(product(power.astype(low_type), grad[:, cols]))
        key_parts.append(product(score_grad, query[:, cols]))
        query_parts.append(product(keys_t[cols], score_grad))
    query_grad = jnp.transpose(jnp.concatenate(query_parts, 0)).astype(low_type)
    out[...] = query_grad * scale
    pair_grad[0] = jnp.concatenate(key_parts, 1).astype(low_type)
    pair_grad[1] = jnp.concatenate(value_parts, 1).astype(low_type)


declared = pl.CostEstimate(flops=2**20, transcendentals=0, bytes_accessed=2**16)


def kernel_options(megabytes):
    return pltpu.CompilerParams(
        dimension_semantics=("arbitrary",), vmem_limit_bytes=megabytes * 2**20
    )


def whole_block(shape):
    return pl.BlockSpec(shape, lambda *_: (0,) * len(shape), pipeline_mode=pl.Buffered(1))


def self_forward(head, owner, slot_of, tok, qkv, blocks=(), weight=None, bias=None, scale=None):
    make = qkv is None
    group = owner.shape[0]
    rows = group * tok
    width = (weight if make else qkv).shape[1] // 3
    inputs = (*blocks, weight, bias[None], scale[None]) if make else (qkv,)
    out_shape = [
        jax.ShapeDtypeStruct((group, HEAD_DIM, tok), low_type),
        jax.ShapeDtypeStruct((group, 1, tok), jnp.float32),
    ]
    out_specs = [
        pl.BlockSpec((None, HEAD_DIM, tok), lambda p, owner, _: (owner[p], 0, 0)),
        pl.BlockSpec((None, 1, tok), lambda p, *_: (p, 0, 0)),
    ]
    if make:
        out_shape = [jax.ShapeDtypeStruct((rows, 3 * width), low_type)] + out_shape
        out_specs = [pl.BlockSpec((rows, 3 * width), lambda *_: (0, 0))] + out_specs
    made = pl.pallas_call(
        functools.partial(
            self_forward_kernel, tok, width, group // 2, head, len(blocks)
        ),
        out_shape=out_shape,
        grid_spec=pltpu.PrefetchScalarGridSpec(
            num_scalar_prefetch=2,
            grid=(group,),
            in_specs=[whole_block(each.shape) for each in inputs],
            out_specs=out_specs,
            scratch_shapes=[pltpu.VMEM((HEAD_DIM, rows), low_type)],
        ),
        compiler_params=kernel_options(52),
        cost_estimate=declared,
        name="self_forward",
    )(owner, slot_of, *inputs)
    return made if make else [qkv, *made]


def self_backward(head, owner, place, blocks, qkv, mixed_grad, mixed, total):
    rows, width = qkv.shape[0], qkv.shape[1] // 3
    tok, model = blocks[0].shape
    group = rows // tok
    owned = pl.BlockSpec((None, HEAD_DIM, tok), lambda p, owner, _: (owner[p], 0, 0))
    return pl.pallas_call(
        functools.partial(
            self_backward_kernel, tok, width, group // 2, head, HEAD_DIM ** (-0.5), group
        ),
        out_shape=(
            jax.ShapeDtypeStruct((group, 3 * HEAD_DIM, tok), low_type),
            jax.ShapeDtypeStruct((model + LANES, 3 * HEAD_DIM), jnp.float32),
        ),
        grid_spec=pltpu.PrefetchScalarGridSpec(
            num_scalar_prefetch=2,
            grid=(group,),
            in_specs=[pl.BlockSpec(memory_space=pl.ANY)] * group
            + [
                whole_block(qkv.shape),
                owned,
                owned,
                pl.BlockSpec((None, 1, tok), lambda p, *_: (p, 0, 0)),
            ],
            out_specs=[
                pl.BlockSpec((group, 3 * HEAD_DIM, tok), lambda *_: (0, 0, 0)),
                pl.BlockSpec((model + LANES, 3 * HEAD_DIM), lambda *_: (0, 0)),
            ],
            scratch_shapes=[
                pltpu.VMEM((HEAD_DIM, rows), low_type),
                pltpu.VMEM((rows, width), jnp.float32),
                pltpu.VMEM((rows, width), jnp.float32),
                pltpu.VMEM((group, tok, model), low_type),
                pltpu.VMEM((3 * HEAD_DIM, model + LANES), jnp.float32),
                pltpu.SemaphoreType.DMA((group,)),
            ],
        ),
        compiler_params=kernel_options(52),
        cost_estimate=declared,
        name="self_backward",
    )(owner, place, *blocks, qkv, mixed_grad, mixed, total)


def split_columns(values, group):
    rows = values.shape[0]
    return values.reshape(rows, group, -1).transpose(1, 0, 2)


def join_columns(values):
    return values.transpose(1, 0, 2).reshape(values.shape[1], -1)


def by_head(values, group):
    rows, width = values.shape[0], values.shape[1] // group
    if width % LANES == 0:
        return values, pl.BlockSpec((rows, width), lambda g: (0, g))
    return split_columns(values, group), pl.BlockSpec((None, rows, width), lambda g: (g, 0, 0))


def of_heads(values, group):
    return values if values.ndim == 2 else join_columns(values)


def cross_forward(queries, pairs):
    group, _, states, width = pairs.shape
    rows = queries.shape[0]
    queries, query_spec = by_head(queries, group)
    mixed, total = pl.pallas_call(
        functools.partial(cross_forward_kernel, width),
        out_shape=(
            jax.ShapeDtypeStruct(queries.shape, low_type),
            jax.ShapeDtypeStruct((group, 8, rows), jnp.float32),
        ),
        grid=(group,),
        in_specs=[query_spec, pl.BlockSpec((None, 2, states, width), lambda g: (g, 0, 0, 0))],
        out_specs=[query_spec, pl.BlockSpec((None, 8, rows), lambda g: (g, 0, 0))],
        compiler_params=kernel_options(32),
        cost_estimate=declared,
        name="cross_forward",
    )(queries, pairs)
    return of_heads(mixed, group), total


def cross_backward(queries, pairs, mixed_grad, mixed, total):
    group, _, states, width = pairs.shape
    rows = queries.shape[0]
    queries, spec = by_head(queries, group)
    mixed_grad, mixed = by_head(mixed_grad, group)[0], by_head(mixed, group)[0]
    pair_spec = pl.BlockSpec((None, 2, states, width), lambda g: (g, 0, 0, 0))
    query_grad, pair_grad = pl.pallas_call(
        functools.partial(cross_backward_kernel, width, HEAD_DIM ** (-0.5)),
        out_shape=(
            jax.ShapeDtypeStruct(queries.shape, low_type),
            jax.ShapeDtypeStruct(pairs.shape, low_type),
        ),
        grid=(group,),
        in_specs=[spec, pair_spec, spec, spec, pl.BlockSpec((None, 8, rows), lambda g: (g, 0, 0))],
        out_specs=[spec, pair_spec],
        compiler_params=kernel_options(32),
        cost_estimate=declared,
        name="cross_backward",
    )(queries, pairs, mixed_grad, mixed, total)
    return of_heads(query_grad, group), pair_grad


def swap(values, axis, offset):
    size = lax.axis_size(axis)
    return lax.ppermute(values, axis, [(i, i ^ offset) for i in range(size)])


def sum_over(values, steps):
    for axis, offset in steps:
        values = (
            values.astype(jnp.float32) + swap(values, axis, offset).astype(jnp.float32)
        ).astype(values.dtype)
    return values


def bits_of(axis):
    return [(axis, 1 << i) for i in range(lax.axis_size(axis).bit_length() - 1)]


def spread_over_rep(values):
    return [values] + [swap(values, "rep", d) for d in range(1, lax.axis_size("rep"))]


def double(values, offset):
    return jnp.concatenate([values, swap(values, "rep", offset)], 0)


def parts_of(values, axis):
    own = lax.axis_index("rep")
    return [
        lax.dynamic_index_in_dim(values, own ^ d, axis, keepdims=False)
        for d in range(values.shape[axis])
    ]


def rep_order(pieces):
    own = lax.axis_index("rep")
    count = len(pieces)
    return [lax.select_n(own, *[pieces[d ^ i] for i in range(count)]) for d in range(count)]


def trade_over_rep(pieces):
    return [pieces[0]] + [swap(pieces[d], "rep", d) for d in range(1, len(pieces))]


def far_terms(pieces):
    if len(pieces) != 4:
        return [swap(pieces[d], "rep", d) for d in range(len(pieces)) if d & (d - 1)]
    half = pieces[3].shape[0] // 2
    return [swap(pieces[3][:half], "rep", 1), swap(pieces[3][half:], "rep", 2)]


def near_terms(pieces, found):
    near = [1 << i for i in range(len(pieces).bit_length() - 1)]
    if len(pieces) != 4:
        return [swap(pieces[d], "rep", d) for d in near]
    half = pieces[3].shape[0] // 2
    one, two = pieces[1], pieces[2]
    one = jnp.concatenate([one[:half], sum_of([one[half:], found[1]]).astype(low_type)], 0)
    two = jnp.concatenate([sum_of([two[:half], found[0]]).astype(low_type), two[half:]], 0)
    return [swap(one, "rep", 1), swap(two, "rep", 2)]


def all_terms(pieces, found, near):
    return [pieces[0]] + near + (found if len(pieces) != 4 else [])


def sum_of(terms):
    return sum(term.astype(jnp.float32) for term in terms)


def trade_over_line(values):
    line, own = lax.axis_size("line"), lax.axis_index("line")
    terms = [lax.dynamic_index_in_dim(values, own, 0, keepdims=False)]
    for k in range(1, line):
        piece = lax.dynamic_index_in_dim(values, (own + k) % line, 0, keepdims=False)
        terms.append(lax.ppermute(piece, "line", [(i, (i + k) % line) for i in range(line)]))
    return terms


def two_rows(values):
    high = values.astype(low_type)
    return jnp.concatenate([high, (values - high.astype(jnp.float32)).astype(low_type)], -2)


def one_row(values):
    high, low = jnp.split(values.astype(jnp.float32), 2, -2)
    return high + low


def stage(values):
    return lax.optimization_barrier(values)


def shift(values):
    line = lax.axis_size("line")
    return lax.ppermute(values, "line", [(i, (i + 1) % line) for i in range(line)])


def gather_rows(values):
    return lax.all_gather(values, SHARD, axis=0, tiled=True)


def scatter_rows(values):
    return lax.psum_scatter(values, SHARD, scatter_dimension=0, tiled=True)


def exchange(values):
    return lax.all_to_all(values, SHARD, split_axis=0, concat_axis=0, tiled=True)


def gelu_and_slope(values):
    reduced = jnp.abs(values) * (0.5**0.5)
    inverse = 1.0 / (1.0 + 0.3275911 * reduced)
    bell = jnp.exp(-(reduced * reduced))
    tail = 1.061405429 * inverse - 1.453152027
    tail = tail * inverse + 1.421413741
    tail = tail * inverse - 0.284496736
    tail = (tail * inverse + 0.254829592) * inverse * bell * 0.5
    normal = jnp.where(values >= 0.0, 1.0 - tail, tail)
    return values * normal, normal + values * (bell * (0.5 / math.pi) ** 0.5)


def local(
    layer_input,
    encoder_states,
    out_grad,
    placement,
    w_self_qkv,
    w_self_out,
    w_cross_q,
    w_cross_kv,
    w_cross_out,
    w_fc1,
    w_fc2,
    proj_biases,
    fc1_bias,
    norm_gains,
    norm_shifts,
):
    reps, line = lax.axis_size("rep"), lax.axis_size("line")
    rep, core = lax.axis_index("rep"), lax.axis_index("core")
    group = 2 * line
    member = 2 * lax.axis_index("line") + core
    tok, model = layer_input.shape
    feed = w_fc1.shape[1]
    weight_rows = w_self_qkv.shape[0]
    width = model // group
    unit = feed // (group * reps)
    score_scale = HEAD_DIM ** (-0.5)
    slot_table = placement[0]
    device_ids = jnp.arange(group, dtype=jnp.int32)
    owners = jnp.sum(
        jnp.where(slot_table[None, :] == device_ids[:, None], device_ids[None, :], 0), 1
    )

    def own_columns(row):
        return lax.dynamic_slice(row, (member * width,), (width,))

    def in_columns(row):
        return lax.dynamic_update_slice(jnp.zeros((model,), jnp.float32), row, (member * width,))

    slices = jnp.concatenate(
        [
            w_self_qkv.reshape(reps, weight_rows // reps, 3, group, width),
            w_cross_kv.reshape(reps, weight_rows // reps, 2, group, width),
        ],
        2,
    )
    slices = lax.dynamic_index_in_dim(slices, rep, 0, keepdims=False)
    slices = slices.transpose(2, 0, 1, 3).reshape(group, weight_rows // reps, 5 * width)
    first_cut = w_fc1.reshape(weight_rows, line, 2, reps, unit)
    first_cut = lax.dynamic_index_in_dim(first_cut, rep, 3, keepdims=False)
    first_own = lax.dynamic_index_in_dim(first_cut, core, 2, keepdims=False)
    first_other = lax.dynamic_index_in_dim(first_cut, 1 - core, 2, keepdims=False)
    first_own = first_own.reshape(weight_rows, line * unit)
    first_other = swap(first_other.reshape(weight_rows, line * unit), "core", 1)
    first_cut = jnp.where(
        core == 0,
        jnp.concatenate([first_own, first_other], 0),
        jnp.concatenate([first_other, first_own], 0),
    )
    second_cut = lax.dynamic_slice_in_dim(w_fc2, rep * unit, unit, 0)
    bias_cut = lax.dynamic_index_in_dim(
        fc1_bias.reshape(line, 2, reps, unit), core, 1, keepdims=False
    )
    bias_cut = [bias_cut[:, r].reshape(line * unit) for r in range(reps)]
    bias_cut = rep_order(bias_cut)

    square = jnp.stack([w_self_out, w_cross_q, w_cross_out], 0)
    square = square.reshape(3, reps, weight_rows // reps, model)
    square = lax.dynamic_index_in_dim(square, rep, 1, keepdims=False)
    square = square.reshape(-1, model // (line * unit), line * unit).transpose(1, 0, 2)
    square = square.reshape(-1, line * unit)

    inputs = layer_input.astype(jnp.float32)
    zeros = jnp.zeros((width,), jnp.float32)
    head_bias = jnp.concatenate([own_columns(proj_biases[0]), zeros, own_columns(proj_biases[1])])
    head_scale = jnp.concatenate([jnp.full((width,), score_scale), jnp.ones((2 * width,))])
    cross_bias = jnp.concatenate([zeros, own_columns(proj_biases[4])])

    near = [1 << i for i in range(reps.bit_length() - 1)]
    far = [d for d in range(1, reps) if d not in near]
    slices = exchange(slices)
    blocks = [layer_input, swap(layer_input, "core", 1)]
    block = shift(layer_input)
    block, slices, blocks, first_cut, square, encoder_states, second_cut = stage(
        (block, slices, blocks, first_cut, square, encoder_states, second_cut)
    )

    both_cut = lax.all_gather(
        jnp.concatenate([first_cut, square], 0), "line", axis=0, tiled=True
    ).reshape(line, -1, line * unit)
    blocks += [block, swap(block, "core", 1)]
    block = shift(block)
    slices = spread_over_rep(slices)
    block, slices, blocks, encoder_states = stage((block, slices, blocks, encoder_states))

    for step in range(line - 3):
        blocks += [block, swap(block, "core", 1)]
        block = shift(block)
    slices = jnp.stack(rep_order(slices), 1).reshape(model, 5 * width)
    head_qkv, head_ckv = slices[:, : 3 * width], slices[:, 3 * width :]
    all_states = gather_rows(encoder_states)
    block, blocks, both_cut, head_qkv, head_ckv, all_states, second_cut = stage(
        (block, blocks, both_cut, head_qkv, head_ckv, all_states, second_cut)
    )

    blocks += [block, swap(block, "core", 1)]
    square = spread_over_rep(both_cut[:, 2 * weight_rows :])
    second_cut = lax.all_gather(second_cut, "line", axis=0, tiled=True)
    wfirst = {0: both_cut[:, : 2 * weight_rows].reshape(model, line * unit)}
    head_pair = (product(all_states, head_ckv) + cross_bias).astype(low_type)
    head_pair = split_columns(head_pair, 2)
    wsecond = {0: second_cut}
    back = (lax.axis_index("line") - owners // 2) % line
    places = 2 * back + ((owners % 2) ^ core)
    slot_of = jnp.sum(
        jnp.where(places[None, :] == device_ids[:, None], device_ids[None, :], 0), 1
    )
    heads = width // HEAD_DIM
    made, turn, self_totals, self_mixed, self_low = None, owners, [], [], []
    for head in range(heads):
        extra = () if head else (blocks, head_qkv, head_bias, head_scale)
        made, mixed, total = self_forward(head, turn, slot_of, tok, made, *extra)
        self_totals.append(total)
        if head == 0:
            mixed, turn, square, head_pair = stage((mixed, turn, square, head_pair))
            wfirst.update({d: swap(wfirst[0], "rep", d) for d in near})
            square = jnp.stack(rep_order(square), 1)
            square_other = swap(square, "core", 1)
        if head == heads - 1:
            held = (mixed, wfirst, square, square_other)
            held, wsecond, self_low = stage((held, wsecond, self_low))
            mixed, wfirst, square, square_other = held
            wfirst.update({d: swap(wfirst[0], "rep", d) for d in far})
            wsecond.update({d: swap(wsecond[0], "rep", d) for d in near})
        self_mixed.append(mixed)
        self_low.append(exchange(mixed))
    qkv = made
    square = jnp.where(
        core == 0, jnp.stack([square, square_other], 1), jnp.stack([square_other, square], 1)
    )
    square = square.reshape(line, 2, reps, -1, 3, weight_rows // reps, line * unit)
    full_out, full_cross_q, full_cross_out = [
        square[:, :, :, :, i].transpose(0, 1, 2, 4, 3, 5).reshape(model, model)
        for i in range(3)
    ]
    pairs = lax.all_gather(head_pair, SHARD, axis=0, tiled=False)
    self_low, pairs = stage((self_low, pairs))
    self_low = jnp.stack(self_low, 1).reshape(model, tok)

    first_sum = inputs + (product_left(self_low, full_out) + proj_biases[2])
    first_norm, norm1_back = jax.vjp(norm_rows, first_sum, norm_gains[0], norm_shifts[0])
    first_low = first_norm.astype(low_type)
    cross_queries = ((product(first_low, full_cross_q) + proj_biases[3]) * score_scale).astype(
        low_type
    )
    cross_low, cross_total = cross_forward(cross_queries, pairs)
    cross_low, wfirst, wsecond = stage((cross_low, wfirst, wsecond))
    wsecond.update({d: swap(wsecond[0], "rep", d) for d in far})
    second_sum = first_norm + (product(cross_low, full_cross_out) + proj_biases[5])
    second_norm, norm2_back = jax.vjp(norm_rows, second_sum, norm_gains[1], norm_shifts[1])
    second_low = second_norm.astype(low_type)

    turned = jnp.transpose(stage((head_qkv, second_low))[0])
    turned = turned.reshape(3, heads, HEAD_DIM, model).transpose(1, 0, 2, 3)
    turned = gather_rows(turned.reshape(-1, model))
    turned = turned.reshape(group, heads, 3 * HEAD_DIM, model)

    second_both = jnp.concatenate([second_low, swap(second_low, "core", 1)], 0)
    feed_sum, hidden, slopes = 0.0, [], []
    for part in range(reps):
        active, slope = gelu_and_slope(product(second_both, wfirst[part]) + bias_cut[part])
        hidden.append(active.astype(low_type))
        slopes.append(slope)
        feed_sum = feed_sum + product(hidden[part], wsecond[part])
    feed_other = swap(feed_sum[tok:].astype(low_type), "core", 1).astype(jnp.float32)
    third_sum = second_norm + (feed_sum[:tok] + feed_other + proj_biases[6])
    result, norm3_back = jax.vjp(norm_rows, third_sum, norm_gains[2], norm_shifts[2])
    output = result.astype(low_type)

    third_grad, gain_three, shift_three = norm3_back(out_grad.astype(jnp.float32))
    feed_grad = third_grad.astype(low_type)
    bias_fc2 = column_sums(feed_grad)
    feed_both = jnp.concatenate([feed_grad, swap(feed_grad, "core", 1)], 0)
    second_parts = [
        product_left(hidden[part], feed_both).astype(low_type) for part in range(reps)
    ]
    feed_both, second_parts = stage((feed_both, second_parts))
    second_found = far_terms(second_parts)
    back_sum, first_parts, bias_parts = 0.0, [], []
    for part in range(reps):
        pre_grad = (product_right(feed_both, wsecond[part]) * slopes[part]).astype(low_type)
        first_parts.append(product_left(second_both, pre_grad).astype(low_type))
        bias_parts.append(column_sums(pre_grad))
        back_sum = back_sum + product_right(pre_grad, wfirst[part])
        if part == reps // 2 - 1:
            feed_both, back_sum, second_found = stage((feed_both, back_sum, second_found))
            second_near = near_terms(second_parts, second_found)
    back_sum, second_near, first_parts = stage((back_sum, second_near, first_parts))
    second_sums = sum_of(all_terms(second_parts, second_found, second_near)).astype(low_type)
    back_other = swap(back_sum[tok:].astype(low_type), "core", 1).astype(jnp.float32)
    second_grad, gain_two, shift_two = norm2_back(third_grad + (back_sum[:tok] + back_other))
    second_grad, second_sums, first_parts = stage((second_grad, second_sums, first_parts))
    second_sums = lax.psum_scatter(second_sums, "line", scatter_dimension=0, tiled=True)
    first_found = far_terms(first_parts)

    cross_out_grad = second_grad.astype(low_type)
    cross_mixed_grad = product_right(cross_out_grad, full_cross_out).astype(low_type)
    cross_q_grad, pair_grad = cross_backward(
        cross_queries, pairs, cross_mixed_grad, cross_low, cross_total
    )
    cross_q_grad, pair_grad, first_found, turned = stage(
        (cross_q_grad, pair_grad, first_found, turned)
    )
    first_near = near_terms(first_parts, first_found)
    own_pair_grad = lax.psum_scatter(pair_grad, SHARD, scatter_dimension=0, tiled=False)
    first_grad, gain_one, shift_one = norm1_back(
        second_grad + product_right(cross_q_grad, full_cross_q)
    )
    self_out_grad = first_grad.astype(low_type)
    mixed_grad = product_right(full_out, self_out_grad).astype(low_type)
    mixed_grad = mixed_grad.reshape(group, heads, HEAD_DIM, tok)
    held = (self_low, first_low, cross_low, self_out_grad, cross_q_grad, cross_out_grad)
    mixed_grad, held = stage((mixed_grad, held))
    self_low, first_low, cross_low, self_out_grad, cross_q_grad, cross_out_grad = held
    mixed_grad = [exchange(mixed_grad[:, head]) for head in range(heads)]
    part_self_out = product(self_low, self_out_grad).astype(low_type)
    part_cross_q = product_left(first_low, cross_q_grad).astype(low_type)
    part_cross_out = product_left(cross_low, cross_out_grad).astype(low_type)
    bias_self_out = column_sums(self_out_grad)
    bias_cross_q = column_sums(cross_q_grad)
    bias_cross_out = column_sums(cross_out_grad)

    square = jnp.stack([part_self_out, part_cross_q, part_cross_out], 0)
    square = square.reshape(3, line, 2, reps, weight_rows // reps, model)
    square_own = lax.dynamic_index_in_dim(square, core, 2, keepdims=False)
    square_other = swap(lax.dynamic_index_in_dim(square, 1 - core, 2, keepdims=False), "core", 1)

    bias_parts = jnp.stack([part.reshape(line, unit) for part in rep_order(bias_parts)], 1)
    bias_fc1 = jnp.where(
        jnp.arange(2)[None, :, None, None] == core, bias_parts[:, None], 0.0
    ).reshape(feed)
    small = jnp.concatenate(
        [
            jnp.stack(
                [
                    bias_self_out,
                    bias_cross_q,
                    bias_cross_out,
                    bias_fc2,
                    gain_one,
                    gain_two,
                    gain_three,
                    shift_one,
                    shift_two,
                    shift_three,
                ],
                0,
            ),
            bias_fc1.reshape(-1, model),
        ],
        0,
    )
    hops = bits_of("core") + bits_of("rep") + bits_of("line")

    def hop(values, count):
        for _ in range(count):
            values = values + swap(values, *hops.pop(0))
        return values

    small = hop(small, 1)
    square = square_own.astype(jnp.float32) + square_other.astype(jnp.float32)
    square = square.astype(low_type).transpose(2, 1, 0, 3, 4)
    square = parts_of(square, 0)
    held = (square, small, second_sums, first_near)
    mixed_grad[0], held = stage((mixed_grad[0], held))
    square, small, second_sums, first_near = held
    first_sums = sum_of(all_terms(first_parts, first_found, first_near)).astype(low_type)
    first_sums = lax.psum_scatter(first_sums, "line", scatter_dimension=0, tiled=True)
    square_terms = trade_over_rep(square)
    wide = 2 * line * unit
    second_sums = second_sums.reshape(unit, model // wide, wide).transpose(1, 0, 2)
    second_sums = double(second_sums.reshape(1, -1, wide), near[0])
    turn = owners

    part_rows = weight_rows // reps

    def with_sums(values, sums):
        rows = two_rows(jnp.broadcast_to(sums, sums.shape[:-2] + (8,) + sums.shape[-1:]))
        return jnp.concatenate([values.astype(low_type), rows], -2)

    def split_sums(values):
        return values[..., :part_rows, :], one_row(values[..., part_rows:, :])[..., :1, :]

    def trade_slices(values):
        sums = jnp.broadcast_to(values[model : model + 1], (group, 1, values.shape[1]))
        values = values[:model].reshape(group, reps, part_rows, -1)
        return trade_over_rep([with_sums(part, sums) for part in parts_of(values, 1)])

    def exchange_slices(terms):
        return exchange(with_sums(*split_sums(sum_of(terms))))

    def join_slices(values):
        values, sums = split_sums(values.astype(jnp.float32))
        values = jnp.stack(rep_order(spread_over_rep(values.astype(low_type))), 0)
        values = values.transpose(0, 2, 1, 3).reshape(weight_rows, group, -1)
        return values, sums[:, 0][None]

    parts, slice_parts = [], []
    for head in range(heads):
        part, slice_part = self_backward(
            head,
            turn,
            places,
            blocks,
            qkv,
            mixed_grad[head],
            self_mixed[head],
            self_totals[head],
        )
        if head == 0:
            small = hop(small, 1)
            held = (part, slice_part, turn, first_sums, second_sums, square_terms, small)
            held, mixed_grad, own_pair_grad = stage((held, mixed_grad, own_pair_grad))
            part, slice_part, turn, first_sums, second_sums, square_terms, small = held
            own_pair_grad = join_columns(own_pair_grad)
            enc_grad = scatter_rows(product_right(own_pair_grad, head_ckv).astype(low_type))
            for offset in near[1:]:
                second_sums = double(second_sums, offset)
            first_sums = first_sums.reshape(2, weight_rows, line * unit).transpose(1, 0, 2)
            first_sums = double(first_sums.reshape(1, -1, wide), near[0])
            pair_sums = jnp.sum(own_pair_grad.astype(jnp.float32), 0)
            pair_sums = jnp.broadcast_to(pair_sums, (LANES, 2 * width))
            pair_slices = jnp.concatenate([product_left(all_states, own_pair_grad), pair_sums], 0)
            square_terms = trade_over_line(sum_of(square_terms).astype(low_type))
        if head == heads - 1:
            held = (part, slice_part, first_sums, second_sums, square_terms, enc_grad)
            held, parts, slice_parts = stage((held, parts, slice_parts))
            part, slice_part, first_sums, second_sums, square_terms, enc_grad = held
        parts.append(exchange(part))
        slice_parts.append(slice_part)

    slice_parts = trade_slices(
        jnp.concatenate([slice_parts[0], pair_slices] + slice_parts[1:], 1)
    )
    for offset in near[1:]:
        first_sums = double(first_sums, offset)
    square = double(sum_of(square_terms).astype(low_type)[None], near[0])
    parts, slice_parts, first_sums, square = stage((parts, slice_parts, first_sums, square))

    slice_parts = exchange_slices(slice_parts)
    for offset in near[1:]:
        square = double(square, offset)
    small = hop(small, 1)
    second_sums = jnp.stack(rep_order([second_sums[d] for d in range(reps)]), 0)
    second_sums = second_sums.reshape(reps, model // wide, unit, wide)
    grad_fc2 = second_sums.transpose(0, 2, 1, 3).reshape(-1, model).astype(jnp.float32)
    first_sums = jnp.stack(rep_order([first_sums[d] for d in range(reps)]), 0)
    first_sums = first_sums.reshape(reps, weight_rows, 2, line, unit)
    first_own = lax.dynamic_index_in_dim(first_sums, core, 2, keepdims=False)
    first_other = lax.dynamic_index_in_dim(first_sums, 1 - core, 2, keepdims=False)
    first_other = swap(first_other.reshape(-1, line * unit), "core", 1)
    first_other = first_other.reshape(first_own.shape)
    input_grad = first_grad
    rows = turned.reshape(-1, model)
    input_grad = input_grad + product_left(jnp.stack(parts, 1).reshape(rows.shape[0], tok), rows)
    held = (first_own, first_other, square, input_grad, grad_fc2, small)
    slice_parts, held = stage((slice_parts, held))
    first_own, first_other, square, input_grad, grad_fc2, small = held

    slice_parts = join_slices(slice_parts)
    small = hop(small, len(hops))
    square = jnp.stack(rep_order([square[d] for d in range(reps)]), 1).astype(jnp.float32)
    grad_self_out, grad_cross_q, grad_cross_out = [
        square[i].reshape(weight_rows, model) for i in range(3)
    ]
    grad_fc1 = jnp.where(
        core == 0, jnp.stack([first_own, first_other], 0), jnp.stack([first_other, first_own], 0)
    )
    grad_fc1 = grad_fc1.transpose(2, 3, 0, 1, 4).reshape(weight_rows, feed).astype(jnp.float32)

    def of_self(values):
        found, start = [], 0
        for head in range(heads):
            found.append(values[..., start : start + 3 * HEAD_DIM])
            start += 3 * HEAD_DIM + (0 if head else 2 * width)
        found = [each.reshape(-1, group, 3, HEAD_DIM) for each in found]
        return jnp.stack(found, 3).transpose(0, 2, 1, 3, 4).reshape(-1, 3, model)

    def of_cross(values):
        values = values[..., 3 * HEAD_DIM : 3 * HEAD_DIM + 2 * width]
        return values.reshape(-1, group, 2, width).transpose(0, 2, 1, 3).reshape(-1, 2, model)

    grad_self_qkv = of_self(slice_parts[0].astype(jnp.float32)).reshape(weight_rows, 3 * model)
    grad_cross_kv = of_cross(slice_parts[0].astype(jnp.float32)).reshape(weight_rows, 2 * model)
    bias_self, bias_cross_v = of_self(slice_parts[1]), of_cross(slice_parts[1])[0, 1]
    grad_biases = jnp.stack(
        [
            bias_self[0, 0],
            bias_self[0, 2],
            small[0],
            small[1],
            bias_cross_v,
            small[2],
            small[3],
        ],
        0,
    )
    return (
        output,
        input_grad,
        enc_grad.astype(jnp.float32),
        grad_self_qkv,
        grad_self_out,
        grad_cross_q,
        grad_cross_kv,
        grad_cross_out,
        grad_fc1,
        grad_fc2,
        grad_biases,
        small[10:].reshape(-1),
        small[4:7],
        small[7:10],
    )


def solution(mesh):
    reps, group = mesh.devices.shape
    split = jax.sharding.Mesh(
        mesh.devices.reshape(reps, group // 2, 2), ("rep",) + SHARD
    )
    rows, cut = P(("rep",) + SHARD, None), P(SHARD, None)
    return jax.shard_map(
        local,
        mesh=split,
        in_specs=(rows,) * 3 + (P("rep", None),) + (cut,) * 7 + (P(),) * 4,
        out_specs=(rows,) * 3 + (cut,) * 7 + (P(),) * 4,
        check_vma=False,
    )
```

```python
import functools
import math

import jax
import jax.numpy as jnp
from jax import lax
from jax.experimental import pallas as pl
from jax.experimental.pallas import tpu as pltpu
from jax.sharding import PartitionSpec as P

HEADS = 16
HEAD_DIM = 64
LANES = 128

masked_score = -1000000000.0
norm_epsilon = 1e-05
low_type = jnp.bfloat16
SHARD = ("line", "core")


def norm_rows(values, gain_row, shift_row):
    row_mean = jnp.mean(values, -1, keepdims=True)
    centered = values - row_mean
    variance = jnp.mean(centered * centered, -1, keepdims=True)
    return centered * lax.rsqrt(variance + norm_epsilon) * gain_row + shift_row


def product(former, latter):
    return jnp.dot(former, latter, preferred_element_type=jnp.float32)


def product_left(former, latter):
    return lax.dot_general(
        former, latter, (((0,), (0,)), ((), ())), preferred_element_type=jnp.float32
    )


def product_right(former, latter):
    return lax.dot_general(
        former, latter, (((1,), (1,)), ((), ())), preferred_element_type=jnp.float32
    )


def column_sums(values):
    return jnp.sum(values.astype(jnp.float32), 0)


def head_columns(index):
    return slice(index * HEAD_DIM, (index + 1) * HEAD_DIM)


def causal_rows(keys, queries):
    key_index = lax.broadcasted_iota(jnp.int32, (keys, queries), 0)
    query_index = lax.broadcasted_iota(jnp.int32, (keys, queries), 1)
    return key_index <= query_index


def of_head(values, head):
    if values.shape[1] == HEAD_DIM:
        return values
    column = lax.broadcasted_iota(jnp.int32, values.shape, 1)
    inside = (column >= head * HEAD_DIM) & (column < (head + 1) * HEAD_DIM)
    return jnp.where(inside, values, jnp.zeros_like(values))


def turn_head(source, start, width, head, out, tok):
    for row in range(0, source.shape[0], tok):
        block = jnp.transpose(source[row : row + tok, start : start + width])
        out[:, row : row + tok] = block[head_columns(head)]


def over_keys(slot, half, tok, step, first, keep):
    @pl.when(slot < half)
    def _():
        keep(
            lax.fori_loop(0, slot, lambda j, c: step(pl.multiple_of(j * tok, tok), tok, c), first)
        )

    @pl.when(slot >= half)
    def _():
        keep(step(0, half * tok, first))


def self_forward_kernel(tok, width, half, head, count, owner, slot_of, *refs):
    if count:
        blocks, (weight, bias, scale, qkv, mixed, total, value_t) = refs[:count], refs[count:]
    else:
        qkv, mixed, total, value_t = refs
    slot = pl.program_id(0)

    @pl.when(slot == 0)
    def _():
        if count:
            for index, block in enumerate(blocks):
                rows = (product(block[...], weight[...]) + bias[...]) * scale[...]
                start = pl.multiple_of(slot_of[index] * tok, tok)
                qkv[pl.ds(start, tok), :] = rows.astype(low_type)
        turn_head(qkv, 2 * width, width, head, value_t, tok)

    base = pl.multiple_of(slot * tok, tok)
    query_t = jnp.transpose(of_head(qkv[pl.ds(base, tok), :width], head))

    def step(start, seen, carry, causal=False):
        top, weight, mix = carry
        keys = qkv[pl.ds(start, seen), width : 2 * width]
        scores = product(keys, query_t)
        if causal:
            scores = jnp.where(causal_rows(seen, tok), scores, masked_score)
        new_top = jnp.maximum(top, jnp.max(scores, 0, keepdims=True))
        scale = jnp.exp(top - new_top)
        power = jnp.exp(scores - new_top)
        weight = weight * scale + jnp.sum(power, 0, keepdims=True)
        mix = mix * scale + product(value_t[:, pl.ds(start, seen)], power.astype(low_type))
        return (new_top, weight, mix)

    first = (
        jnp.full((1, tok), -1e30, jnp.float32),
        jnp.zeros((1, tok), jnp.float32),
        jnp.zeros((HEAD_DIM, tok), jnp.float32),
    )

    def keep(carry):
        top, weight, mix = step(base, tok, carry, True)
        mixed[...] = (mix / weight).astype(low_type)
        total[...] = top + jnp.log(weight)

    over_keys(slot, half, tok, step, first, keep)


def self_backward_kernel(tok, width, half, head, scale, count, owner, place, *refs):
    blocks, refs = refs[:count], refs[count:]
    before, refs = refs[:-12], refs[-12:]
    qkv, mixed_grad, mixed, total, out, slice_grad = refs[:6]
    key_t, key_sum, value_sum, rows, slice_sum, arrived = refs[6:]
    slot = pl.program_id(0)
    copies = [
        pltpu.make_async_copy(block, rows.at[i], arrived.at[i]) for i, block in enumerate(blocks)
    ]

    @pl.when(slot == 0)
    def _():
        for copy in copies:
            copy.start()
        turn_head(qkv, width, width, head, key_t, tok)
        key_sum[...] = jnp.zeros_like(key_sum)
        value_sum[...] = jnp.zeros_like(value_sum)

    base = pl.multiple_of(slot * tok, tok)
    query = of_head(qkv[pl.ds(base, tok), :width], head)
    query_t = jnp.transpose(query)
    narrow = mixed_grad[...]
    delta = jnp.sum(narrow.astype(jnp.float32) * mixed[...].astype(jnp.float32), 0, keepdims=True)
    empty = jnp.zeros_like(narrow)
    heads = width // HEAD_DIM
    grad_t = jnp.concatenate([narrow if h == head else empty for h in range(heads)], 0)
    grad = jnp.transpose(grad_t)

    def step(start, seen, carry, causal=False):
        keys = qkv[pl.ds(start, seen), width : 2 * width]
        values = qkv[pl.ds(start, seen), 2 * width :]
        power = jnp.exp(product(keys, query_t) - total[...])
        if causal:
            power = jnp.where(causal_rows(seen, tok), power, 0.0)
        slope = product(values, grad_t)
        score_grad = (power * (slope - delta)).astype(low_type)
        value_sum[pl.ds(start, seen), :] += product(power.astype(low_type), grad)
        key_sum[pl.ds(start, seen), :] += product(score_grad, query)
        return carry + product(key_t[:, pl.ds(start, seen)], score_grad)

    def keep(carry):
        query_grad = step(base, tok, carry, True).astype(low_type) * scale
        out[pl.ds(owner[slot], 1), :HEAD_DIM, :] = query_grad[None]

    over_keys(slot, half, tok, step, jnp.zeros((HEAD_DIM, tok), jnp.float32), keep)

    @pl.when(slot == pl.num_programs(0) - 1)
    def _():
        for copy in copies:
            copy.wait()
        slice_sum[...] = jnp.zeros_like(slice_sum)
        model = rows.shape[2]
        ones = jnp.ones((tok, LANES), low_type)

        def finish(p, carry):
            source = pl.ds(pl.multiple_of(p * tok, tok), tok)
            key_grad = jnp.transpose(key_sum[source, :])[head_columns(head)]
            value_grad = jnp.transpose(value_sum[source, :])[head_columns(head)]
            target = pl.ds(owner[p], 1)
            out[target, HEAD_DIM : 2 * HEAD_DIM, :] = key_grad.astype(low_type)[None]
            out[target, 2 * HEAD_DIM :, :] = value_grad.astype(low_type)[None]
            columns = out[target][0]
            slice_sum[:, :model] += product(columns, rows[pl.ds(place[p], 1)][0])
            slice_sum[:, model:] += product(columns, ones)
            return carry

        lax.fori_loop(0, pl.num_programs(0), finish, 0)
        if head < heads - 1:
            slice_grad[...] = slice_sum[...]
        else:
            kinds = [slice(k * HEAD_DIM, (k + 1) * HEAD_DIM) for k in range(3)]
            every = [part[kind, :] for kind in kinds for part in (*before, slice_sum)]
            slice_grad[...] = jnp.transpose(jnp.concatenate(every, 0))


def cross_forward_kernel(width, query, pair, mixed, total):
    keys, values = pair[0], jnp.transpose(pair[1])
    mixes = []
    for head in range(width // HEAD_DIM):
        cols = head_columns(head)
        scores = product_right(keys[:, cols], query[:, cols])
        top = jnp.max(scores, 0, keepdims=True)
        power = jnp.exp(scores - top)
        weight = jnp.sum(power, 0, keepdims=True)
        mixes.append(product(values[cols], power.astype(low_type)) / weight)
        total[head : head + 1, :] = top + jnp.log(weight)
    mixed[...] = jnp.transpose(jnp.concatenate(mixes, 0)).astype(low_type)


def cross_backward_kernel(width, scale, query, pair, mixed_grad, mixed, total, out, pair_grad):
    heads = width // HEAD_DIM
    keys, values = pair[0], pair[1]
    keys_t = jnp.transpose(keys)
    grad = mixed_grad[...]
    both = jnp.transpose(grad.astype(jnp.float32) * mixed[...].astype(jnp.float32))
    query_parts, key_parts, value_parts = [], [], []
    for head in range(heads):
        cols = head_columns(head)
        scores = product_right(keys[:, cols], query[:, cols])
        power = jnp.exp(scores - total[head : head + 1, :])
        slope = product_right(values[:, cols], grad[:, cols])
        delta = jnp.sum(both[cols], 0, keepdims=True)
        score_grad = (power * (slope - delta)).astype(low_type)
        value_parts.append(product(power.astype(low_type), grad[:, cols]))
        key_parts.append(product(score_grad, query[:, cols]))
        query_parts.append(product(keys_t[cols], score_grad))
    query_grad = jnp.transpose(jnp.concatenate(query_parts, 0)).astype(low_type)
    out[...] = query_grad * scale
    pair_grad[0] = jnp.concatenate(key_parts, 1).astype(low_type)
    pair_grad[1] = jnp.concatenate(value_parts, 1).astype(low_type)


declared = pl.CostEstimate(flops=2**20, transcendentals=0, bytes_accessed=2**16)


def kernel_options(megabytes):
    return pltpu.CompilerParams(
        dimension_semantics=("arbitrary",), vmem_limit_bytes=megabytes * 2**20
    )


def whole_block(shape):
    return pl.BlockSpec(shape, lambda *_: (0,) * len(shape), pipeline_mode=pl.Buffered(1))


def self_forward(head, owner, slot_of, tok, qkv, blocks=(), weight=None, bias=None, scale=None):
    make = qkv is None
    group = owner.shape[0]
    rows = group * tok
    width = (weight if make else qkv).shape[1] // 3
    inputs = (*blocks, weight, bias[None], scale[None]) if make else (qkv,)
    out_shape = [
        jax.ShapeDtypeStruct((group, HEAD_DIM, tok), low_type),
        jax.ShapeDtypeStruct((group, 1, tok), jnp.float32),
    ]
    out_specs = [
        pl.BlockSpec((None, HEAD_DIM, tok), lambda p, owner, _: (owner[p], 0, 0)),
        pl.BlockSpec((None, 1, tok), lambda p, *_: (p, 0, 0)),
    ]
    if make:
        out_shape = [jax.ShapeDtypeStruct((rows, 3 * width), low_type)] + out_shape
        out_specs = [pl.BlockSpec((rows, 3 * width), lambda *_: (0, 0))] + out_specs
    made = pl.pallas_call(
        functools.partial(
            self_forward_kernel, tok, width, group // 2, head, len(blocks)
        ),
        out_shape=out_shape,
        grid_spec=pltpu.PrefetchScalarGridSpec(
            num_scalar_prefetch=2,
            grid=(group,),
            in_specs=[whole_block(each.shape) for each in inputs],
            out_specs=out_specs,
            scratch_shapes=[pltpu.VMEM((HEAD_DIM, rows), low_type)],
        ),
        compiler_params=kernel_options(52),
        cost_estimate=declared,
        name="self_forward",
    )(owner, slot_of, *inputs)
    return made if make else [qkv, *made]


def self_backward(head, owner, place, blocks, before, qkv, mixed_grad, mixed, total):
    rows, width = qkv.shape[0], qkv.shape[1] // 3
    tok, model = blocks[0].shape
    group = rows // tok
    owned = pl.BlockSpec((None, HEAD_DIM, tok), lambda p, owner, _: (owner[p], 0, 0))
    slices = (3 * HEAD_DIM, model + LANES)
    if head == width // HEAD_DIM - 1:
        slices = (model + LANES, 3 * width)
    else:
        before = ()
    return pl.pallas_call(
        functools.partial(
            self_backward_kernel, tok, width, group // 2, head, HEAD_DIM ** (-0.5), group
        ),
        out_shape=(
            jax.ShapeDtypeStruct((group, 3 * HEAD_DIM, tok), low_type),
            jax.ShapeDtypeStruct(slices, jnp.float32),
        ),
        grid_spec=pltpu.PrefetchScalarGridSpec(
            num_scalar_prefetch=2,
            grid=(group,),
            in_specs=[pl.BlockSpec(memory_space=pl.ANY)] * group
            + [whole_block(each.shape) for each in before]
            + [
                whole_block(qkv.shape),
                owned,
                owned,
                pl.BlockSpec((None, 1, tok), lambda p, *_: (p, 0, 0)),
            ],
            out_specs=[
                pl.BlockSpec((group, 3 * HEAD_DIM, tok), lambda *_: (0, 0, 0)),
                pl.BlockSpec(slices, lambda *_: (0, 0)),
            ],
            scratch_shapes=[
                pltpu.VMEM((HEAD_DIM, rows), low_type),
                pltpu.VMEM((rows, width), jnp.float32),
                pltpu.VMEM((rows, width), jnp.float32),
                pltpu.VMEM((group, tok, model), low_type),
                pltpu.VMEM((3 * HEAD_DIM, model + LANES), jnp.float32),
                pltpu.SemaphoreType.DMA((group,)),
            ],
        ),
        compiler_params=kernel_options(52),
        cost_estimate=declared,
        name="self_backward",
    )(owner, place, *blocks, *before, qkv, mixed_grad, mixed, total)


def split_columns(values, group):
    rows = values.shape[0]
    return values.reshape(rows, group, -1).transpose(1, 0, 2)


def join_columns(values):
    return values.transpose(1, 0, 2).reshape(values.shape[1], -1)


def by_head(values, group):
    rows, width = values.shape[0], values.shape[1] // group
    if width % LANES == 0:
        return values, pl.BlockSpec((rows, width), lambda g: (0, g))
    return split_columns(values, group), pl.BlockSpec((None, rows, width), lambda g: (g, 0, 0))


def of_heads(values, group):
    return values if values.ndim == 2 else join_columns(values)


def cross_forward(queries, pairs):
    group, _, states, width = pairs.shape
    rows = queries.shape[0]
    queries, query_spec = by_head(queries, group)
    mixed, total = pl.pallas_call(
        functools.partial(cross_forward_kernel, width),
        out_shape=(
            jax.ShapeDtypeStruct(queries.shape, low_type),
            jax.ShapeDtypeStruct((group, 8, rows), jnp.float32),
        ),
        grid=(group,),
        in_specs=[query_spec, pl.BlockSpec((None, 2, states, width), lambda g: (g, 0, 0, 0))],
        out_specs=[query_spec, pl.BlockSpec((None, 8, rows), lambda g: (g, 0, 0))],
        compiler_params=kernel_options(32),
        cost_estimate=declared,
        name="cross_forward",
    )(queries, pairs)
    return of_heads(mixed, group), total


def cross_backward(queries, pairs, mixed_grad, mixed, total):
    group, _, states, width = pairs.shape
    rows = queries.shape[0]
    queries, spec = by_head(queries, group)
    mixed_grad, mixed = by_head(mixed_grad, group)[0], by_head(mixed, group)[0]
    pair_spec = pl.BlockSpec((None, 2, states, width), lambda g: (g, 0, 0, 0))
    query_grad, pair_grad = pl.pallas_call(
        functools.partial(cross_backward_kernel, width, HEAD_DIM ** (-0.5)),
        out_shape=(
            jax.ShapeDtypeStruct(queries.shape, low_type),
            jax.ShapeDtypeStruct(pairs.shape, low_type),
        ),
        grid=(group,),
        in_specs=[spec, pair_spec, spec, spec, pl.BlockSpec((None, 8, rows), lambda g: (g, 0, 0))],
        out_specs=[spec, pair_spec],
        compiler_params=kernel_options(32),
        cost_estimate=declared,
        name="cross_backward",
    )(queries, pairs, mixed_grad, mixed, total)
    return of_heads(query_grad, group), pair_grad


def swap(values, axis, offset):
    size = lax.axis_size(axis)
    return lax.ppermute(values, axis, [(i, i ^ offset) for i in range(size)])


def sum_over(values, steps):
    for axis, offset in steps:
        values = (
            values.astype(jnp.float32) + swap(values, axis, offset).astype(jnp.float32)
        ).astype(values.dtype)
    return values


def bits_of(axis):
    return [(axis, 1 << i) for i in range(lax.axis_size(axis).bit_length() - 1)]


def spread_over_rep(values):
    return [values] + [swap(values, "rep", d) for d in range(1, lax.axis_size("rep"))]


def double(values, offset):
    return jnp.concatenate([values, swap(values, "rep", offset)], 0)


def parts_of(values, axis):
    own = lax.axis_index("rep")
    return [
        lax.dynamic_index_in_dim(values, own ^ d, axis, keepdims=False)
        for d in range(values.shape[axis])
    ]


def rep_order(pieces):
    own = lax.axis_index("rep")
    count = len(pieces)
    return [lax.select_n(own, *[pieces[d ^ i] for i in range(count)]) for d in range(count)]


def trade_over_rep(pieces):
    return [pieces[0]] + [swap(pieces[d], "rep", d) for d in range(1, len(pieces))]


def far_terms(pieces):
    if len(pieces) != 4:
        return [swap(pieces[d], "rep", d) for d in range(len(pieces)) if d & (d - 1)]
    half = pieces[3].shape[0] // 2
    return [swap(pieces[3][:half], "rep", 1), swap(pieces[3][half:], "rep", 2)]


def near_terms(pieces, found):
    near = [1 << i for i in range(len(pieces).bit_length() - 1)]
    if len(pieces) != 4:
        return [swap(pieces[d], "rep", d) for d in near]
    half = pieces[3].shape[0] // 2
    one, two = pieces[1], pieces[2]
    one = jnp.concatenate([one[:half], sum_of([one[half:], found[1]]).astype(low_type)], 0)
    two = jnp.concatenate([sum_of([two[:half], found[0]]).astype(low_type), two[half:]], 0)
    return [swap(one, "rep", 1), swap(two, "rep", 2)]


def all_terms(pieces, found, near):
    return [pieces[0]] + near + (found if len(pieces) != 4 else [])


def sum_of(terms):
    return sum(term.astype(jnp.float32) for term in terms)


def trade_over_line(values):
    line, own = lax.axis_size("line"), lax.axis_index("line")
    terms = [lax.dynamic_index_in_dim(values, own, 0, keepdims=False)]
    for k in range(1, line):
        piece = lax.dynamic_index_in_dim(values, (own + k) % line, 0, keepdims=False)
        terms.append(lax.ppermute(piece, "line", [(i, (i + k) % line) for i in range(line)]))
    return terms


def two_rows(values):
    high = values.astype(low_type)
    return jnp.concatenate([high, (values - high.astype(jnp.float32)).astype(low_type)], -2)


def one_row(values):
    high, low = jnp.split(values.astype(jnp.float32), 2, -2)
    return high + low


def stage(values):
    return lax.optimization_barrier(values)


def shift(values):
    line = lax.axis_size("line")
    return lax.ppermute(values, "line", [(i, (i + 1) % line) for i in range(line)])


def gather_rows(values):
    return lax.all_gather(values, SHARD, axis=0, tiled=True)


def scatter_rows(values):
    return lax.psum_scatter(values, SHARD, scatter_dimension=0, tiled=True)


def exchange(values):
    return lax.all_to_all(values, SHARD, split_axis=0, concat_axis=0, tiled=True)


def gelu_and_slope(values):
    reduced = jnp.abs(values) * (0.5**0.5)
    inverse = 1.0 / (1.0 + 0.3275911 * reduced)
    bell = jnp.exp(-(reduced * reduced))
    tail = 1.061405429 * inverse - 1.453152027
    tail = tail * inverse + 1.421413741
    tail = tail * inverse - 0.284496736
    tail = (tail * inverse + 0.254829592) * inverse * bell * 0.5
    normal = jnp.where(values >= 0.0, 1.0 - tail, tail)
    return values * normal, normal + values * (bell * (0.5 / math.pi) ** 0.5)


def local(
    layer_input,
    encoder_states,
    out_grad,
    placement,
    w_self_qkv,
    w_self_out,
    w_cross_q,
    w_cross_kv,
    w_cross_out,
    w_fc1,
    w_fc2,
    proj_biases,
    fc1_bias,
    norm_gains,
    norm_shifts,
):
    reps, line = lax.axis_size("rep"), lax.axis_size("line")
    rep, core = lax.axis_index("rep"), lax.axis_index("core")
    group = 2 * line
    member = 2 * lax.axis_index("line") + core
    tok, model = layer_input.shape
    feed = w_fc1.shape[1]
    weight_rows = w_self_qkv.shape[0]
    width = model // group
    unit = feed // (group * reps)
    score_scale = HEAD_DIM ** (-0.5)
    slot_table = placement[0]
    device_ids = jnp.arange(group, dtype=jnp.int32)
    owners = jnp.sum(
        jnp.where(slot_table[None, :] == device_ids[:, None], device_ids[None, :], 0), 1
    )

    def own_columns(row):
        return lax.dynamic_slice(row, (member * width,), (width,))

    def in_columns(row):
        return lax.dynamic_update_slice(jnp.zeros((model,), jnp.float32), row, (member * width,))

    part_rows = weight_rows // reps
    slices = jnp.concatenate(
        [
            lax.dynamic_slice_in_dim(weight, rep * part_rows, part_rows, 0).reshape(
                part_rows, -1, group, width
            )
            for weight in (w_self_qkv, w_cross_kv)
        ],
        1,
    )
    slices = slices.transpose(2, 0, 1, 3).reshape(group, weight_rows // reps, 5 * width)
    first_cut = w_fc1.reshape(weight_rows, line, 2, reps, unit)
    first_cut = lax.dynamic_index_in_dim(first_cut, rep, 3, keepdims=False)
    first_own = lax.dynamic_index_in_dim(first_cut, core, 2, keepdims=False)
    first_other = lax.dynamic_index_in_dim(first_cut, 1 - core, 2, keepdims=False)
    first_own = first_own.reshape(weight_rows, line * unit)
    first_other = swap(first_other.reshape(weight_rows, line * unit), "core", 1)
    first_cut = jnp.where(
        core == 0,
        jnp.concatenate([first_own, first_other], 0),
        jnp.concatenate([first_other, first_own], 0),
    )
    second_cut = lax.dynamic_slice_in_dim(w_fc2, rep * unit, unit, 0)
    bias_cut = lax.dynamic_index_in_dim(
        fc1_bias.reshape(line, 2, reps, unit), core, 1, keepdims=False
    )
    bias_cut = [bias_cut[:, r].reshape(line * unit) for r in range(reps)]
    bias_cut = rep_order(bias_cut)

    square = jnp.stack([w_self_out, w_cross_q, w_cross_out], 0)
    square = square.reshape(3, reps, weight_rows // reps, model)
    square = lax.dynamic_index_in_dim(square, rep, 1, keepdims=False).reshape(-1, model)

    inputs = layer_input.astype(jnp.float32)
    zeros = jnp.zeros((width,), jnp.float32)
    head_bias = jnp.concatenate([own_columns(proj_biases[0]), zeros, own_columns(proj_biases[1])])
    head_scale = jnp.concatenate([jnp.full((width,), score_scale), jnp.ones((2 * width,))])
    cross_bias = jnp.concatenate([zeros, own_columns(proj_biases[4])])

    near = [1 << i for i in range(reps.bit_length() - 1)]
    far = [d for d in range(1, reps) if d not in near]
    slices = exchange(slices)
    blocks = [layer_input, swap(layer_input, "core", 1)]
    block = shift(layer_input)
    block, slices, blocks, first_cut, square, encoder_states, second_cut = stage(
        (block, slices, blocks, first_cut, square, encoder_states, second_cut)
    )

    both_cut = lax.all_gather(
        jnp.concatenate([second_cut, square], 0), "line", axis=0, tiled=True
    ).reshape(line, -1, model)
    blocks += [block, swap(block, "core", 1)]
    block = shift(block)
    slices = spread_over_rep(slices)
    block, slices, blocks, encoder_states = stage((block, slices, blocks, encoder_states))

    for step in range(line - 3):
        blocks += [block, swap(block, "core", 1)]
        block = shift(block)
    slices = jnp.stack(rep_order(slices), 1).reshape(model, 5 * width)
    head_qkv, head_ckv = slices[:, : 3 * width], slices[:, 3 * width :]
    all_states = gather_rows(encoder_states)
    block, blocks, both_cut, head_qkv, head_ckv, all_states, first_cut = stage(
        (block, blocks, both_cut, head_qkv, head_ckv, all_states, first_cut)
    )

    blocks += [block, swap(block, "core", 1)]
    square = spread_over_rep(both_cut[:, unit:])
    wfirst = {0: lax.all_gather(first_cut, "line", axis=0, tiled=True)}
    head_pair = (product(all_states, head_ckv) + cross_bias).astype(low_type)
    head_pair = split_columns(head_pair, 2)
    wsecond = {0: both_cut[:, :unit].reshape(line * unit, model)}
    back = (lax.axis_index("line") - owners // 2) % line
    places = 2 * back + ((owners % 2) ^ core)
    slot_of = jnp.sum(
        jnp.where(places[None, :] == device_ids[:, None], device_ids[None, :], 0), 1
    )
    heads = width // HEAD_DIM
    made, turn, self_totals, self_mixed, self_low = None, owners, [], [], []
    for head in range(heads):
        extra = () if head else (blocks, head_qkv, head_bias, head_scale)
        made, mixed, total = self_forward(head, turn, slot_of, tok, made, *extra)
        self_totals.append(total)
        if head == 0:
            mixed, turn, square, head_pair = stage((mixed, turn, square, head_pair))
            wsecond.update({d: swap(wsecond[0], "rep", d) for d in near})
            square = jnp.stack(rep_order(square), 1)
            square_other = swap(square, "core", 1)
        if head == heads - 1:
            held = (mixed, wfirst, square, square_other)
            held, wsecond, self_low = stage((held, wsecond, self_low))
            mixed, wfirst, square, square_other = held
            wsecond.update({d: swap(wsecond[0], "rep", d) for d in far})
            wfirst.update({d: swap(wfirst[0], "rep", d) for d in near})
        self_mixed.append(mixed)
        self_low.append(exchange(mixed))
    qkv = made
    square = jnp.where(
        core == 0, jnp.stack([square, square_other], 1), jnp.stack([square_other, square], 1)
    )
    square = square.reshape(line, 2, reps, 3, weight_rows // reps, model)
    full_out, full_cross_q, full_cross_out = [
        square[:, :, :, i].reshape(model, model) for i in range(3)
    ]
    pairs = lax.all_gather(head_pair, SHARD, axis=0, tiled=False)
    self_low, pairs = stage((self_low, pairs))
    self_low = jnp.stack(self_low, 1).reshape(model, tok)

    first_sum = inputs + (product_left(self_low, full_out) + proj_biases[2])
    first_norm, norm1_back = jax.vjp(norm_rows, first_sum, norm_gains[0], norm_shifts[0])
    first_low = first_norm.astype(low_type)
    cross_queries = ((product(first_low, full_cross_q) + proj_biases[3]) * score_scale).astype(
        low_type
    )
    cross_low, cross_total = cross_forward(cross_queries, pairs)
    cross_low, wfirst, wsecond = stage((cross_low, wfirst, wsecond))
    wfirst.update({d: swap(wfirst[0], "rep", d) for d in far})
    second_sum = first_norm + (product(cross_low, full_cross_out) + proj_biases[5])
    second_norm, norm2_back = jax.vjp(norm_rows, second_sum, norm_gains[1], norm_shifts[1])
    second_low = second_norm.astype(low_type)

    turned = jnp.transpose(stage((head_qkv, second_low))[0])
    turned = turned.reshape(3, heads, HEAD_DIM, model).transpose(1, 0, 2, 3)
    turned = gather_rows(turned.reshape(-1, model))
    turned = turned.reshape(group, heads, 3 * HEAD_DIM, model)

    second_both = jnp.concatenate([second_low, swap(second_low, "core", 1)], 0)
    feed_sum, hidden, slopes = 0.0, [], []
    for part in range(reps):
        active, slope = gelu_and_slope(product(second_both, wfirst[part]) + bias_cut[part])
        hidden.append(active.astype(low_type))
        slopes.append(slope)
        feed_sum = feed_sum + product(hidden[part], wsecond[part])
    feed_other = swap(feed_sum[tok:].astype(low_type), "core", 1).astype(jnp.float32)
    third_sum = second_norm + (feed_sum[:tok] + feed_other + proj_biases[6])
    result, norm3_back = jax.vjp(norm_rows, third_sum, norm_gains[2], norm_shifts[2])
    output = result.astype(low_type)

    third_grad, gain_three, shift_three = norm3_back(out_grad.astype(jnp.float32))
    feed_grad = third_grad.astype(low_type)
    bias_fc2 = column_sums(feed_grad)
    feed_both = jnp.concatenate([feed_grad, swap(feed_grad, "core", 1)], 0)
    second_parts = [
        product_left(hidden[part], feed_both).astype(low_type) for part in range(reps)
    ]
    feed_both, second_parts = stage((feed_both, second_parts))
    second_found = far_terms(second_parts)
    back_sum, first_parts, bias_parts = 0.0, [], []
    for part in range(reps):
        pre_grad = (product_right(feed_both, wsecond[part]) * slopes[part]).astype(low_type)
        first_parts.append(product_left(second_both, pre_grad).astype(low_type))
        bias_parts.append(column_sums(pre_grad))
        back_sum = back_sum + product_right(pre_grad, wfirst[part])
        if part == reps // 2 - 1:
            feed_both, back_sum, second_found = stage((feed_both, back_sum, second_found))
            second_near = near_terms(second_parts, second_found)
    back_sum, second_near, first_parts = stage((back_sum, second_near, first_parts))
    second_sums = sum_of(all_terms(second_parts, second_found, second_near)).astype(low_type)
    back_other = swap(back_sum[tok:].astype(low_type), "core", 1).astype(jnp.float32)
    second_grad, gain_two, shift_two = norm2_back(third_grad + (back_sum[:tok] + back_other))
    second_grad, second_sums, first_parts = stage((second_grad, second_sums, first_parts))
    second_sums = lax.psum_scatter(second_sums, "line", scatter_dimension=0, tiled=True)
    first_found = far_terms(first_parts)

    cross_out_grad = second_grad.astype(low_type)
    cross_mixed_grad = product_right(cross_out_grad, full_cross_out).astype(low_type)
    cross_q_grad, pair_grad = cross_backward(
        cross_queries, pairs, cross_mixed_grad, cross_low, cross_total
    )
    cross_q_grad, pair_grad, first_found, turned = stage(
        (cross_q_grad, pair_grad, first_found, turned)
    )
    first_near = near_terms(first_parts, first_found)
    own_pair_grad = lax.psum_scatter(pair_grad, SHARD, scatter_dimension=0, tiled=False)
    first_grad, gain_one, shift_one = norm1_back(
        second_grad + product_right(cross_q_grad, full_cross_q)
    )
    self_out_grad = first_grad.astype(low_type)
    mixed_grad = product_right(full_out, self_out_grad).astype(low_type)
    mixed_grad = mixed_grad.reshape(group, heads, HEAD_DIM, tok)
    held = (self_low, first_low, cross_low, self_out_grad, cross_q_grad, cross_out_grad)
    mixed_grad, held = stage((mixed_grad, held))
    self_low, first_low, cross_low, self_out_grad, cross_q_grad, cross_out_grad = held
    mixed_grad = [exchange(mixed_grad[:, head]) for head in range(heads)]
    part_self_out = product(self_low, self_out_grad).astype(low_type)
    part_cross_q = product_left(first_low, cross_q_grad).astype(low_type)
    part_cross_out = product_left(cross_low, cross_out_grad).astype(low_type)
    bias_self_out = column_sums(self_out_grad)
    bias_cross_q = column_sums(cross_q_grad)
    bias_cross_out = column_sums(cross_out_grad)

    square = jnp.stack([part_self_out, part_cross_q, part_cross_out], 0)
    square = square.reshape(3, line, 2, reps, weight_rows // reps, model)
    square_own = lax.dynamic_index_in_dim(square, core, 2, keepdims=False)
    square_other = swap(lax.dynamic_index_in_dim(square, 1 - core, 2, keepdims=False), "core", 1)

    bias_parts = jnp.stack([part.reshape(line, unit) for part in rep_order(bias_parts)], 1)
    bias_fc1 = jnp.where(
        jnp.arange(2)[None, :, None, None] == core, bias_parts[:, None], 0.0
    ).reshape(feed)
    small = jnp.concatenate(
        [
            jnp.stack(
                [
                    bias_self_out,
                    bias_cross_q,
                    bias_cross_out,
                    bias_fc2,
                    gain_one,
                    gain_two,
                    gain_three,
                    shift_one,
                    shift_two,
                    shift_three,
                ],
                0,
            ),
            bias_fc1.reshape(-1, model),
        ],
        0,
    )
    hops = bits_of("core") + bits_of("rep") + bits_of("line")

    def hop(values, count):
        for _ in range(count):
            values = values + swap(values, *hops.pop(0))
        return values

    small = hop(small, 1)
    square = square_own.astype(jnp.float32) + square_other.astype(jnp.float32)
    square = square.astype(low_type).transpose(2, 1, 0, 3, 4)
    square = parts_of(square, 0)
    held = (square, small, second_sums, first_near)
    mixed_grad[0], held = stage((mixed_grad[0], held))
    square, small, second_sums, first_near = held
    first_sums = sum_of(all_terms(first_parts, first_found, first_near)).astype(low_type)
    first_sums = lax.psum_scatter(first_sums, "line", scatter_dimension=0, tiled=True)
    square_terms = trade_over_rep(square)
    wide = 2 * line * unit
    second_sums = second_sums.reshape(unit, model // wide, wide).transpose(1, 0, 2)
    second_sums = double(second_sums.reshape(1, -1, wide), near[0])
    turn = owners

    part_rows = weight_rows // reps

    def with_sums(values, sums):
        rows = two_rows(jnp.broadcast_to(sums, sums.shape[:-2] + (8,) + sums.shape[-1:]))
        return jnp.concatenate([values.astype(low_type), rows], -2)

    def split_sums(values):
        return values[..., :part_rows, :], one_row(values[..., part_rows:, :])[..., :1, :]

    def trade_slices(values):
        sums = jnp.broadcast_to(values[model : model + 1], (group, 1, values.shape[1]))
        values = values[:model].reshape(group, reps, part_rows, -1)
        return trade_over_rep([with_sums(part, sums) for part in parts_of(values, 1)])

    def exchange_slices(terms):
        return exchange(with_sums(*split_sums(sum_of(terms))))

    def join_slices(values):
        values, sums = split_sums(values.astype(jnp.float32))
        values = jnp.stack(rep_order(spread_over_rep(values.astype(low_type))), 0)
        values = values.transpose(0, 2, 1, 3).reshape(weight_rows, group, -1)
        return values, sums[:, 0][None]

    parts, slice_parts = [], []
    for head in range(heads):
        part, slice_part = self_backward(
            head,
            turn,
            places,
            blocks,
            slice_parts,
            qkv,
            mixed_grad[head],
            self_mixed[head],
            self_totals[head],
        )
        if head == 0:
            small = hop(small, 1)
            held = (part, slice_part, turn, first_sums, second_sums, square_terms, small)
            held, mixed_grad, own_pair_grad = stage((held, mixed_grad, own_pair_grad))
            part, slice_part, turn, first_sums, second_sums, square_terms, small = held
            own_pair_grad = join_columns(own_pair_grad)
            enc_grad = scatter_rows(product_right(own_pair_grad, head_ckv).astype(low_type))
            for offset in near[1:]:
                second_sums = double(second_sums, offset)
            first_sums = first_sums.reshape(2, weight_rows, line * unit).transpose(1, 0, 2)
            first_sums = double(first_sums.reshape(1, -1, wide), near[0])
            pair_sums = jnp.sum(own_pair_grad.astype(jnp.float32), 0)
            pair_sums = jnp.broadcast_to(pair_sums, (LANES, 2 * width))
            pair_slices = jnp.concatenate([product_left(all_states, own_pair_grad), pair_sums], 0)
            square_terms = trade_over_line(sum_of(square_terms).astype(low_type))
        if head == heads - 1:
            held = (part, slice_part, first_sums, second_sums, square_terms, enc_grad)
            held, parts, slice_parts = stage((held, parts, slice_parts))
            part, slice_part, first_sums, second_sums, square_terms, enc_grad = held
        parts.append(exchange(part))
        slice_parts.append(slice_part)

    slice_parts = trade_slices(jnp.concatenate([slice_parts[-1], pair_slices], 1))
    for offset in near[1:]:
        first_sums = double(first_sums, offset)
    square = double(sum_of(square_terms).astype(low_type)[None], near[0])
    small = hop(small, 1)
    held = (first_sums, square, small)
    parts, slice_parts, held = stage((parts, slice_parts, held))
    first_sums, square, small = held

    slice_parts = exchange_slices(slice_parts)
    for offset in near[1:]:
        square = double(square, offset)
    small = hop(small, 1)
    second_sums = jnp.stack(rep_order([second_sums[d] for d in range(reps)]), 0)
    second_sums = second_sums.reshape(reps, model // wide, unit, wide)
    grad_fc2 = second_sums.transpose(0, 2, 1, 3).reshape(-1, model).astype(jnp.float32)
    first_sums = jnp.stack(rep_order([first_sums[d] for d in range(reps)]), 0)
    first_sums = first_sums.reshape(reps, weight_rows, 2, line, unit)
    first_own = lax.dynamic_index_in_dim(first_sums, core, 2, keepdims=False)
    first_other = lax.dynamic_index_in_dim(first_sums, 1 - core, 2, keepdims=False)
    first_other = swap(first_other.reshape(-1, line * unit), "core", 1)
    first_other = first_other.reshape(first_own.shape)
    input_grad = first_grad
    rows = turned.reshape(-1, model)
    input_grad = input_grad + product_left(jnp.stack(parts, 1).reshape(rows.shape[0], tok), rows)
    held = (first_own, first_other, square, input_grad, grad_fc2, small)
    slice_parts, held = stage((slice_parts, held))
    first_own, first_other, square, input_grad, grad_fc2, small = held

    slice_parts = join_slices(slice_parts)
    small = hop(small, len(hops))
    square = jnp.stack(rep_order([square[d] for d in range(reps)]), 1).astype(jnp.float32)
    grad_self_out, grad_cross_q, grad_cross_out = [
        square[i].reshape(weight_rows, model) for i in range(3)
    ]
    grad_fc1 = jnp.where(
        core == 0, jnp.stack([first_own, first_other], 0), jnp.stack([first_other, first_own], 0)
    )
    grad_fc1 = grad_fc1.transpose(2, 3, 0, 1, 4).reshape(weight_rows, feed).astype(jnp.float32)

    def of_self(values):
        values = values[..., : 3 * width].reshape(-1, group, 3, width)
        return values.transpose(0, 2, 1, 3).reshape(-1, 3, model)

    def of_cross(values):
        values = values[..., 3 * width :].reshape(-1, group, 2, width)
        return values.transpose(0, 2, 1, 3).reshape(-1, 2, model)

    grad_self_qkv = of_self(slice_parts[0].astype(jnp.float32)).reshape(weight_rows, 3 * model)
    grad_cross_kv = of_cross(slice_parts[0].astype(jnp.float32)).reshape(weight_rows, 2 * model)
    bias_self, bias_cross_v = of_self(slice_parts[1]), of_cross(slice_parts[1])[0, 1]
    grad_biases = jnp.stack(
        [
            bias_self[0, 0],
            bias_self[0, 2],
            small[0],
            small[1],
            bias_cross_v,
            small[2],
            small[3],
        ],
        0,
    )
    return (
        output,
        input_grad,
        enc_grad.astype(jnp.float32),
        grad_self_qkv,
        grad_self_out,
        grad_cross_q,
        grad_cross_kv,
        grad_cross_out,
        grad_fc1,
        grad_fc2,
        grad_biases,
        small[10:].reshape(-1),
        small[4:7],
        small[7:10],
    )


def solution(mesh):
    reps, group = mesh.devices.shape
    split = jax.sharding.Mesh(
        mesh.devices.reshape(reps, group // 2, 2), ("rep",) + SHARD
    )
    rows, cut = P(("rep",) + SHARD, None), P(SHARD, None)
    return jax.shard_map(
        local,
        mesh=split,
        in_specs=(rows,) * 3 + (P("rep", None),) + (cut,) * 7 + (P(),) * 4,
        out_specs=(rows,) * 3 + (cut,) * 7 + (P(),) * 4,
        check_vma=False,
    )
```

```python
import functools
import math

import jax
import jax.numpy as jnp
from jax import lax
from jax.experimental import pallas as pl
from jax.experimental.pallas import tpu as pltpu
from jax.sharding import PartitionSpec as P

HEADS = 16
HEAD_DIM = 64
LANES = 128

masked_score = -1000000000.0
norm_epsilon = 1e-05
low_type = jnp.bfloat16
SHARD = ("line", "core")


def norm_rows(values, gain_row, shift_row):
    row_mean = jnp.mean(values, -1, keepdims=True)
    centered = values - row_mean
    variance = jnp.mean(centered * centered, -1, keepdims=True)
    return centered * lax.rsqrt(variance + norm_epsilon) * gain_row + shift_row


def product(former, latter):
    return jnp.dot(former, latter, preferred_element_type=jnp.float32)


def product_left(former, latter):
    return lax.dot_general(
        former, latter, (((0,), (0,)), ((), ())), preferred_element_type=jnp.float32
    )


def product_right(former, latter):
    return lax.dot_general(
        former, latter, (((1,), (1,)), ((), ())), preferred_element_type=jnp.float32
    )


def column_sums(values):
    return jnp.sum(values.astype(jnp.float32), 0)


def head_columns(index):
    return slice(index * HEAD_DIM, (index + 1) * HEAD_DIM)


def causal_rows(keys, queries):
    key_index = lax.broadcasted_iota(jnp.int32, (keys, queries), 0)
    query_index = lax.broadcasted_iota(jnp.int32, (keys, queries), 1)
    return key_index <= query_index


def of_head(values, head):
    if values.shape[1] == HEAD_DIM:
        return values
    column = lax.broadcasted_iota(jnp.int32, values.shape, 1)
    inside = (column >= head * HEAD_DIM) & (column < (head + 1) * HEAD_DIM)
    return jnp.where(inside, values, jnp.zeros_like(values))


def turn_head(source, start, width, head, out, tok):
    for row in range(0, source.shape[0], tok):
        block = jnp.transpose(source[row : row + tok, start : start + width])
        out[:, row : row + tok] = block[head_columns(head)]


def over_keys(slot, half, tok, step, first, keep):
    @pl.when(slot < half)
    def _():
        keep(
            lax.fori_loop(0, slot, lambda j, c: step(pl.multiple_of(j * tok, tok), tok, c), first)
        )

    @pl.when(slot >= half)
    def _():
        keep(step(0, half * tok, first))


def self_forward_kernel(tok, width, half, head, count, owner, slot_of, *refs):
    if count:
        blocks, (weight, bias, scale, qkv, mixed, total, value_t) = refs[:count], refs[count:]
    else:
        qkv, mixed, total, value_t = refs
    slot = pl.program_id(0)

    @pl.when(slot == 0)
    def _():
        if count:
            for index, block in enumerate(blocks):
                rows = (product(block[...], weight[...]) + bias[...]) * scale[...]
                start = pl.multiple_of(slot_of[index] * tok, tok)
                qkv[pl.ds(start, tok), :] = rows.astype(low_type)
        turn_head(qkv, 2 * width, width, head, value_t, tok)

    base = pl.multiple_of(slot * tok, tok)
    query_t = jnp.transpose(of_head(qkv[pl.ds(base, tok), :width], head))

    def step(start, seen, carry, causal=False):
        top, weight, mix = carry
        keys = qkv[pl.ds(start, seen), width : 2 * width]
        scores = product(keys, query_t)
        if causal:
            scores = jnp.where(causal_rows(seen, tok), scores, masked_score)
        new_top = jnp.maximum(top, jnp.max(scores, 0, keepdims=True))
        scale = jnp.exp(top - new_top)
        power = jnp.exp(scores - new_top)
        weight = weight * scale + jnp.sum(power, 0, keepdims=True)
        mix = mix * scale + product(value_t[:, pl.ds(start, seen)], power.astype(low_type))
        return (new_top, weight, mix)

    first = (
        jnp.full((1, tok), -1e30, jnp.float32),
        jnp.zeros((1, tok), jnp.float32),
        jnp.zeros((HEAD_DIM, tok), jnp.float32),
    )

    def keep(carry):
        top, weight, mix = step(base, tok, carry, True)
        mixed[...] = (mix / weight).astype(low_type)
        total[...] = top + jnp.log(weight)

    over_keys(slot, half, tok, step, first, keep)


def self_backward_kernel(tok, width, half, head, scale, count, owner, place, *refs):
    blocks, refs = refs[:count], refs[count:]
    before, refs = refs[:-12], refs[-12:]
    qkv, mixed_grad, mixed, total, out, slice_grad = refs[:6]
    key_t, key_sum, value_sum, rows, slice_sum, arrived = refs[6:]
    slot = pl.program_id(0)
    copies = [
        pltpu.make_async_copy(block, rows.at[i], arrived.at[i]) for i, block in enumerate(blocks)
    ]

    @pl.when(slot == 0)
    def _():
        for copy in copies:
            copy.start()
        turn_head(qkv, width, width, head, key_t, tok)
        key_sum[...] = jnp.zeros_like(key_sum)
        value_sum[...] = jnp.zeros_like(value_sum)

    base = pl.multiple_of(slot * tok, tok)
    query = of_head(qkv[pl.ds(base, tok), :width], head)
    query_t = jnp.transpose(query)
    narrow = mixed_grad[...]
    delta = jnp.sum(narrow.astype(jnp.float32) * mixed[...].astype(jnp.float32), 0, keepdims=True)
    empty = jnp.zeros_like(narrow)
    heads = width // HEAD_DIM
    grad_t = jnp.concatenate([narrow if h == head else empty for h in range(heads)], 0)
    grad = jnp.transpose(grad_t)

    def step(start, seen, carry, causal=False):
        keys = qkv[pl.ds(start, seen), width : 2 * width]
        values = qkv[pl.ds(start, seen), 2 * width :]
        power = jnp.exp(product(keys, query_t) - total[...])
        if causal:
            power = jnp.where(causal_rows(seen, tok), power, 0.0)
        slope = product(values, grad_t)
        score_grad = (power * (slope - delta)).astype(low_type)
        value_sum[pl.ds(start, seen), :] += product(power.astype(low_type), grad)
        key_sum[pl.ds(start, seen), :] += product(score_grad, query)
        return carry + product(key_t[:, pl.ds(start, seen)], score_grad)

    def keep(carry):
        query_grad = step(base, tok, carry, True).astype(low_type) * scale
        out[pl.ds(owner[slot], 1), :HEAD_DIM, :] = query_grad[None]

    over_keys(slot, half, tok, step, jnp.zeros((HEAD_DIM, tok), jnp.float32), keep)

    @pl.when(slot == pl.num_programs(0) - 1)
    def _():
        for copy in copies:
            copy.wait()
        slice_sum[...] = jnp.zeros_like(slice_sum)
        model = rows.shape[2]
        ones = jnp.ones((tok, LANES), low_type)

        def finish(p, carry):
            source = pl.ds(pl.multiple_of(p * tok, tok), tok)
            key_grad = jnp.transpose(key_sum[source, :])[head_columns(head)]
            value_grad = jnp.transpose(value_sum[source, :])[head_columns(head)]
            target = pl.ds(owner[p], 1)
            out[target, HEAD_DIM : 2 * HEAD_DIM, :] = key_grad.astype(low_type)[None]
            out[target, 2 * HEAD_DIM :, :] = value_grad.astype(low_type)[None]
            columns = out[target][0]
            slice_sum[:, :model] += product(columns, rows[pl.ds(place[p], 1)][0])
            slice_sum[:, model:] += product(columns, ones)
            return carry

        lax.fori_loop(0, pl.num_programs(0), finish, 0)
        if head < heads - 1:
            slice_grad[...] = slice_sum[...]
        else:
            kinds = [slice(k * HEAD_DIM, (k + 1) * HEAD_DIM) for k in range(3)]
            every = [part[kind, :] for kind in kinds for part in (*before, slice_sum)]
            slice_grad[...] = jnp.transpose(jnp.concatenate(every, 0))


def cross_forward_kernel(width, query, pair, mixed, total):
    keys, values = pair[0], jnp.transpose(pair[1])
    mixes = []
    for head in range(width // HEAD_DIM):
        cols = head_columns(head)
        scores = product_right(keys[:, cols], query[:, cols])
        top = jnp.max(scores, 0, keepdims=True)
        power = jnp.exp(scores - top)
        weight = jnp.sum(power, 0, keepdims=True)
        mixes.append(product(values[cols], power.astype(low_type)) / weight)
        total[head : head + 1, :] = top + jnp.log(weight)
    mixed[...] = jnp.transpose(jnp.concatenate(mixes, 0)).astype(low_type)


def cross_backward_kernel(width, scale, query, pair, mixed_grad, mixed, total, out, pair_grad):
    heads = width // HEAD_DIM
    keys, values = pair[0], pair[1]
    keys_t = jnp.transpose(keys)
    grad = mixed_grad[...]
    both = jnp.transpose(grad.astype(jnp.float32) * mixed[...].astype(jnp.float32))
    query_parts, key_parts, value_parts = [], [], []
    for head in range(heads):
        cols = head_columns(head)
        scores = product_right(keys[:, cols], query[:, cols])
        power = jnp.exp(scores - total[head : head + 1, :])
        slope = product_right(values[:, cols], grad[:, cols])
        delta = jnp.sum(both[cols], 0, keepdims=True)
        score_grad = (power * (slope - delta)).astype(low_type)
        value_parts.append(product(power.astype(low_type), grad[:, cols]))
        key_parts.append(product(score_grad, query[:, cols]))
        query_parts.append(product(keys_t[cols], score_grad))
    query_grad = jnp.transpose(jnp.concatenate(query_parts, 0)).astype(low_type)
    out[...] = query_grad * scale
    pair_grad[0] = jnp.concatenate(key_parts, 1).astype(low_type)
    pair_grad[1] = jnp.concatenate(value_parts, 1).astype(low_type)


declared = pl.CostEstimate(flops=2**20, transcendentals=0, bytes_accessed=2**16)


def kernel_options(megabytes):
    return pltpu.CompilerParams(
        dimension_semantics=("arbitrary",), vmem_limit_bytes=megabytes * 2**20
    )


def whole_block(shape):
    return pl.BlockSpec(shape, lambda *_: (0,) * len(shape), pipeline_mode=pl.Buffered(1))


def self_forward(head, owner, slot_of, tok, qkv, blocks=(), weight=None, bias=None, scale=None):
    make = qkv is None
    group = owner.shape[0]
    rows = group * tok
    width = (weight if make else qkv).shape[1] // 3
    inputs = (*blocks, weight, bias[None], scale[None]) if make else (qkv,)
    out_shape = [
        jax.ShapeDtypeStruct((group, HEAD_DIM, tok), low_type),
        jax.ShapeDtypeStruct((group, 1, tok), jnp.float32),
    ]
    out_specs = [
        pl.BlockSpec((None, HEAD_DIM, tok), lambda p, owner, _: (owner[p], 0, 0)),
        pl.BlockSpec((None, 1, tok), lambda p, *_: (p, 0, 0)),
    ]
    if make:
        out_shape = [jax.ShapeDtypeStruct((rows, 3 * width), low_type)] + out_shape
        out_specs = [pl.BlockSpec((rows, 3 * width), lambda *_: (0, 0))] + out_specs
    made = pl.pallas_call(
        functools.partial(
            self_forward_kernel, tok, width, group // 2, head, len(blocks)
        ),
        out_shape=out_shape,
        grid_spec=pltpu.PrefetchScalarGridSpec(
            num_scalar_prefetch=2,
            grid=(group,),
            in_specs=[whole_block(each.shape) for each in inputs],
            out_specs=out_specs,
            scratch_shapes=[pltpu.VMEM((HEAD_DIM, rows), low_type)],
        ),
        compiler_params=kernel_options(52),
        cost_estimate=declared,
        name="self_forward",
    )(owner, slot_of, *inputs)
    return made if make else [qkv, *made]


def self_backward(head, owner, place, blocks, before, qkv, mixed_grad, mixed, total):
    rows, width = qkv.shape[0], qkv.shape[1] // 3
    tok, model = blocks[0].shape
    group = rows // tok
    owned = pl.BlockSpec((None, HEAD_DIM, tok), lambda p, owner, _: (owner[p], 0, 0))
    slices = (3 * HEAD_DIM, model + LANES)
    if head == width // HEAD_DIM - 1:
        slices = (model + LANES, 3 * width)
    else:
        before = ()
    return pl.pallas_call(
        functools.partial(
            self_backward_kernel, tok, width, group // 2, head, HEAD_DIM ** (-0.5), group
        ),
        out_shape=(
            jax.ShapeDtypeStruct((group, 3 * HEAD_DIM, tok), low_type),
            jax.ShapeDtypeStruct(slices, jnp.float32),
        ),
        grid_spec=pltpu.PrefetchScalarGridSpec(
            num_scalar_prefetch=2,
            grid=(group,),
            in_specs=[pl.BlockSpec(memory_space=pl.ANY)] * group
            + [whole_block(each.shape) for each in before]
            + [
                whole_block(qkv.shape),
                owned,
                owned,
                pl.BlockSpec((None, 1, tok), lambda p, *_: (p, 0, 0)),
            ],
            out_specs=[
                pl.BlockSpec((group, 3 * HEAD_DIM, tok), lambda *_: (0, 0, 0)),
                pl.BlockSpec(slices, lambda *_: (0, 0)),
            ],
            scratch_shapes=[
                pltpu.VMEM((HEAD_DIM, rows), low_type),
                pltpu.VMEM((rows, width), jnp.float32),
                pltpu.VMEM((rows, width), jnp.float32),
                pltpu.VMEM((group, tok, model), low_type),
                pltpu.VMEM((3 * HEAD_DIM, model + LANES), jnp.float32),
                pltpu.SemaphoreType.DMA((group,)),
            ],
        ),
        compiler_params=kernel_options(52),
        cost_estimate=declared,
        name="self_backward",
    )(owner, place, *blocks, *before, qkv, mixed_grad, mixed, total)


def split_columns(values, group):
    rows = values.shape[0]
    return values.reshape(rows, group, -1).transpose(1, 0, 2)


def join_columns(values):
    return values.transpose(1, 0, 2).reshape(values.shape[1], -1)


def by_head(values, group):
    rows, width = values.shape[0], values.shape[1] // group
    if width % LANES == 0:
        return values, pl.BlockSpec((rows, width), lambda g: (0, g))
    return split_columns(values, group), pl.BlockSpec((None, rows, width), lambda g: (g, 0, 0))


def of_heads(values, group):
    return values if values.ndim == 2 else join_columns(values)


def cross_forward(queries, pairs):
    group, _, states, width = pairs.shape
    rows = queries.shape[0]
    queries, query_spec = by_head(queries, group)
    mixed, total = pl.pallas_call(
        functools.partial(cross_forward_kernel, width),
        out_shape=(
            jax.ShapeDtypeStruct(queries.shape, low_type),
            jax.ShapeDtypeStruct((group, 8, rows), jnp.float32),
        ),
        grid=(group,),
        in_specs=[query_spec, pl.BlockSpec((None, 2, states, width), lambda g: (g, 0, 0, 0))],
        out_specs=[query_spec, pl.BlockSpec((None, 8, rows), lambda g: (g, 0, 0))],
        compiler_params=kernel_options(32),
        cost_estimate=declared,
        name="cross_forward",
    )(queries, pairs)
    return of_heads(mixed, group), total


def cross_backward(queries, pairs, mixed_grad, mixed, total):
    group, _, states, width = pairs.shape
    rows = queries.shape[0]
    queries, spec = by_head(queries, group)
    mixed_grad, mixed = by_head(mixed_grad, group)[0], by_head(mixed, group)[0]
    pair_spec = pl.BlockSpec((None, 2, states, width), lambda g: (g, 0, 0, 0))
    query_grad, pair_grad = pl.pallas_call(
        functools.partial(cross_backward_kernel, width, HEAD_DIM ** (-0.5)),
        out_shape=(
            jax.ShapeDtypeStruct(queries.shape, low_type),
            jax.ShapeDtypeStruct(pairs.shape, low_type),
        ),
        grid=(group,),
        in_specs=[spec, pair_spec, spec, spec, pl.BlockSpec((None, 8, rows), lambda g: (g, 0, 0))],
        out_specs=[spec, pair_spec],
        compiler_params=kernel_options(32),
        cost_estimate=declared,
        name="cross_backward",
    )(queries, pairs, mixed_grad, mixed, total)
    return of_heads(query_grad, group), pair_grad


def swap(values, axis, offset):
    size = lax.axis_size(axis)
    return lax.ppermute(values, axis, [(i, i ^ offset) for i in range(size)])


def sum_over(values, steps):
    for axis, offset in steps:
        values = (
            values.astype(jnp.float32) + swap(values, axis, offset).astype(jnp.float32)
        ).astype(values.dtype)
    return values


def bits_of(axis):
    return [(axis, 1 << i) for i in range(lax.axis_size(axis).bit_length() - 1)]


def spread_over_rep(values):
    return [values] + [swap(values, "rep", d) for d in range(1, lax.axis_size("rep"))]


def double(values, offset):
    return jnp.concatenate([values, swap(values, "rep", offset)], 0)


def parts_of(values, axis):
    own = lax.axis_index("rep")
    return [
        lax.dynamic_index_in_dim(values, own ^ d, axis, keepdims=False)
        for d in range(values.shape[axis])
    ]


def rep_order(pieces):
    own = lax.axis_index("rep")
    count = len(pieces)
    return [lax.select_n(own, *[pieces[d ^ i] for i in range(count)]) for d in range(count)]


def trade_over_rep(pieces):
    return [pieces[0]] + [swap(pieces[d], "rep", d) for d in range(1, len(pieces))]


def far_terms(pieces):
    if len(pieces) != 4:
        return [swap(pieces[d], "rep", d) for d in range(len(pieces)) if d & (d - 1)]
    half = pieces[3].shape[0] // 2
    return [swap(pieces[3][:half], "rep", 1), swap(pieces[3][half:], "rep", 2)]


def near_terms(pieces, found):
    near = [1 << i for i in range(len(pieces).bit_length() - 1)]
    if len(pieces) != 4:
        return [swap(pieces[d], "rep", d) for d in near]
    half = pieces[3].shape[0] // 2
    one, two = pieces[1], pieces[2]
    one = jnp.concatenate([one[:half], sum_of([one[half:], found[1]]).astype(low_type)], 0)
    two = jnp.concatenate([sum_of([two[:half], found[0]]).astype(low_type), two[half:]], 0)
    return [swap(one, "rep", 1), swap(two, "rep", 2)]


def all_terms(pieces, found, near):
    return [pieces[0]] + near + (found if len(pieces) != 4 else [])


def sum_of(terms):
    return sum(term.astype(jnp.float32) for term in terms)


def trade_over_line(values):
    line, own = lax.axis_size("line"), lax.axis_index("line")
    terms = [lax.dynamic_index_in_dim(values, own, 0, keepdims=False)]
    for k in range(1, line):
        piece = lax.dynamic_index_in_dim(values, (own + k) % line, 0, keepdims=False)
        terms.append(lax.ppermute(piece, "line", [(i, (i + k) % line) for i in range(line)]))
    return terms


def two_rows(values):
    high = values.astype(low_type)
    return jnp.concatenate([high, (values - high.astype(jnp.float32)).astype(low_type)], -2)


def one_row(values):
    high, low = jnp.split(values.astype(jnp.float32), 2, -2)
    return high + low


def stage(values):
    return lax.optimization_barrier(values)


def shift(values):
    line = lax.axis_size("line")
    return lax.ppermute(values, "line", [(i, (i + 1) % line) for i in range(line)])


def gather_rows(values):
    return lax.all_gather(values, SHARD, axis=0, tiled=True)


def scatter_rows(values):
    return lax.psum_scatter(values, SHARD, scatter_dimension=0, tiled=True)


def exchange(values):
    return lax.all_to_all(values, SHARD, split_axis=0, concat_axis=0, tiled=True)


def gelu_and_slope(values):
    reduced = jnp.abs(values) * (0.5**0.5)
    inverse = 1.0 / (1.0 + 0.3275911 * reduced)
    bell = jnp.exp(-(reduced * reduced))
    tail = 1.061405429 * inverse - 1.453152027
    tail = tail * inverse + 1.421413741
    tail = tail * inverse - 0.284496736
    tail = (tail * inverse + 0.254829592) * inverse * bell * 0.5
    normal = jnp.where(values >= 0.0, 1.0 - tail, tail)
    return values * normal, normal + values * (bell * (0.5 / math.pi) ** 0.5)


def local(
    layer_input,
    encoder_states,
    out_grad,
    placement,
    w_self_qkv,
    w_self_out,
    w_cross_q,
    w_cross_kv,
    w_cross_out,
    w_fc1,
    w_fc2,
    proj_biases,
    fc1_bias,
    norm_gains,
    norm_shifts,
):
    reps, line = lax.axis_size("rep"), lax.axis_size("line")
    rep, core = lax.axis_index("rep"), lax.axis_index("core")
    group = 2 * line
    member = 2 * lax.axis_index("line") + core
    tok, model = layer_input.shape
    feed = w_fc1.shape[1]
    weight_rows = w_self_qkv.shape[0]
    width = model // group
    unit = feed // (group * reps)
    score_scale = HEAD_DIM ** (-0.5)
    slot_table = placement[0]
    device_ids = jnp.arange(group, dtype=jnp.int32)
    owners = jnp.sum(
        jnp.where(slot_table[None, :] == device_ids[:, None], device_ids[None, :], 0), 1
    )

    def own_columns(row):
        return lax.dynamic_slice(row, (member * width,), (width,))

    def in_columns(row):
        return lax.dynamic_update_slice(jnp.zeros((model,), jnp.float32), row, (member * width,))

    part_rows = weight_rows // reps
    slices = jnp.concatenate(
        [
            lax.dynamic_slice_in_dim(weight, rep * part_rows, part_rows, 0).reshape(
                part_rows, -1, group, width
            )
            for weight in (w_self_qkv, w_cross_kv)
        ],
        1,
    )
    slices = slices.transpose(2, 0, 1, 3).reshape(group, weight_rows // reps, 5 * width)
    first_cut = w_fc1.reshape(weight_rows, line, 2, reps, unit)
    first_cut = lax.dynamic_index_in_dim(first_cut, rep, 3, keepdims=False)
    first_own = lax.dynamic_index_in_dim(first_cut, core, 2, keepdims=False)
    first_other = lax.dynamic_index_in_dim(first_cut, 1 - core, 2, keepdims=False)
    first_own = first_own.reshape(weight_rows, line * unit)
    first_other = swap(first_other.reshape(weight_rows, line * unit), "core", 1)
    first_cut = jnp.where(
        core == 0,
        jnp.concatenate([first_own, first_other], 0),
        jnp.concatenate([first_other, first_own], 0),
    )
    second_cut = lax.dynamic_slice_in_dim(w_fc2, rep * unit, unit, 0)
    bias_cut = lax.dynamic_index_in_dim(
        fc1_bias.reshape(line, 2, reps, unit), core, 1, keepdims=False
    )
    bias_cut = [bias_cut[:, r].reshape(line * unit) for r in range(reps)]
    bias_cut = rep_order(bias_cut)

    square = jnp.stack([w_self_out, w_cross_q, w_cross_out], 0)
    square = square.reshape(3, reps, weight_rows // reps, model)
    square = lax.dynamic_index_in_dim(square, rep, 1, keepdims=False).reshape(-1, model)

    inputs = layer_input.astype(jnp.float32)
    zeros = jnp.zeros((width,), jnp.float32)
    head_bias = jnp.concatenate([own_columns(proj_biases[0]), zeros, own_columns(proj_biases[1])])
    head_scale = jnp.concatenate([jnp.full((width,), score_scale), jnp.ones((2 * width,))])
    cross_bias = jnp.concatenate([zeros, own_columns(proj_biases[4])])

    near = [1 << i for i in range(reps.bit_length() - 1)]
    far = [d for d in range(1, reps) if d not in near]
    slices = exchange(slices)
    blocks = [layer_input, swap(layer_input, "core", 1)]
    block = shift(layer_input)
    block, slices, blocks, first_cut, square, encoder_states, second_cut = stage(
        (block, slices, blocks, first_cut, square, encoder_states, second_cut)
    )

    both_cut = lax.all_gather(
        jnp.concatenate([second_cut, square], 0), "line", axis=0, tiled=True
    ).reshape(line, -1, model)
    blocks += [block, swap(block, "core", 1)]
    block = shift(block)
    slices = spread_over_rep(slices)
    block, slices, blocks, encoder_states = stage((block, slices, blocks, encoder_states))

    for step in range(line - 3):
        blocks += [block, swap(block, "core", 1)]
        block = shift(block)
    slices = jnp.stack(rep_order(slices), 1).reshape(model, 5 * width)
    head_qkv, head_ckv = slices[:, : 3 * width], slices[:, 3 * width :]
    all_states = gather_rows(encoder_states)
    block, blocks, both_cut, head_qkv, head_ckv, all_states, first_cut = stage(
        (block, blocks, both_cut, head_qkv, head_ckv, all_states, first_cut)
    )

    blocks += [block, swap(block, "core", 1)]
    square = spread_over_rep(both_cut[:, unit:])
    wfirst = {0: lax.all_gather(first_cut, "line", axis=0, tiled=True)}
    head_pair = (product(all_states, head_ckv) + cross_bias).astype(low_type)
    head_pair = split_columns(head_pair, 2)
    wsecond = {0: both_cut[:, :unit].reshape(line * unit, model)}
    back = (lax.axis_index("line") - owners // 2) % line
    places = 2 * back + ((owners % 2) ^ core)
    slot_of = jnp.sum(
        jnp.where(places[None, :] == device_ids[:, None], device_ids[None, :], 0), 1
    )
    heads = width // HEAD_DIM
    made, turn, self_totals, self_mixed, self_low = None, owners, [], [], []
    for head in range(heads):
        extra = () if head else (blocks, head_qkv, head_bias, head_scale)
        made, mixed, total = self_forward(head, turn, slot_of, tok, made, *extra)
        self_totals.append(total)
        if head == 0:
            mixed, turn, square, head_pair = stage((mixed, turn, square, head_pair))
            wsecond.update({d: swap(wsecond[0], "rep", d) for d in near})
            square = jnp.stack(rep_order(square), 1)
            square_other = swap(square, "core", 1)
        if head == heads - 1:
            held = (mixed, wfirst, square, square_other)
            held, wsecond, self_low = stage((held, wsecond, self_low))
            mixed, wfirst, square, square_other = held
            wsecond.update({d: swap(wsecond[0], "rep", d) for d in far})
            wfirst.update({d: swap(wfirst[0], "rep", d) for d in near})
        self_mixed.append(mixed)
        self_low.append(exchange(mixed))
    qkv = made
    square = jnp.where(
        core == 0, jnp.stack([square, square_other], 1), jnp.stack([square_other, square], 1)
    )
    square = square.reshape(line, 2, reps, 3, weight_rows // reps, model)
    full_out, full_cross_q, full_cross_out = [
        square[:, :, :, i].reshape(model, model) for i in range(3)
    ]
    pairs = lax.all_gather(head_pair, SHARD, axis=0, tiled=False)
    self_low, pairs = stage((self_low, pairs))
    self_low = jnp.stack(self_low, 1).reshape(model, tok)

    first_sum = inputs + (product_left(self_low, full_out) + proj_biases[2])
    first_norm, norm1_back = jax.vjp(norm_rows, first_sum, norm_gains[0], norm_shifts[0])
    first_low = first_norm.astype(low_type)
    cross_queries = ((product(first_low, full_cross_q) + proj_biases[3]) * score_scale).astype(
        low_type
    )
    cross_low, cross_total = cross_forward(cross_queries, pairs)
    cross_low, wfirst, wsecond = stage((cross_low, wfirst, wsecond))
    wfirst.update({d: swap(wfirst[0], "rep", d) for d in far})
    second_sum = first_norm + (product(cross_low, full_cross_out) + proj_biases[5])
    second_norm, norm2_back = jax.vjp(norm_rows, second_sum, norm_gains[1], norm_shifts[1])
    second_low = second_norm.astype(low_type)

    turned = jnp.transpose(stage((head_qkv, second_low))[0])
    turned = turned.reshape(3, heads, HEAD_DIM, model).transpose(1, 0, 2, 3)
    turned = gather_rows(turned.reshape(-1, model))
    turned = turned.reshape(group, heads, 3 * HEAD_DIM, model)

    second_both = jnp.concatenate([second_low, swap(second_low, "core", 1)], 0)
    feed_sum, hidden, slopes = 0.0, [], []
    for part in range(reps):
        active, slope = gelu_and_slope(product(second_both, wfirst[part]) + bias_cut[part])
        hidden.append(active.astype(low_type))
        slopes.append(slope)
        feed_sum = feed_sum + product(hidden[part], wsecond[part])
    feed_other = swap(feed_sum[tok:].astype(low_type), "core", 1).astype(jnp.float32)
    third_sum = second_norm + (feed_sum[:tok] + feed_other + proj_biases[6])
    result, norm3_back = jax.vjp(norm_rows, third_sum, norm_gains[2], norm_shifts[2])
    output = result.astype(low_type)

    third_grad, gain_three, shift_three = norm3_back(out_grad.astype(jnp.float32))
    feed_grad = third_grad.astype(low_type)
    bias_fc2 = column_sums(feed_grad)
    feed_both = jnp.concatenate([feed_grad, swap(feed_grad, "core", 1)], 0)
    second_parts = [
        product_left(hidden[part], feed_both).astype(low_type) for part in range(reps)
    ]
    feed_both, second_parts = stage((feed_both, second_parts))
    second_found = far_terms(second_parts)
    back_sum, first_parts, bias_parts = 0.0, [], []
    for part in range(reps):
        pre_grad = (product_right(feed_both, wsecond[part]) * slopes[part]).astype(low_type)
        first_parts.append(product_left(second_both, pre_grad).astype(low_type))
        bias_parts.append(column_sums(pre_grad))
        back_sum = back_sum + product_right(pre_grad, wfirst[part])
        if part == reps // 2 - 1:
            feed_both, back_sum, second_found = stage((feed_both, back_sum, second_found))
            second_near = near_terms(second_parts, second_found)
    back_sum, second_near, first_parts = stage((back_sum, second_near, first_parts))
    second_sums = sum_of(all_terms(second_parts, second_found, second_near)).astype(low_type)
    back_other = swap(back_sum[tok:].astype(low_type), "core", 1).astype(jnp.float32)
    second_grad, gain_two, shift_two = norm2_back(third_grad + (back_sum[:tok] + back_other))
    second_grad, second_sums, first_parts = stage((second_grad, second_sums, first_parts))
    second_sums = lax.psum_scatter(second_sums, "line", scatter_dimension=0, tiled=True)
    first_found = far_terms(first_parts)

    cross_out_grad = second_grad.astype(low_type)
    cross_mixed_grad = product_right(cross_out_grad, full_cross_out).astype(low_type)
    cross_q_grad, pair_grad = cross_backward(
        cross_queries, pairs, cross_mixed_grad, cross_low, cross_total
    )
    cross_q_grad, pair_grad, first_found, turned = stage(
        (cross_q_grad, pair_grad, first_found, turned)
    )
    first_near = near_terms(first_parts, first_found)
    own_pair_grad = lax.psum_scatter(pair_grad, SHARD, scatter_dimension=0, tiled=False)
    first_grad, gain_one, shift_one = norm1_back(
        second_grad + product_right(cross_q_grad, full_cross_q)
    )
    self_out_grad = first_grad.astype(low_type)
    mixed_grad = product_right(full_out, self_out_grad).astype(low_type)
    mixed_grad = mixed_grad.reshape(group, heads, HEAD_DIM, tok)
    held = (self_low, first_low, cross_low, self_out_grad, cross_q_grad, cross_out_grad)
    mixed_grad, held = stage((mixed_grad, held))
    self_low, first_low, cross_low, self_out_grad, cross_q_grad, cross_out_grad = held
    mixed_grad = [exchange(mixed_grad[:, head]) for head in range(heads)]
    part_self_out = product(self_low, self_out_grad).astype(low_type)
    part_cross_q = product_left(first_low, cross_q_grad).astype(low_type)
    part_cross_out = product_left(cross_low, cross_out_grad).astype(low_type)
    bias_self_out = column_sums(self_out_grad)
    bias_cross_q = column_sums(cross_q_grad)
    bias_cross_out = column_sums(cross_out_grad)

    square = jnp.stack([part_self_out, part_cross_q, part_cross_out], 0)
    square = square.reshape(3, line, 2, reps, weight_rows // reps, model)
    square_own = lax.dynamic_index_in_dim(square, core, 2, keepdims=False)
    square_other = swap(lax.dynamic_index_in_dim(square, 1 - core, 2, keepdims=False), "core", 1)

    bias_parts = jnp.stack([part.reshape(line, unit) for part in rep_order(bias_parts)], 1)
    bias_fc1 = jnp.where(
        jnp.arange(2)[None, :, None, None] == core, bias_parts[:, None], 0.0
    ).reshape(feed)
    small = jnp.concatenate(
        [
            jnp.stack(
                [
                    bias_self_out,
                    bias_cross_q,
                    bias_cross_out,
                    bias_fc2,
                    gain_one,
                    gain_two,
                    gain_three,
                    shift_one,
                    shift_two,
                    shift_three,
                ],
                0,
            ),
            bias_fc1.reshape(-1, model),
        ],
        0,
    )
    hops = bits_of("core") + bits_of("rep") + bits_of("line")

    def hop(values, count):
        for _ in range(count):
            values = values + swap(values, *hops.pop(0))
        return values

    small = hop(small, 1)
    square = square_own.astype(jnp.float32) + square_other.astype(jnp.float32)
    square = square.astype(low_type).transpose(2, 1, 0, 3, 4)
    square = parts_of(square, 0)
    held = (square, small, second_sums, first_near)
    mixed_grad[0], held = stage((mixed_grad[0], held))
    square, small, second_sums, first_near = held
    first_sums = sum_of(all_terms(first_parts, first_found, first_near)).astype(low_type)
    first_sums = lax.psum_scatter(first_sums, "line", scatter_dimension=0, tiled=True)
    square_terms = trade_over_rep(square)
    wide = 2 * line * unit
    second_sums = second_sums.reshape(unit, model // wide, wide).transpose(1, 0, 2)
    second_sums = double(second_sums.reshape(1, -1, wide), near[0])
    turn = owners

    part_rows = weight_rows // reps

    def with_sums(values, sums):
        rows = two_rows(jnp.broadcast_to(sums, sums.shape[:-2] + (8,) + sums.shape[-1:]))
        return jnp.concatenate([values.astype(low_type), rows], -2)

    def split_sums(values):
        return values[..., :part_rows, :], one_row(values[..., part_rows:, :])[..., :1, :]

    def trade_slices(values):
        columns = values.shape[1]
        sums = two_rows(jnp.broadcast_to(values[model : model + 1], (8, columns)))
        values = values[:model].reshape(group, reps, part_rows, columns).astype(low_type)
        return trade_over_rep(
            [
                jnp.concatenate([part.reshape(-1, columns), sums], 0)
                for part in parts_of(values, 1)
            ]
        )

    def exchange_slices(terms):
        values = sum_of(terms)
        sums = one_row(values[group * part_rows :])[:1]
        sums = jnp.broadcast_to(sums, (group,) + sums.shape)
        values = values[: group * part_rows].reshape(group, part_rows, -1)
        return exchange(with_sums(values, sums))

    def join_slices(values):
        values, sums = split_sums(values.astype(jnp.float32))
        values = jnp.stack(rep_order(spread_over_rep(values.astype(low_type))), 0)
        values = values.transpose(0, 2, 1, 3).reshape(weight_rows, group, -1)
        return values, sums[:, 0][None]

    parts, slice_parts = [], []
    for head in range(heads):
        part, slice_part = self_backward(
            head,
            turn,
            places,
            blocks,
            slice_parts,
            qkv,
            mixed_grad[head],
            self_mixed[head],
            self_totals[head],
        )
        if head == 0:
            small = hop(small, 1)
            held = (part, slice_part, turn, first_sums, second_sums, square_terms, small)
            held, mixed_grad, own_pair_grad = stage((held, mixed_grad, own_pair_grad))
            part, slice_part, turn, first_sums, second_sums, square_terms, small = held
            own_pair_grad = join_columns(own_pair_grad)
            for offset in near[1:]:
                second_sums = double(second_sums, offset)
            first_sums = first_sums.reshape(2, weight_rows, line * unit).transpose(1, 0, 2)
            first_sums = double(first_sums.reshape(1, -1, wide), near[0])
            pair_sums = jnp.sum(own_pair_grad.astype(jnp.float32), 0)
            pair_sums = jnp.broadcast_to(pair_sums, (LANES, 2 * width))
            pair_slices = jnp.concatenate([product_left(all_states, own_pair_grad), pair_sums], 0)
            square_terms = trade_over_line(sum_of(square_terms).astype(low_type))
        if head == heads - 1:
            held = (part, slice_part, first_sums, second_sums, square_terms)
            held, parts, slice_parts = stage((held, parts, slice_parts))
            part, slice_part, first_sums, second_sums, square_terms = held
        parts.append(exchange(part))
        slice_parts.append(slice_part)

    slice_parts = trade_slices(jnp.concatenate([slice_parts[-1], pair_slices], 1))
    for offset in near[1:]:
        first_sums = double(first_sums, offset)
    square = double(sum_of(square_terms).astype(low_type)[None], near[0])
    small = hop(small, 1)
    enc_terms = product_right(own_pair_grad, head_ckv).astype(low_type)
    held = (first_sums, square, small, enc_terms)
    parts, slice_parts, held = stage((parts, slice_parts, held))
    first_sums, square, small, enc_terms = held
    enc_grad = scatter_rows(enc_terms)

    slice_parts = exchange_slices(slice_parts)
    for offset in near[1:]:
        square = double(square, offset)
    small = hop(small, 1)
    second_sums = jnp.stack(rep_order([second_sums[d] for d in range(reps)]), 0)
    second_sums = second_sums.reshape(reps, model // wide, unit, wide)
    grad_fc2 = second_sums.transpose(0, 2, 1, 3).reshape(-1, model).astype(jnp.float32)
    first_sums = jnp.stack(rep_order([first_sums[d] for d in range(reps)]), 0)
    first_sums = first_sums.reshape(reps, weight_rows, 2, line, unit)
    first_own = lax.dynamic_index_in_dim(first_sums, core, 2, keepdims=False)
    first_other = lax.dynamic_index_in_dim(first_sums, 1 - core, 2, keepdims=False)
    first_other = swap(first_other.reshape(-1, line * unit), "core", 1)
    first_other = first_other.reshape(first_own.shape)
    input_grad = first_grad
    rows = turned.reshape(-1, model)
    input_grad = input_grad + product_left(jnp.stack(parts, 1).reshape(rows.shape[0], tok), rows)
    held = (first_own, first_other, square, input_grad, grad_fc2, small)
    slice_parts, held = stage((slice_parts, held))
    first_own, first_other, square, input_grad, grad_fc2, small = held

    slice_parts = join_slices(slice_parts)
    small = hop(small, len(hops))
    square = jnp.stack(rep_order([square[d] for d in range(reps)]), 1).astype(jnp.float32)
    grad_self_out, grad_cross_q, grad_cross_out = [
        square[i].reshape(weight_rows, model) for i in range(3)
    ]
    grad_fc1 = jnp.where(
        core == 0, jnp.stack([first_own, first_other], 0), jnp.stack([first_other, first_own], 0)
    )
    grad_fc1 = grad_fc1.transpose(2, 3, 0, 1, 4).reshape(weight_rows, feed).astype(jnp.float32)

    def of_self(values):
        values = values[..., : 3 * width].reshape(-1, group, 3, width)
        return values.transpose(0, 2, 1, 3).reshape(-1, 3, model)

    def of_cross(values):
        values = values[..., 3 * width :].reshape(-1, group, 2, width)
        return values.transpose(0, 2, 1, 3).reshape(-1, 2, model)

    grad_self_qkv = of_self(slice_parts[0].astype(jnp.float32)).reshape(weight_rows, 3 * model)
    grad_cross_kv = of_cross(slice_parts[0].astype(jnp.float32)).reshape(weight_rows, 2 * model)
    bias_self, bias_cross_v = of_self(slice_parts[1]), of_cross(slice_parts[1])[0, 1]
    grad_biases = jnp.stack(
        [
            bias_self[0, 0],
            bias_self[0, 2],
            small[0],
            small[1],
            bias_cross_v,
            small[2],
            small[3],
        ],
        0,
    )
    return (
        output,
        input_grad,
        enc_grad.astype(jnp.float32),
        grad_self_qkv,
        grad_self_out,
        grad_cross_q,
        grad_cross_kv,
        grad_cross_out,
        grad_fc1,
        grad_fc2,
        grad_biases,
        small[10:].reshape(-1),
        small[4:7],
        small[7:10],
    )


def solution(mesh):
    reps, group = mesh.devices.shape
    split = jax.sharding.Mesh(
        mesh.devices.reshape(reps, group // 2, 2), ("rep",) + SHARD
    )
    rows, cut = P(("rep",) + SHARD, None), P(SHARD, None)
    return jax.shard_map(
        local,
        mesh=split,
        in_specs=(rows,) * 3 + (P("rep", None),) + (cut,) * 7 + (P(),) * 4,
        out_specs=(rows,) * 3 + (cut,) * 7 + (P(),) * 4,
        check_vma=False,
    )
```

```python
import functools
import math

import jax
import jax.numpy as jnp
from jax import lax
from jax.experimental import pallas as pl
from jax.experimental.pallas import tpu as pltpu
from jax.sharding import PartitionSpec as P

HEADS = 16
HEAD_DIM = 64
LANES = 128

masked_score = -1000000000.0
norm_epsilon = 1e-05
low_type = jnp.bfloat16
SHARD = ("line", "core")


def norm_rows(values, gain_row, shift_row):
    row_mean = jnp.mean(values, -1, keepdims=True)
    centered = values - row_mean
    variance = jnp.mean(centered * centered, -1, keepdims=True)
    return centered * lax.rsqrt(variance + norm_epsilon) * gain_row + shift_row


def product(former, latter):
    return jnp.dot(former, latter, preferred_element_type=jnp.float32)


def product_left(former, latter):
    return lax.dot_general(
        former, latter, (((0,), (0,)), ((), ())), preferred_element_type=jnp.float32
    )


def product_right(former, latter):
    return lax.dot_general(
        former, latter, (((1,), (1,)), ((), ())), preferred_element_type=jnp.float32
    )


def column_sums(values):
    return jnp.sum(values.astype(jnp.float32), 0)


def head_columns(index):
    return slice(index * HEAD_DIM, (index + 1) * HEAD_DIM)


def causal_rows(keys, queries):
    key_index = lax.broadcasted_iota(jnp.int32, (keys, queries), 0)
    query_index = lax.broadcasted_iota(jnp.int32, (keys, queries), 1)
    return key_index <= query_index


def of_head(values, head):
    if values.shape[1] == HEAD_DIM:
        return values
    column = lax.broadcasted_iota(jnp.int32, values.shape, 1)
    inside = (column >= head * HEAD_DIM) & (column < (head + 1) * HEAD_DIM)
    return jnp.where(inside, values, jnp.zeros_like(values))


def turn_head(source, start, width, head, out, tok):
    for row in range(0, source.shape[0], tok):
        block = jnp.transpose(source[row : row + tok, start : start + width])
        out[:, row : row + tok] = block[head_columns(head)]


def over_keys(slot, half, tok, step, first, keep):
    @pl.when(slot < half)
    def _():
        keep(
            lax.fori_loop(0, slot, lambda j, c: step(pl.multiple_of(j * tok, tok), tok, c), first)
        )

    @pl.when(slot >= half)
    def _():
        keep(step(0, half * tok, first))


def self_forward_kernel(tok, width, half, head, count, owner, slot_of, *refs):
    if count:
        blocks, (weight, bias, scale, qkv, mixed, total, value_t) = refs[:count], refs[count:]
    else:
        qkv, mixed, total, value_t = refs
    slot = pl.program_id(0)

    @pl.when(slot == 0)
    def _():
        if count:
            for index, block in enumerate(blocks):
                rows = (product(block[...], weight[...]) + bias[...]) * scale[...]
                start = pl.multiple_of(slot_of[index] * tok, tok)
                qkv[pl.ds(start, tok), :] = rows.astype(low_type)
        turn_head(qkv, 2 * width, width, head, value_t, tok)

    base = pl.multiple_of(slot * tok, tok)
    query_t = jnp.transpose(of_head(qkv[pl.ds(base, tok), :width], head))

    def step(start, seen, carry, causal=False):
        top, weight, mix = carry
        keys = qkv[pl.ds(start, seen), width : 2 * width]
        scores = product(keys, query_t)
        if causal:
            scores = jnp.where(causal_rows(seen, tok), scores, masked_score)
        new_top = jnp.maximum(top, jnp.max(scores, 0, keepdims=True))
        scale = jnp.exp(top - new_top)
        power = jnp.exp(scores - new_top)
        weight = weight * scale + jnp.sum(power, 0, keepdims=True)
        mix = mix * scale + product(value_t[:, pl.ds(start, seen)], power.astype(low_type))
        return (new_top, weight, mix)

    first = (
        jnp.full((1, tok), -1e30, jnp.float32),
        jnp.zeros((1, tok), jnp.float32),
        jnp.zeros((HEAD_DIM, tok), jnp.float32),
    )

    def keep(carry):
        top, weight, mix = step(base, tok, carry, True)
        mixed[...] = (mix / weight).astype(low_type)
        total[...] = top + jnp.log(weight)

    over_keys(slot, half, tok, step, first, keep)


def self_backward_kernel(tok, width, half, head, scale, count, owner, place, *refs):
    blocks, refs = refs[:count], refs[count:]
    before, refs = refs[:-12], refs[-12:]
    qkv, mixed_grad, mixed, total, out, slice_grad = refs[:6]
    key_t, key_sum, value_sum, rows, slice_sum, arrived = refs[6:]
    slot = pl.program_id(0)
    copies = [
        pltpu.make_async_copy(block, rows.at[i], arrived.at[i]) for i, block in enumerate(blocks)
    ]

    @pl.when(slot == 0)
    def _():
        for copy in copies:
            copy.start()
        turn_head(qkv, width, width, head, key_t, tok)
        key_sum[...] = jnp.zeros_like(key_sum)
        value_sum[...] = jnp.zeros_like(value_sum)

    base = pl.multiple_of(slot * tok, tok)
    query = of_head(qkv[pl.ds(base, tok), :width], head)
    query_t = jnp.transpose(query)
    narrow = mixed_grad[...]
    delta = jnp.sum(narrow.astype(jnp.float32) * mixed[...].astype(jnp.float32), 0, keepdims=True)
    empty = jnp.zeros_like(narrow)
    heads = width // HEAD_DIM
    grad_t = jnp.concatenate([narrow if h == head else empty for h in range(heads)], 0)
    grad = jnp.transpose(grad_t)

    def step(start, seen, carry, causal=False):
        keys = qkv[pl.ds(start, seen), width : 2 * width]
        values = qkv[pl.ds(start, seen), 2 * width :]
        power = jnp.exp(product(keys, query_t) - total[...])
        if causal:
            power = jnp.where(causal_rows(seen, tok), power, 0.0)
        slope = product(values, grad_t)
        score_grad = (power * (slope - delta)).astype(low_type)
        value_sum[pl.ds(start, seen), :] += product(power.astype(low_type), grad)
        key_sum[pl.ds(start, seen), :] += product(score_grad, query)
        return carry + product(key_t[:, pl.ds(start, seen)], score_grad)

    def keep(carry):
        query_grad = step(base, tok, carry, True).astype(low_type) * scale
        out[pl.ds(owner[slot], 1), :HEAD_DIM, :] = query_grad[None]

    over_keys(slot, half, tok, step, jnp.zeros((HEAD_DIM, tok), jnp.float32), keep)

    @pl.when(slot == pl.num_programs(0) - 1)
    def _():
        for copy in copies:
            copy.wait()
        slice_sum[...] = jnp.zeros_like(slice_sum)
        model = rows.shape[2]
        ones = jnp.ones((tok, LANES), low_type)

        def finish(p, carry):
            source = pl.ds(pl.multiple_of(p * tok, tok), tok)
            key_grad = jnp.transpose(key_sum[source, :])[head_columns(head)]
            value_grad = jnp.transpose(value_sum[source, :])[head_columns(head)]
            target = pl.ds(owner[p], 1)
            out[target, HEAD_DIM : 2 * HEAD_DIM, :] = key_grad.astype(low_type)[None]
            out[target, 2 * HEAD_DIM :, :] = value_grad.astype(low_type)[None]
            columns = out[target][0]
            slice_sum[:, :model] += product(columns, rows[pl.ds(place[p], 1)][0])
            slice_sum[:, model:] += product(columns, ones)
            return carry

        lax.fori_loop(0, pl.num_programs(0), finish, 0)
        if head < heads - 1:
            slice_grad[...] = slice_sum[...]
        else:
            kinds = [slice(k * HEAD_DIM, (k + 1) * HEAD_DIM) for k in range(3)]
            every = [part[kind, :] for kind in kinds for part in (*before, slice_sum)]
            slice_grad[...] = jnp.transpose(jnp.concatenate(every, 0))


def cross_forward_kernel(width, query, pair, mixed, total):
    keys, values = pair[0], jnp.transpose(pair[1])
    mixes = []
    for head in range(width // HEAD_DIM):
        cols = head_columns(head)
        scores = product_right(keys[:, cols], query[:, cols])
        top = jnp.max(scores, 0, keepdims=True)
        power = jnp.exp(scores - top)
        weight = jnp.sum(power, 0, keepdims=True)
        mixes.append(product(values[cols], power.astype(low_type)) / weight)
        total[head : head + 1, :] = top + jnp.log(weight)
    mixed[...] = jnp.transpose(jnp.concatenate(mixes, 0)).astype(low_type)


def cross_backward_kernel(width, scale, query, pair, mixed_grad, mixed, total, out, pair_grad):
    heads = width // HEAD_DIM
    keys, values = pair[0], pair[1]
    keys_t = jnp.transpose(keys)
    grad = mixed_grad[...]
    both = jnp.transpose(grad.astype(jnp.float32) * mixed[...].astype(jnp.float32))
    query_parts, key_parts, value_parts = [], [], []
    for head in range(heads):
        cols = head_columns(head)
        scores = product_right(keys[:, cols], query[:, cols])
        power = jnp.exp(scores - total[head : head + 1, :])
        slope = product_right(values[:, cols], grad[:, cols])
        delta = jnp.sum(both[cols], 0, keepdims=True)
        score_grad = (power * (slope - delta)).astype(low_type)
        value_parts.append(product(power.astype(low_type), grad[:, cols]))
        key_parts.append(product(score_grad, query[:, cols]))
        query_parts.append(product(keys_t[cols], score_grad))
    query_grad = jnp.transpose(jnp.concatenate(query_parts, 0)).astype(low_type)
    out[...] = query_grad * scale
    pair_grad[0] = jnp.concatenate(key_parts, 1).astype(low_type)
    pair_grad[1] = jnp.concatenate(value_parts, 1).astype(low_type)


declared = pl.CostEstimate(flops=2**20, transcendentals=0, bytes_accessed=2**16)


def kernel_options(megabytes):
    return pltpu.CompilerParams(
        dimension_semantics=("arbitrary",), vmem_limit_bytes=megabytes * 2**20
    )


def whole_block(shape):
    return pl.BlockSpec(shape, lambda *_: (0,) * len(shape), pipeline_mode=pl.Buffered(1))


def self_forward(head, owner, slot_of, tok, qkv, blocks=(), weight=None, bias=None, scale=None):
    make = qkv is None
    group = owner.shape[0]
    rows = group * tok
    width = (weight if make else qkv).shape[1] // 3
    inputs = (*blocks, weight, bias[None], scale[None]) if make else (qkv,)
    out_shape = [
        jax.ShapeDtypeStruct((group, HEAD_DIM, tok), low_type),
        jax.ShapeDtypeStruct((group, 1, tok), jnp.float32),
    ]
    out_specs = [
        pl.BlockSpec((None, HEAD_DIM, tok), lambda p, owner, _: (owner[p], 0, 0)),
        pl.BlockSpec((None, 1, tok), lambda p, *_: (p, 0, 0)),
    ]
    if make:
        out_shape = [jax.ShapeDtypeStruct((rows, 3 * width), low_type)] + out_shape
        out_specs = [pl.BlockSpec((rows, 3 * width), lambda *_: (0, 0))] + out_specs
    made = pl.pallas_call(
        functools.partial(
            self_forward_kernel, tok, width, group // 2, head, len(blocks)
        ),
        out_shape=out_shape,
        grid_spec=pltpu.PrefetchScalarGridSpec(
            num_scalar_prefetch=2,
            grid=(group,),
            in_specs=[whole_block(each.shape) for each in inputs],
            out_specs=out_specs,
            scratch_shapes=[pltpu.VMEM((HEAD_DIM, rows), low_type)],
        ),
        compiler_params=kernel_options(52),
        cost_estimate=declared,
        name="self_forward",
    )(owner, slot_of, *inputs)
    return made if make else [qkv, *made]


def self_backward(head, owner, place, blocks, before, qkv, mixed_grad, mixed, total):
    rows, width = qkv.shape[0], qkv.shape[1] // 3
    tok, model = blocks[0].shape
    group = rows // tok
    owned = pl.BlockSpec((None, HEAD_DIM, tok), lambda p, owner, _: (owner[p], 0, 0))
    slices = (3 * HEAD_DIM, model + LANES)
    if head == width // HEAD_DIM - 1:
        slices = (model + LANES, 3 * width)
    else:
        before = ()
    return pl.pallas_call(
        functools.partial(
            self_backward_kernel, tok, width, group // 2, head, HEAD_DIM ** (-0.5), group
        ),
        out_shape=(
            jax.ShapeDtypeStruct((group, 3 * HEAD_DIM, tok), low_type),
            jax.ShapeDtypeStruct(slices, jnp.float32),
        ),
        grid_spec=pltpu.PrefetchScalarGridSpec(
            num_scalar_prefetch=2,
            grid=(group,),
            in_specs=[pl.BlockSpec(memory_space=pl.ANY)] * group
            + [whole_block(each.shape) for each in before]
            + [
                whole_block(qkv.shape),
                owned,
                owned,
                pl.BlockSpec((None, 1, tok), lambda p, *_: (p, 0, 0)),
            ],
            out_specs=[
                pl.BlockSpec((group, 3 * HEAD_DIM, tok), lambda *_: (0, 0, 0)),
                pl.BlockSpec(slices, lambda *_: (0, 0)),
            ],
            scratch_shapes=[
                pltpu.VMEM((HEAD_DIM, rows), low_type),
                pltpu.VMEM((rows, width), jnp.float32),
                pltpu.VMEM((rows, width), jnp.float32),
                pltpu.VMEM((group, tok, model), low_type),
                pltpu.VMEM((3 * HEAD_DIM, model + LANES), jnp.float32),
                pltpu.SemaphoreType.DMA((group,)),
            ],
        ),
        compiler_params=kernel_options(52),
        cost_estimate=declared,
        name="self_backward",
    )(owner, place, *blocks, *before, qkv, mixed_grad, mixed, total)


def split_columns(values, group):
    rows = values.shape[0]
    return values.reshape(rows, group, -1).transpose(1, 0, 2)


def join_columns(values):
    return values.transpose(1, 0, 2).reshape(values.shape[1], -1)


def by_head(values, group):
    rows, width = values.shape[0], values.shape[1] // group
    if width % LANES == 0:
        return values, pl.BlockSpec((rows, width), lambda g: (0, g))
    return split_columns(values, group), pl.BlockSpec((None, rows, width), lambda g: (g, 0, 0))


def of_heads(values, group):
    return values if values.ndim == 2 else join_columns(values)


def cross_forward(queries, pairs):
    group, _, states, width = pairs.shape
    rows = queries.shape[0]
    queries, query_spec = by_head(queries, group)
    mixed, total = pl.pallas_call(
        functools.partial(cross_forward_kernel, width),
        out_shape=(
            jax.ShapeDtypeStruct(queries.shape, low_type),
            jax.ShapeDtypeStruct((group, 8, rows), jnp.float32),
        ),
        grid=(group,),
        in_specs=[query_spec, pl.BlockSpec((None, 2, states, width), lambda g: (g, 0, 0, 0))],
        out_specs=[query_spec, pl.BlockSpec((None, 8, rows), lambda g: (g, 0, 0))],
        compiler_params=kernel_options(32),
        cost_estimate=declared,
        name="cross_forward",
    )(queries, pairs)
    return of_heads(mixed, group), total


def cross_backward(queries, pairs, mixed_grad, mixed, total):
    group, _, states, width = pairs.shape
    rows = queries.shape[0]
    queries, spec = by_head(queries, group)
    mixed_grad, mixed = by_head(mixed_grad, group)[0], by_head(mixed, group)[0]
    pair_spec = pl.BlockSpec((None, 2, states, width), lambda g: (g, 0, 0, 0))
    query_grad, pair_grad = pl.pallas_call(
        functools.partial(cross_backward_kernel, width, HEAD_DIM ** (-0.5)),
        out_shape=(
            jax.ShapeDtypeStruct(queries.shape, low_type),
            jax.ShapeDtypeStruct(pairs.shape, low_type),
        ),
        grid=(group,),
        in_specs=[spec, pair_spec, spec, spec, pl.BlockSpec((None, 8, rows), lambda g: (g, 0, 0))],
        out_specs=[spec, pair_spec],
        compiler_params=kernel_options(32),
        cost_estimate=declared,
        name="cross_backward",
    )(queries, pairs, mixed_grad, mixed, total)
    return of_heads(query_grad, group), pair_grad


def swap(values, axis, offset):
    size = lax.axis_size(axis)
    return lax.ppermute(values, axis, [(i, i ^ offset) for i in range(size)])


def sum_over(values, steps):
    for axis, offset in steps:
        values = (
            values.astype(jnp.float32) + swap(values, axis, offset).astype(jnp.float32)
        ).astype(values.dtype)
    return values


def bits_of(axis):
    return [(axis, 1 << i) for i in range(lax.axis_size(axis).bit_length() - 1)]


def spread_over_rep(values):
    return [values] + [swap(values, "rep", d) for d in range(1, lax.axis_size("rep"))]


def double(values, offset):
    return jnp.concatenate([values, swap(values, "rep", offset)], 0)


def parts_of(values, axis):
    own = lax.axis_index("rep")
    return [
        lax.dynamic_index_in_dim(values, own ^ d, axis, keepdims=False)
        for d in range(values.shape[axis])
    ]


def rep_order(pieces):
    own = lax.axis_index("rep")
    count = len(pieces)
    return [lax.select_n(own, *[pieces[d ^ i] for i in range(count)]) for d in range(count)]


def trade_over_rep(pieces):
    return [pieces[0]] + [swap(pieces[d], "rep", d) for d in range(1, len(pieces))]


def far_terms(pieces):
    if len(pieces) != 4:
        return [swap(pieces[d], "rep", d) for d in range(len(pieces)) if d & (d - 1)]
    half = pieces[3].shape[0] // 2
    return [swap(pieces[3][:half], "rep", 1), swap(pieces[3][half:], "rep", 2)]


def near_terms(pieces, found):
    near = [1 << i for i in range(len(pieces).bit_length() - 1)]
    if len(pieces) != 4:
        return [swap(pieces[d], "rep", d) for d in near]
    half = pieces[3].shape[0] // 2
    one, two = pieces[1], pieces[2]
    one = jnp.concatenate([one[:half], sum_of([one[half:], found[1]]).astype(low_type)], 0)
    two = jnp.concatenate([sum_of([two[:half], found[0]]).astype(low_type), two[half:]], 0)
    return [swap(one, "rep", 1), swap(two, "rep", 2)]


def all_terms(pieces, found, near):
    return [pieces[0]] + near + (found if len(pieces) != 4 else [])


def sum_of(terms):
    return sum(term.astype(jnp.float32) for term in terms)


def trade_over_line(values):
    line, own = lax.axis_size("line"), lax.axis_index("line")
    terms = [lax.dynamic_index_in_dim(values, own, 0, keepdims=False)]
    for k in range(1, line):
        piece = lax.dynamic_index_in_dim(values, (own + k) % line, 0, keepdims=False)
        terms.append(lax.ppermute(piece, "line", [(i, (i + k) % line) for i in range(line)]))
    return terms


def two_rows(values):
    high = values.astype(low_type)
    return jnp.concatenate([high, (values - high.astype(jnp.float32)).astype(low_type)], -2)


def one_row(values):
    high, low = jnp.split(values.astype(jnp.float32), 2, -2)
    return high + low


def stage(values):
    return lax.optimization_barrier(values)


def shift(values):
    line = lax.axis_size("line")
    return lax.ppermute(values, "line", [(i, (i + 1) % line) for i in range(line)])


def gather_rows(values):
    return lax.all_gather(values, SHARD, axis=0, tiled=True)


def scatter_rows(values):
    return lax.psum_scatter(values, SHARD, scatter_dimension=0, tiled=True)


def exchange(values):
    return lax.all_to_all(values, SHARD, split_axis=0, concat_axis=0, tiled=True)


def gelu_and_slope(values):
    reduced = jnp.abs(values) * (0.5**0.5)
    inverse = 1.0 / (1.0 + 0.3275911 * reduced)
    bell = jnp.exp(-(reduced * reduced))
    tail = 1.061405429 * inverse - 1.453152027
    tail = tail * inverse + 1.421413741
    tail = tail * inverse - 0.284496736
    tail = (tail * inverse + 0.254829592) * inverse * bell * 0.5
    normal = jnp.where(values >= 0.0, 1.0 - tail, tail)
    return values * normal, normal + values * (bell * (0.5 / math.pi) ** 0.5)


def local(
    layer_input,
    encoder_states,
    out_grad,
    placement,
    w_self_qkv,
    w_self_out,
    w_cross_q,
    w_cross_kv,
    w_cross_out,
    w_fc1,
    w_fc2,
    proj_biases,
    fc1_bias,
    norm_gains,
    norm_shifts,
):
    reps, line = lax.axis_size("rep"), lax.axis_size("line")
    rep, core = lax.axis_index("rep"), lax.axis_index("core")
    group = 2 * line
    member = 2 * lax.axis_index("line") + core
    tok, model = layer_input.shape
    feed = w_fc1.shape[1]
    weight_rows = w_self_qkv.shape[0]
    width = model // group
    unit = feed // (group * reps)
    score_scale = HEAD_DIM ** (-0.5)
    slot_table = placement[0]
    device_ids = jnp.arange(group, dtype=jnp.int32)
    owners = jnp.sum(
        jnp.where(slot_table[None, :] == device_ids[:, None], device_ids[None, :], 0), 1
    )

    def own_columns(row):
        return lax.dynamic_slice(row, (member * width,), (width,))

    def in_columns(row):
        return lax.dynamic_update_slice(jnp.zeros((model,), jnp.float32), row, (member * width,))

    part_rows = weight_rows // reps
    slices = jnp.concatenate(
        [
            lax.dynamic_slice_in_dim(weight, rep * part_rows, part_rows, 0).reshape(
                part_rows, -1, group, width
            )
            for weight in (w_self_qkv, w_cross_kv)
        ],
        1,
    )
    slices = slices.transpose(2, 0, 1, 3).reshape(group, weight_rows // reps, 5 * width)
    first_cut = w_fc1.reshape(weight_rows, line, 2, reps, unit)
    first_cut = lax.dynamic_index_in_dim(first_cut, rep, 3, keepdims=False)
    first_own = lax.dynamic_index_in_dim(first_cut, core, 2, keepdims=False)
    first_other = lax.dynamic_index_in_dim(first_cut, 1 - core, 2, keepdims=False)
    first_own = first_own.reshape(weight_rows, line * unit)
    first_other = swap(first_other.reshape(weight_rows, line * unit), "core", 1)
    first_cut = jnp.where(
        core == 0,
        jnp.concatenate([first_own, first_other], 0),
        jnp.concatenate([first_other, first_own], 0),
    )
    second_cut = lax.dynamic_slice_in_dim(w_fc2, rep * unit, unit, 0)
    bias_cut = lax.dynamic_index_in_dim(
        fc1_bias.reshape(line, 2, reps, unit), core, 1, keepdims=False
    )
    bias_cut = [bias_cut[:, r].reshape(line * unit) for r in range(reps)]
    bias_cut = rep_order(bias_cut)

    square = jnp.stack([w_self_out, w_cross_q, w_cross_out], 0)
    square = square.reshape(3, reps, weight_rows // reps, model)
    square = lax.dynamic_index_in_dim(square, rep, 1, keepdims=False).reshape(-1, model)

    inputs = layer_input.astype(jnp.float32)
    zeros = jnp.zeros((width,), jnp.float32)
    head_bias = jnp.concatenate([own_columns(proj_biases[0]), zeros, own_columns(proj_biases[1])])
    head_scale = jnp.concatenate([jnp.full((width,), score_scale), jnp.ones((2 * width,))])
    cross_bias = jnp.concatenate([zeros, own_columns(proj_biases[4])])

    near = [1 << i for i in range(reps.bit_length() - 1)]
    far = [d for d in range(1, reps) if d not in near]
    slices = exchange(slices)
    blocks = [layer_input, swap(layer_input, "core", 1)]
    block = shift(layer_input)
    block, slices, blocks, first_cut, square, encoder_states, second_cut = stage(
        (block, slices, blocks, first_cut, square, encoder_states, second_cut)
    )

    both_cut = lax.all_gather(
        jnp.concatenate([second_cut, square], 0), "line", axis=0, tiled=True
    ).reshape(line, -1, model)
    blocks += [block, swap(block, "core", 1)]
    block = shift(block)
    slices = spread_over_rep(slices)
    block, slices, blocks, encoder_states = stage((block, slices, blocks, encoder_states))

    for step in range(line - 3):
        blocks += [block, swap(block, "core", 1)]
        block = shift(block)
    slices = jnp.stack(rep_order(slices), 1).reshape(model, 5 * width)
    head_qkv, head_ckv = slices[:, : 3 * width], slices[:, 3 * width :]
    all_states = gather_rows(encoder_states)
    block, blocks, both_cut, head_qkv, head_ckv, all_states, first_cut = stage(
        (block, blocks, both_cut, head_qkv, head_ckv, all_states, first_cut)
    )

    blocks += [block, swap(block, "core", 1)]
    square = spread_over_rep(both_cut[:, unit:])
    wfirst = {0: lax.all_gather(first_cut, "line", axis=0, tiled=True)}
    head_pair = (product(all_states, head_ckv) + cross_bias).astype(low_type)
    head_pair = split_columns(head_pair, 2)
    wsecond = {0: both_cut[:, :unit].reshape(line * unit, model)}
    back = (lax.axis_index("line") - owners // 2) % line
    places = 2 * back + ((owners % 2) ^ core)
    slot_of = jnp.sum(
        jnp.where(places[None, :] == device_ids[:, None], device_ids[None, :], 0), 1
    )
    heads = width // HEAD_DIM
    made, turn, self_totals, self_mixed, self_low = None, owners, [], [], []
    for head in range(heads):
        extra = () if head else (blocks, head_qkv, head_bias, head_scale)
        made, mixed, total = self_forward(head, turn, slot_of, tok, made, *extra)
        self_totals.append(total)
        if head == 0:
            mixed, turn, square, head_pair = stage((mixed, turn, square, head_pair))
            wsecond.update({d: swap(wsecond[0], "rep", d) for d in near})
            square = jnp.stack(rep_order(square), 1)
            square_other = swap(square, "core", 1)
        if head == heads - 1:
            held = (mixed, wfirst, square, square_other)
            held, wsecond, self_low = stage((held, wsecond, self_low))
            mixed, wfirst, square, square_other = held
            wsecond.update({d: swap(wsecond[0], "rep", d) for d in far})
            wfirst.update({d: swap(wfirst[0], "rep", d) for d in near})
        self_mixed.append(mixed)
        self_low.append(exchange(mixed))
    qkv = made
    square = jnp.where(
        core == 0, jnp.stack([square, square_other], 1), jnp.stack([square_other, square], 1)
    )
    square = square.reshape(line, 2, reps, 3, weight_rows // reps, model)
    full_out, full_cross_q, full_cross_out = [
        square[:, :, :, i].reshape(model, model) for i in range(3)
    ]
    pairs = lax.all_gather(head_pair, SHARD, axis=0, tiled=False)
    self_low, pairs = stage((self_low, pairs))
    self_low = jnp.stack(self_low, 1).reshape(model, tok)

    first_sum = inputs + (product_left(self_low, full_out) + proj_biases[2])
    first_norm, norm1_back = jax.vjp(norm_rows, first_sum, norm_gains[0], norm_shifts[0])
    first_low = first_norm.astype(low_type)
    cross_queries = ((product(first_low, full_cross_q) + proj_biases[3]) * score_scale).astype(
        low_type
    )
    cross_low, cross_total = cross_forward(cross_queries, pairs)
    cross_low, wfirst, wsecond = stage((cross_low, wfirst, wsecond))
    wfirst.update({d: swap(wfirst[0], "rep", d) for d in far})
    second_sum = first_norm + (product(cross_low, full_cross_out) + proj_biases[5])
    second_norm, norm2_back = jax.vjp(norm_rows, second_sum, norm_gains[1], norm_shifts[1])
    second_low = second_norm.astype(low_type)

    turned = jnp.transpose(stage((head_qkv, second_low))[0])
    turned = turned.reshape(3, heads, HEAD_DIM, model).transpose(1, 0, 2, 3)
    turned = gather_rows(turned.reshape(-1, model))
    turned = turned.reshape(group, heads, 3 * HEAD_DIM, model)

    second_both = jnp.concatenate([second_low, swap(second_low, "core", 1)], 0)
    feed_sum, hidden, slopes = 0.0, [], []
    for part in range(reps):
        active, slope = gelu_and_slope(product(second_both, wfirst[part]) + bias_cut[part])
        hidden.append(active.astype(low_type))
        slopes.append(slope)
        feed_sum = feed_sum + product(hidden[part], wsecond[part])
    feed_other = swap(feed_sum[tok:].astype(low_type), "core", 1).astype(jnp.float32)
    third_sum = second_norm + (feed_sum[:tok] + feed_other + proj_biases[6])
    result, norm3_back = jax.vjp(norm_rows, third_sum, norm_gains[2], norm_shifts[2])
    output = result.astype(low_type)

    third_grad, gain_three, shift_three = norm3_back(out_grad.astype(jnp.float32))
    feed_grad = third_grad.astype(low_type)
    bias_fc2 = column_sums(feed_grad)
    feed_both = jnp.concatenate([feed_grad, swap(feed_grad, "core", 1)], 0)
    second_parts = [
        product_left(hidden[part], feed_both).astype(low_type) for part in range(reps)
    ]
    feed_both, second_parts = stage((feed_both, second_parts))
    second_found = far_terms(second_parts)
    back_sum, first_parts, bias_parts = 0.0, [], []
    for part in range(reps):
        pre_grad = (product_right(feed_both, wsecond[part]) * slopes[part]).astype(low_type)
        first_parts.append(product_left(second_both, pre_grad).astype(low_type))
        bias_parts.append(column_sums(pre_grad))
        back_sum = back_sum + product_right(pre_grad, wfirst[part])
        if part == reps // 2 - 1:
            feed_both, back_sum, second_found = stage((feed_both, back_sum, second_found))
            second_near = near_terms(second_parts, second_found)
    back_sum, second_near, first_parts = stage((back_sum, second_near, first_parts))
    second_sums = sum_of(all_terms(second_parts, second_found, second_near)).astype(low_type)
    back_other = swap(back_sum[tok:].astype(low_type), "core", 1).astype(jnp.float32)
    second_grad, gain_two, shift_two = norm2_back(third_grad + (back_sum[:tok] + back_other))
    second_grad, second_sums, first_parts = stage((second_grad, second_sums, first_parts))
    second_sums = lax.psum_scatter(second_sums, "line", scatter_dimension=0, tiled=True)
    first_found = far_terms(first_parts)

    cross_out_grad = second_grad.astype(low_type)
    cross_mixed_grad = product_right(cross_out_grad, full_cross_out).astype(low_type)
    cross_q_grad, pair_grad = cross_backward(
        cross_queries, pairs, cross_mixed_grad, cross_low, cross_total
    )
    cross_q_grad, pair_grad, first_found, turned = stage(
        (cross_q_grad, pair_grad, first_found, turned)
    )
    first_near = near_terms(first_parts, first_found)
    own_pair_grad = lax.psum_scatter(pair_grad, SHARD, scatter_dimension=0, tiled=False)
    first_grad, gain_one, shift_one = norm1_back(
        second_grad + product_right(cross_q_grad, full_cross_q)
    )
    self_out_grad = first_grad.astype(low_type)
    mixed_grad = product_right(full_out, self_out_grad).astype(low_type)
    mixed_grad = mixed_grad.reshape(group, heads, HEAD_DIM, tok)
    held = (self_low, first_low, cross_low, self_out_grad, cross_q_grad, cross_out_grad)
    mixed_grad, held = stage((mixed_grad, held))
    self_low, first_low, cross_low, self_out_grad, cross_q_grad, cross_out_grad = held
    mixed_grad = [exchange(mixed_grad[:, head]) for head in range(heads)]
    part_self_out = product(self_low, self_out_grad).astype(low_type)
    part_cross_q = product_left(first_low, cross_q_grad).astype(low_type)
    part_cross_out = product_left(cross_low, cross_out_grad).astype(low_type)
    bias_self_out = column_sums(self_out_grad)
    bias_cross_q = column_sums(cross_q_grad)
    bias_cross_out = column_sums(cross_out_grad)

    square = [
        part.reshape(line, 2, reps, part_rows, model)
        for part in (part_self_out, part_cross_q, part_cross_out)
    ]

    def of_core(index):
        rows = [lax.dynamic_index_in_dim(part, index, 1, keepdims=False) for part in square]
        return jnp.stack(rows, 0)

    square_own, square_other = of_core(core), swap(of_core(1 - core), "core", 1)

    bias_parts = jnp.stack([part.reshape(line, unit) for part in rep_order(bias_parts)], 1)
    bias_fc1 = jnp.where(
        jnp.arange(2)[None, :, None, None] == core, bias_parts[:, None], 0.0
    ).reshape(feed)
    small = jnp.concatenate(
        [
            jnp.stack(
                [
                    bias_self_out,
                    bias_cross_q,
                    bias_cross_out,
                    bias_fc2,
                    gain_one,
                    gain_two,
                    gain_three,
                    shift_one,
                    shift_two,
                    shift_three,
                ],
                0,
            ),
            bias_fc1.reshape(-1, model),
        ],
        0,
    )
    hops = bits_of("core") + bits_of("rep") + bits_of("line")

    def hop(values, count):
        for _ in range(count):
            values = values + swap(values, *hops.pop(0))
        return values

    small = hop(small, 1)
    square = square_own.astype(jnp.float32) + square_other.astype(jnp.float32)
    square = square.astype(low_type).transpose(2, 1, 0, 3, 4)
    square = parts_of(square, 0)
    held = (square, small, second_sums, first_near)
    mixed_grad[0], held = stage((mixed_grad[0], held))
    square, small, second_sums, first_near = held
    first_sums = sum_of(all_terms(first_parts, first_found, first_near)).astype(low_type)
    first_sums = lax.psum_scatter(first_sums, "line", scatter_dimension=0, tiled=True)
    square_terms = trade_over_rep(square)
    wide = 2 * line * unit
    second_sums = second_sums.reshape(unit, model // wide, wide).transpose(1, 0, 2)
    second_sums = double(second_sums.reshape(1, -1, wide), near[0])
    turn = owners

    part_rows = weight_rows // reps

    def with_sums(values, sums):
        rows = two_rows(jnp.broadcast_to(sums, sums.shape[:-2] + (8,) + sums.shape[-1:]))
        return jnp.concatenate([values.astype(low_type), rows], -2)

    def split_sums(values):
        return values[..., :part_rows, :], one_row(values[..., part_rows:, :])[..., :1, :]

    def trade_slices(values):
        columns = values.shape[1]
        sums = two_rows(jnp.broadcast_to(values[model : model + 1], (8, columns)))
        values = values[:model].reshape(group, reps, part_rows, columns).astype(low_type)
        return trade_over_rep(
            [
                jnp.concatenate([part.reshape(-1, columns), sums], 0)
                for part in parts_of(values, 1)
            ]
        )

    def exchange_slices(terms):
        values = sum_of(terms)
        sums = one_row(values[group * part_rows :])[:1]
        sums = jnp.broadcast_to(sums, (group,) + sums.shape)
        values = values[: group * part_rows].reshape(group, part_rows, -1)
        return exchange(with_sums(values, sums))

    def join_slices(values):
        values, sums = split_sums(values.astype(jnp.float32))
        values = jnp.stack(rep_order(spread_over_rep(values.astype(low_type))), 0)
        values = values.transpose(0, 2, 1, 3).reshape(weight_rows, group, -1)
        return values, sums[:, 0][None]

    parts, slice_parts = [], []
    for head in range(heads):
        part, slice_part = self_backward(
            head,
            turn,
            places,
            blocks,
            slice_parts,
            qkv,
            mixed_grad[head],
            self_mixed[head],
            self_totals[head],
        )
        if head == 0:
            small = hop(small, 1)
            held = (part, slice_part, turn, first_sums, second_sums, square_terms, small)
            held, mixed_grad, own_pair_grad = stage((held, mixed_grad, own_pair_grad))
            part, slice_part, turn, first_sums, second_sums, square_terms, small = held
            own_pair_grad = join_columns(own_pair_grad)
            for offset in near[1:]:
                second_sums = double(second_sums, offset)
            first_sums = first_sums.reshape(2, weight_rows, line * unit).transpose(1, 0, 2)
            first_sums = double(first_sums.reshape(1, -1, wide), near[0])
            pair_sums = jnp.sum(own_pair_grad.astype(jnp.float32), 0)
            pair_sums = jnp.broadcast_to(pair_sums, (LANES, 2 * width))
            pair_slices = jnp.concatenate([product_left(all_states, own_pair_grad), pair_sums], 0)
            square_terms = trade_over_line(sum_of(square_terms).astype(low_type))
        if head == heads - 1:
            held = (part, slice_part, first_sums, second_sums, square_terms)
            held, parts, slice_parts = stage((held, parts, slice_parts))
            part, slice_part, first_sums, second_sums, square_terms = held
        parts.append(exchange(part))
        slice_parts.append(slice_part)

    slice_parts = trade_slices(jnp.concatenate([slice_parts[-1], pair_slices], 1))
    for offset in near[1:]:
        first_sums = double(first_sums, offset)
    square = double(sum_of(square_terms).astype(low_type)[None], near[0])
    small = hop(small, 1)
    enc_terms = product_right(own_pair_grad, head_ckv).astype(low_type)
    held = (first_sums, square, small, enc_terms)
    parts, slice_parts, held = stage((parts, slice_parts, held))
    first_sums, square, small, enc_terms = held
    enc_grad = scatter_rows(enc_terms)

    slice_parts = exchange_slices(slice_parts)
    for offset in near[1:]:
        square = double(square, offset)
    small = hop(small, 1)
    second_sums = jnp.stack(rep_order([second_sums[d] for d in range(reps)]), 0)
    second_sums = second_sums.reshape(reps, model // wide, unit, wide)
    grad_fc2 = second_sums.transpose(0, 2, 1, 3).reshape(-1, model).astype(jnp.float32)
    first_sums = jnp.stack(rep_order([first_sums[d] for d in range(reps)]), 0)
    first_sums = first_sums.reshape(reps, weight_rows, 2, line, unit)
    first_own = lax.dynamic_index_in_dim(first_sums, core, 2, keepdims=False)
    first_other = lax.dynamic_index_in_dim(first_sums, 1 - core, 2, keepdims=False)
    first_other = swap(first_other.reshape(-1, line * unit), "core", 1)
    first_other = first_other.reshape(first_own.shape)
    input_grad = first_grad
    rows = turned.reshape(-1, model)
    input_grad = input_grad + product_left(jnp.stack(parts, 1).reshape(rows.shape[0], tok), rows)
    held = (first_own, first_other, square, input_grad, grad_fc2, small)
    slice_parts, held = stage((slice_parts, held))
    first_own, first_other, square, input_grad, grad_fc2, small = held

    slice_parts = join_slices(slice_parts)
    small = hop(small, len(hops))
    square = jnp.stack(rep_order([square[d] for d in range(reps)]), 1).astype(jnp.float32)
    grad_self_out, grad_cross_q, grad_cross_out = [
        square[i].reshape(weight_rows, model) for i in range(3)
    ]
    grad_fc1 = jnp.where(
        core == 0, jnp.stack([first_own, first_other], 0), jnp.stack([first_other, first_own], 0)
    )
    grad_fc1 = grad_fc1.transpose(2, 3, 0, 1, 4).reshape(weight_rows, feed).astype(jnp.float32)

    def of_self(values):
        values = values[..., : 3 * width].reshape(-1, group, 3, width)
        return values.transpose(0, 2, 1, 3).reshape(-1, 3, model)

    def of_cross(values):
        values = values[..., 3 * width :].reshape(-1, group, 2, width)
        return values.transpose(0, 2, 1, 3).reshape(-1, 2, model)

    grad_self_qkv = of_self(slice_parts[0].astype(jnp.float32)).reshape(weight_rows, 3 * model)
    grad_cross_kv = of_cross(slice_parts[0].astype(jnp.float32)).reshape(weight_rows, 2 * model)
    bias_self, bias_cross_v = of_self(slice_parts[1]), of_cross(slice_parts[1])[0, 1]
    grad_biases = jnp.stack(
        [
            bias_self[0, 0],
            bias_self[0, 2],
            small[0],
            small[1],
            bias_cross_v,
            small[2],
            small[3],
        ],
        0,
    )
    return (
        output,
        input_grad,
        enc_grad.astype(jnp.float32),
        grad_self_qkv,
        grad_self_out,
        grad_cross_q,
        grad_cross_kv,
        grad_cross_out,
        grad_fc1,
        grad_fc2,
        grad_biases,
        small[10:].reshape(-1),
        small[4:7],
        small[7:10],
    )


def solution(mesh):
    reps, group = mesh.devices.shape
    split = jax.sharding.Mesh(
        mesh.devices.reshape(reps, group // 2, 2), ("rep",) + SHARD
    )
    rows, cut = P(("rep",) + SHARD, None), P(SHARD, None)
    return jax.shard_map(
        local,
        mesh=split,
        in_specs=(rows,) * 3 + (P("rep", None),) + (cut,) * 7 + (P(),) * 4,
        out_specs=(rows,) * 3 + (cut,) * 7 + (P(),) * 4,
        check_vma=False,
    )
```
